256 devices in a mesh: dp: 2 (over core), pipe: 8 (over y, x_lo), tensor: 16 (over x_hi, z).
Axes of the slice: x: 4 (x_hi: 2, x_lo: 2; x = x_hi * 2 + x_lo), y: 4, z: 8, core: 2. Of those that a mesh axis runs over, the one named last changes fastest.
Arguments:
- forward_acts: bfloat16 [1024, 8192], P(('dp', 'tensor'), 'pipe'), parts along dimension 0, may hold values from -6 to 6
- backward_grad: bfloat16 [1024, 8192], P(('dp', 'tensor'), 'pipe'), parts along dimension 0, may hold values from -6 to 6
- stored_gate: bfloat16 [1024, 14336], P(('dp', 'pipe'), 'tensor'), parts along dimension 0, may hold values from -8 to 8
- stored_up: bfloat16 [1024, 14336], P(('dp', 'pipe'), 'tensor'), parts along dimension 0, may hold values from -6 to 6
- gate_weight: bfloat16 [8192, 14336], P('pipe', 'tensor'), may hold values from -0.0625 to 0.0625
- up_weight: bfloat16 [8192, 14336], P('pipe', 'tensor'), may hold values from -0.0625 to 0.0625
- down_weight: bfloat16 [14336, 8192], P('tensor', 'pipe'), may hold values from -0.046875 to 0.046875
Outputs:
- layer_output: bfloat16 [1024, 8192], P(('dp', 'tensor'), 'pipe'), parts along dimension 0
- input_grad: bfloat16 [1024, 8192], P(('dp', 'tensor'), 'pipe'), parts along dimension 0
The draws below stay inside these ranges and needn't reach their ends.
There are 2 independent parts, one for each index of `dp`. The reference program is written for one: setup_inputs(seed, part) draws one part's arguments, and reference() takes and returns one part's arrays. A program takes and returns all parts, laid end to end along the dimension named above; an argument that names none is the same for every part. Nothing has to cross between parts.
All inputs are finite; a program needn't handle non-finite values.
Results may differ from the reference program's by a relative error of at most 0.005.
Values may be sent and summed in bfloat16 or wider, within the bound.
A program may use at most 64 MiB of HBM per device.

```python
import jax
import jax.numpy as jnp
from jax import lax

D = 8192
FF = 14336
TOK = 512


def block_levels(stream_key, dims, cuts, smallest, top_value):
    factor_of = 1.0
    for position, parts in cuts:
        draws = jax.random.uniform(jax.random.fold_in(jax.random.fold_in(stream_key, 6), position), (parts,), jnp.float32, smallest / len(cuts), top_value / len(cuts))
        factor_of = factor_of * jnp.repeat(jnp.exp(draws), dims[position] // parts).reshape((-1,) + (1,) * (len(dims) - 1 - position))
    return factor_of


def scatter_about(stream_key, shape, scale, bound, cuts=(), dtype=jnp.bfloat16):
    result = jax.random.normal(stream_key, shape, jnp.float32) * scale
    if len(cuts) > 0:
        result = block_levels(stream_key, shape, cuts, -0.22, 0.18) * result
    return jnp.clip(result, min=-bound, max=bound).astype(dtype)


def setup_inputs(seed: int = 0, part: int = 0) -> dict:
    key_list = jax.random.split(jax.random.key(seed), 8)
    part_keys = jax.random.split(jax.random.fold_in(key_list[7], part), 8)
    forward_acts = scatter_about(part_keys[0], (TOK, D), 1.0, 6.0, ((0, 16), (1, 8)))
    backward_grad = scatter_about(part_keys[1], (TOK, D), 1.0, 6.0, ((0, 16), (1, 8)))
    stored_gate = scatter_about(part_keys[2], (TOK, FF), 1.5, 8.0, ((0, 8), (1, 16)))
    stored_up = scatter_about(part_keys[3], (TOK, FF), 1.0, 6.0, ((0, 8), (1, 16)))
    gate_weight = scatter_about(key_list[4], (D, FF), D ** -0.5, 0.0625, ((0, 8), (1, 16)))
    up_weight = scatter_about(key_list[5], (D, FF), D ** -0.5, 0.0625, ((0, 8), (1, 16)))
    down_weight = scatter_about(key_list[6], (FF, D), FF ** -0.5, 0.046875, ((0, 16), (1, 8)))
    return {"forward_acts": forward_acts, "backward_grad": backward_grad, "stored_gate": stored_gate, "stored_up": stored_up, "gate_weight": gate_weight, "up_weight": up_weight, "down_weight": down_weight}


def reference(forward_acts, backward_grad, stored_gate, stored_up, gate_weight, up_weight, down_weight):
    paired = jnp.concatenate([gate_weight, up_weight], axis=1)
    projected = jnp.dot(forward_acts, paired, preferred_element_type=jnp.float32)
    hidden = (jax.nn.silu(projected[:, :FF]) * projected[:, FF:]).astype(jnp.bfloat16)
    layer_output = jnp.dot(hidden, down_weight, preferred_element_type=jnp.float32).astype(jnp.bfloat16)
    hidden_grad = lax.dot_general(backward_grad, down_weight, (((1,), (1,)), ((), ())), preferred_element_type=jnp.float32)
    gate_vals = stored_gate.astype(jnp.float32)
    up_vals = stored_up.astype(jnp.float32)
    sigma = jax.nn.sigmoid(gate_vals)
    gate_slope = (hidden_grad * up_vals * sigma * (1.0 + gate_vals * (1.0 - sigma))).astype(jnp.bfloat16)
    up_slope = (hidden_grad * gate_vals * sigma).astype(jnp.bfloat16)
    slopes = jnp.concatenate([gate_slope, up_slope], axis=1)
    input_grad = lax.dot_general(slopes, paired, (((1,), (1,)), ((), ())), preferred_element_type=jnp.float32).astype(jnp.bfloat16)
    return layer_output, input_grad
```

```python
import jax
import jax.numpy as jnp
from jax import lax
from jax.sharding import PartitionSpec as P


def make_slopes(hidden_grad, gate_vals, up_vals):
    gate_wide = gate_vals.astype(jnp.float32)
    up_wide = up_vals.astype(jnp.float32)
    sigma = jax.nn.sigmoid(gate_wide)
    gate_slope = (hidden_grad * up_wide * sigma * (1.0 + gate_wide * (1.0 - sigma))).astype(
        jnp.bfloat16
    )
    up_slope = (hidden_grad * gate_wide * sigma).astype(jnp.bfloat16)
    return jnp.concatenate([gate_slope, up_slope], axis=1)


def gather_rows(block, axis, count):
    sent = jnp.broadcast_to(block[None], (count,) + block.shape)
    got = lax.all_to_all(sent, axis, 0, 0, tiled=False)
    return got.reshape((count * block.shape[0],) + block.shape[1:])


def scatter_sum_rows(partial, axis, count):
    rows = partial.shape[0] // count
    sent = partial.reshape((count, rows) + partial.shape[1:]).astype(jnp.bfloat16)
    got = lax.all_to_all(sent, axis, 0, 0, tiled=False)
    return got.astype(jnp.float32).sum(axis=0)


def per_device(
    forward_acts, backward_grad, stored_gate, stored_up, gate_weight, up_weight, down_weight
):
    n_pipe = lax.axis_size("pipe")
    n_tensor = lax.axis_size("tensor")
    hidden_width = gate_weight.shape[1]
    contract_last = (((1,), (1,)), ((), ()))

    whole_acts = gather_rows(forward_acts, "tensor", n_tensor)
    gate_part = jnp.dot(whole_acts, gate_weight, preferred_element_type=jnp.float32)
    up_part = jnp.dot(whole_acts, up_weight, preferred_element_type=jnp.float32)
    summed = scatter_sum_rows(jnp.concatenate([gate_part, up_part], axis=1), "pipe", n_pipe)
    hidden_part = (jax.nn.silu(summed[:, :hidden_width]) * summed[:, hidden_width:]).astype(
        jnp.bfloat16
    )
    hidden = gather_rows(hidden_part, "pipe", n_pipe)
    layer_output = scatter_sum_rows(
        jnp.dot(hidden, down_weight, preferred_element_type=jnp.float32), "tensor", n_tensor
    ).astype(jnp.bfloat16)

    whole_grad = gather_rows(backward_grad, "tensor", n_tensor)
    hidden_grad = scatter_sum_rows(
        lax.dot_general(whole_grad, down_weight, contract_last, preferred_element_type=jnp.float32),
        "pipe",
        n_pipe,
    )
    local_slopes = make_slopes(hidden_grad, stored_gate, stored_up)
    all_slopes = gather_rows(local_slopes, "pipe", n_pipe)
    input_grad_part = lax.dot_general(
        all_slopes[:, :hidden_width], gate_weight, contract_last, preferred_element_type=jnp.float32
    ) + lax.dot_general(
        all_slopes[:, hidden_width:], up_weight, contract_last, preferred_element_type=jnp.float32
    )
    input_grad = scatter_sum_rows(input_grad_part, "tensor", n_tensor).astype(jnp.bfloat16)
    return (layer_output, input_grad)


def solution(mesh):
    in_specs = (
        P(("dp", "tensor"), "pipe"),
        P(("dp", "tensor"), "pipe"),
        P(("dp", "pipe"), "tensor"),
        P(("dp", "pipe"), "tensor"),
        P("pipe", "tensor"),
        P("pipe", "tensor"),
        P("tensor", "pipe"),
    )
    out_specs = (P(("dp", "tensor"), "pipe"), P(("dp", "tensor"), "pipe"))
    return jax.shard_map(
        per_device, mesh=mesh, in_specs=in_specs, out_specs=out_specs, check_vma=False
    )
```

```python
import jax
import jax.numpy as jnp
from jax import lax
from jax.sharding import PartitionSpec as P

PIPE_LINK = jnp.float32
TENSOR_LINK = jnp.bfloat16


def make_slopes(hidden_grad, gate_vals, up_vals):
    gate_wide = gate_vals.astype(jnp.float32)
    up_wide = up_vals.astype(jnp.float32)
    sigma = jax.nn.sigmoid(gate_wide)
    gate_slope = (hidden_grad * up_wide * sigma * (1.0 + gate_wide * (1.0 - sigma))).astype(
        jnp.bfloat16
    )
    up_slope = (hidden_grad * gate_wide * sigma).astype(jnp.bfloat16)
    return jnp.concatenate([gate_slope, up_slope], axis=1)


def gather_rows(block, axis, count):
    sent = jnp.broadcast_to(block[None], (count,) + block.shape)
    got = lax.all_to_all(sent, axis, 0, 0, tiled=False)
    return got.reshape((count * block.shape[0],) + block.shape[1:])


def scatter_sum_rows(partial, axis, count, link_dtype):
    rows = partial.shape[0] // count
    sent = partial.reshape((count, rows) + partial.shape[1:]).astype(link_dtype)
    got = lax.all_to_all(sent, axis, 0, 0, tiled=False)
    return got.astype(jnp.float32).sum(axis=0)


def per_device(
    forward_acts, backward_grad, stored_gate, stored_up, gate_weight, up_weight, down_weight
):
    n_pipe = lax.axis_size("pipe")
    n_tensor = lax.axis_size("tensor")
    hidden_width = gate_weight.shape[1]
    model_width = forward_acts.shape[1]
    contract_last = (((1,), (1,)), ((), ()))

    both = gather_rows(jnp.concatenate([forward_acts, backward_grad], axis=1), "tensor", n_tensor)
    whole_acts = both[:, :model_width]
    whole_grad = both[:, model_width:]

    gate_part = jnp.dot(whole_acts, gate_weight, preferred_element_type=jnp.float32)
    up_part = jnp.dot(whole_acts, up_weight, preferred_element_type=jnp.float32)
    grad_part = lax.dot_general(
        whole_grad, down_weight, contract_last, preferred_element_type=jnp.float32
    )
    summed = scatter_sum_rows(
        jnp.concatenate([gate_part, up_part, grad_part], axis=1), "pipe", n_pipe, PIPE_LINK
    )
    gate_pre = summed[:, :hidden_width]
    up_pre = summed[:, hidden_width : 2 * hidden_width]
    hidden_grad = summed[:, 2 * hidden_width :]
    hidden_part = (jax.nn.silu(gate_pre) * up_pre).astype(jnp.bfloat16)
    local_slopes = make_slopes(hidden_grad, stored_gate, stored_up)

    rows = gather_rows(jnp.concatenate([hidden_part, local_slopes], axis=1), "pipe", n_pipe)
    hidden = rows[:, :hidden_width]
    gate_slopes = rows[:, hidden_width : 2 * hidden_width]
    up_slopes = rows[:, 2 * hidden_width :]

    out_part = jnp.dot(hidden, down_weight, preferred_element_type=jnp.float32)
    in_part = lax.dot_general(
        gate_slopes, gate_weight, contract_last, preferred_element_type=jnp.float32
    ) + lax.dot_general(up_slopes, up_weight, contract_last, preferred_element_type=jnp.float32)
    finished = scatter_sum_rows(
        jnp.concatenate([out_part, in_part], axis=1), "tensor", n_tensor, TENSOR_LINK
    ).astype(jnp.bfloat16)
    return (finished[:, :model_width], finished[:, model_width:])


def solution(mesh):
    in_specs = (
        P(("dp", "tensor"), "pipe"),
        P(("dp", "tensor"), "pipe"),
        P(("dp", "pipe"), "tensor"),
        P(("dp", "pipe"), "tensor"),
        P("pipe", "tensor"),
        P("pipe", "tensor"),
        P("tensor", "pipe"),
    )
    out_specs = (P(("dp", "tensor"), "pipe"), P(("dp", "tensor"), "pipe"))
    return jax.shard_map(
        per_device, mesh=mesh, in_specs=in_specs, out_specs=out_specs, check_vma=False
    )
```

```python
import jax
import jax.numpy as jnp
from jax import lax
from jax.sharding import PartitionSpec as P

PIPE_LINK = jnp.float32
TENSOR_LINK = jnp.bfloat16


def make_slopes(hidden_grad, gate_vals, up_vals):
    gate_wide = gate_vals.astype(jnp.float32)
    up_wide = up_vals.astype(jnp.float32)
    sigma = jax.nn.sigmoid(gate_wide)
    gate_slope = (hidden_grad * up_wide * sigma * (1.0 + gate_wide * (1.0 - sigma))).astype(
        jnp.bfloat16
    )
    up_slope = (hidden_grad * gate_wide * sigma).astype(jnp.bfloat16)
    return jnp.concatenate([gate_slope, up_slope], axis=1)


def gather_rows(block, axis, count):
    sent = jnp.broadcast_to(block[None], (count,) + block.shape)
    got = lax.all_to_all(sent, axis, 0, 0, tiled=False)
    return got.reshape((count * block.shape[0],) + block.shape[1:])


def scatter_sum_rows(partial, axis, count, link_dtype):
    rows = partial.shape[0] // count
    sent = partial.reshape((count, rows) + partial.shape[1:]).astype(link_dtype)
    got = lax.all_to_all(sent, axis, 0, 0, tiled=False)
    return got.astype(jnp.float32).sum(axis=0)


def ring_gather_tensor(first, second, count):
    ring = count // 2
    me = lax.axis_index("tensor")
    z = me % ring
    high = me // ring
    swap = [(h * ring + k, (1 - h) * ring + k) for h in range(2) for k in range(ring)]
    up = [(h * ring + k, h * ring + (k + 1) % ring) for h in range(2) for k in range(ring)]
    down = [(h * ring + k, h * ring + (k - 1) % ring) for h in range(2) for k in range(ring)]
    mine = jnp.stack([first, second])
    theirs = lax.ppermute(mine, "tensor", swap)
    pair = jnp.where(high == 0, jnp.stack([mine, theirs]), jnp.stack([theirs, mine]))
    rows, width = first.shape
    out_first = jnp.zeros((2, ring, rows, width), first.dtype)
    out_second = jnp.zeros((2, ring, rows, width), second.dtype)
    going_up = pair[:, 0]
    going_down = pair[:, 1]
    zero = jnp.int32(0)
    for step in range(ring):
        if step > 0:
            going_up = lax.ppermute(going_up, "tensor", up)
            going_down = lax.ppermute(going_down, "tensor", down)
        src_up = (z - step) % ring
        src_down = (z + step) % ring
        out_first = lax.dynamic_update_slice(out_first, going_up[:, None], (zero, src_up, zero, zero))
        out_second = lax.dynamic_update_slice(
            out_second, going_down[:, None], (zero, src_down, zero, zero)
        )
    return jnp.concatenate(
        [out_first.reshape(count * rows, width), out_second.reshape(count * rows, width)], axis=1
    )


def per_device(
    forward_acts, backward_grad, stored_gate, stored_up, gate_weight, up_weight, down_weight
):
    n_pipe = lax.axis_size("pipe")
    n_tensor = lax.axis_size("tensor")
    hidden_width = gate_weight.shape[1]
    model_width = forward_acts.shape[1]
    contract_last = (((1,), (1,)), ((), ()))

    both = ring_gather_tensor(forward_acts, backward_grad, n_tensor)
    whole_acts = both[:, :model_width]
    whole_grad = both[:, model_width:]

    gate_part = jnp.dot(whole_acts, gate_weight, preferred_element_type=jnp.float32)
    up_part = jnp.dot(whole_acts, up_weight, preferred_element_type=jnp.float32)
    grad_part = lax.dot_general(
        whole_grad, down_weight, contract_last, preferred_element_type=jnp.float32
    )
    summed = scatter_sum_rows(
        jnp.concatenate([gate_part, up_part, grad_part], axis=1), "pipe", n_pipe, PIPE_LINK
    )
    gate_pre = summed[:, :hidden_width]
    up_pre = summed[:, hidden_width : 2 * hidden_width]
    hidden_grad = summed[:, 2 * hidden_width :]
    hidden_part = (jax.nn.silu(gate_pre) * up_pre).astype(jnp.bfloat16)
    local_slopes = make_slopes(hidden_grad, stored_gate, stored_up)

    rows = gather_rows(jnp.concatenate([hidden_part, local_slopes], axis=1), "pipe", n_pipe)
    hidden = rows[:, :hidden_width]
    gate_slopes = rows[:, hidden_width : 2 * hidden_width]
    up_slopes = rows[:, 2 * hidden_width :]

    out_part = jnp.dot(hidden, down_weight, preferred_element_type=jnp.float32)
    in_part = lax.dot_general(
        gate_slopes, gate_weight, contract_last, preferred_element_type=jnp.float32
    ) + lax.dot_general(up_slopes, up_weight, contract_last, preferred_element_type=jnp.float32)
    finished = scatter_sum_rows(
        jnp.concatenate([out_part, in_part], axis=1), "tensor", n_tensor, TENSOR_LINK
    ).astype(jnp.bfloat16)
    return (finished[:, :model_width], finished[:, model_width:])


def solution(mesh):
    in_specs = (
        P(("dp", "tensor"), "pipe"),
        P(("dp", "tensor"), "pipe"),
        P(("dp", "pipe"), "tensor"),
        P(("dp", "pipe"), "tensor"),
        P("pipe", "tensor"),
        P("pipe", "tensor"),
        P("tensor", "pipe"),
    )
    out_specs = (P(("dp", "tensor"), "pipe"), P(("dp", "tensor"), "pipe"))
    return jax.shard_map(
        per_device, mesh=mesh, in_specs=in_specs, out_specs=out_specs, check_vma=False
    )
```

```python
import functools

import jax
import jax.numpy as jnp
from jax import lax
from jax.experimental import pallas as pl
from jax.experimental.pallas import tpu as pltpu
from jax.sharding import PartitionSpec as P

PIPE_LINK = jnp.float32
TENSOR_LINK = jnp.bfloat16
MESH = pl.DeviceIdType.MESH


def make_slopes(hidden_grad, gate_vals, up_vals):
    gate_wide = gate_vals.astype(jnp.float32)
    up_wide = up_vals.astype(jnp.float32)
    sigma = jax.nn.sigmoid(gate_wide)
    gate_slope = (hidden_grad * up_wide * sigma * (1.0 + gate_wide * (1.0 - sigma))).astype(
        jnp.bfloat16
    )
    up_slope = (hidden_grad * gate_wide * sigma).astype(jnp.bfloat16)
    return jnp.concatenate([gate_slope, up_slope], axis=1)


def gather_rows(block, axis, count):
    sent = jnp.broadcast_to(block[None], (count,) + block.shape)
    got = lax.all_to_all(sent, axis, 0, 0, tiled=False)
    return got.reshape((count * block.shape[0],) + block.shape[1:])


def scatter_sum_rows(partial, axis, count, link_dtype):
    rows = partial.shape[0] // count
    sent = partial.reshape((count, rows) + partial.shape[1:]).astype(link_dtype)
    got = lax.all_to_all(sent, axis, 0, 0, tiled=False)
    return got.astype(jnp.float32).sum(axis=0)


def _ring_gather_kernel(axis, outer, inner, ring_on_inner, x_ref, first_ref, second_ref, send_sems, recv_sems, local_sems):
    me = lax.axis_index(axis)
    o = me // inner
    i = me % inner
    if ring_on_inner:
        ring = inner
        pos, other = i, o
        def at(p, q):
            return q * inner + p
    else:
        ring = outer
        pos, other = o, i
        def at(p, q):
            return p * inner + q
    partner = at(pos, 1 - other)
    up = at(lax.rem(pos + 1, ring), other)
    down = at(lax.rem(pos + ring - 1, ring), other)

    barrier = pltpu.get_barrier_semaphore()
    for peer in (partner, up, down):
        pl.semaphore_signal(barrier, inc=1, device_id={axis: peer}, device_id_type=MESH)
    pl.semaphore_wait(barrier, 3)

    own_first = pltpu.make_async_copy(x_ref.at[0], first_ref.at[other, pos], local_sems.at[0])
    own_second = pltpu.make_async_copy(x_ref.at[1], second_ref.at[other, pos], local_sems.at[1])
    own_first.start()
    own_second.start()
    swap_first = pltpu.make_async_remote_copy(
        src_ref=x_ref.at[0], dst_ref=first_ref.at[other, pos],
        send_sem=send_sems.at[0], recv_sem=recv_sems.at[0],
        device_id={axis: partner}, device_id_type=MESH)
    swap_second = pltpu.make_async_remote_copy(
        src_ref=x_ref.at[1], dst_ref=second_ref.at[other, pos],
        send_sem=send_sems.at[1], recv_sem=recv_sems.at[1],
        device_id={axis: partner}, device_id_type=MESH)
    swap_first.start()
    swap_second.start()
    own_first.wait()
    own_second.wait()
    swap_first.wait()
    swap_second.wait()

    for step in range(1, ring):
        src_up = lax.rem(pos - step + 1 + ring, ring)
        src_down = lax.rem(pos + step - 1, ring)
        go_up = pltpu.make_async_remote_copy(
            src_ref=first_ref.at[:, src_up], dst_ref=first_ref.at[:, src_up],
            send_sem=send_sems.at[2 * step], recv_sem=recv_sems.at[2 * step],
            device_id={axis: up}, device_id_type=MESH)
        go_down = pltpu.make_async_remote_copy(
            src_ref=second_ref.at[:, src_down], dst_ref=second_ref.at[:, src_down],
            send_sem=send_sems.at[2 * step + 1], recv_sem=recv_sems.at[2 * step + 1],
            device_id={axis: down}, device_id_type=MESH)
        go_up.start()
        go_down.start()
        go_up.wait()
        go_down.wait()


def ring_gather(first, second, axis, outer, inner, ring_on_inner, cid):
    rows, width = first.shape
    ring = inner if ring_on_inner else outer
    shape = (2, ring, rows, width)
    x = jnp.stack([first, second])
    f, s = pl.pallas_call(
        functools.partial(_ring_gather_kernel, axis, outer, inner, ring_on_inner),
        out_shape=(jax.ShapeDtypeStruct(shape, first.dtype), jax.ShapeDtypeStruct(shape, second.dtype)),
        in_specs=[pl.BlockSpec(memory_space=pltpu.VMEM)],
        out_specs=(pl.BlockSpec(memory_space=pltpu.VMEM), pl.BlockSpec(memory_space=pltpu.VMEM)),
        scratch_shapes=[pltpu.SemaphoreType.DMA((2 * ring,)), pltpu.SemaphoreType.DMA((2 * ring,)), pltpu.SemaphoreType.DMA((2,))],
        compiler_params=pltpu.CompilerParams(collective_id=cid, has_side_effects=True),
    )(x)
    if ring_on_inner:
        return f.reshape(2 * ring * rows, width), s.reshape(2 * ring * rows, width)
    return (f.transpose(1, 0, 2, 3).reshape(2 * ring * rows, width),
            s.transpose(1, 0, 2, 3).reshape(2 * ring * rows, width))


def per_device(
    forward_acts, backward_grad, stored_gate, stored_up, gate_weight, up_weight, down_weight
):
    n_pipe = lax.axis_size("pipe")
    n_tensor = lax.axis_size("tensor")
    hidden_width = gate_weight.shape[1]
    model_width = forward_acts.shape[1]
    contract_last = (((1,), (1,)), ((), ()))

    whole_acts, whole_grad = ring_gather(
        forward_acts, backward_grad, "tensor", 2, n_tensor // 2, True, 0
    )

    gate_part = jnp.dot(whole_acts, gate_weight, preferred_element_type=jnp.float32)
    up_part = jnp.dot(whole_acts, up_weight, preferred_element_type=jnp.float32)
    grad_part = lax.dot_general(
        whole_grad, down_weight, contract_last, preferred_element_type=jnp.float32
    )
    summed = scatter_sum_rows(
        jnp.concatenate([gate_part, up_part, grad_part], axis=1), "pipe", n_pipe, PIPE_LINK
    )
    gate_pre = summed[:, :hidden_width]
    up_pre = summed[:, hidden_width : 2 * hidden_width]
    hidden_grad = summed[:, 2 * hidden_width :]
    hidden_part = (jax.nn.silu(gate_pre) * up_pre).astype(jnp.bfloat16)
    local_slopes = make_slopes(hidden_grad, stored_gate, stored_up)

    rows = gather_rows(jnp.concatenate([hidden_part, local_slopes], axis=1), "pipe", n_pipe)
    hidden = rows[:, :hidden_width]
    gate_slopes = rows[:, hidden_width : 2 * hidden_width]
    up_slopes = rows[:, 2 * hidden_width :]

    out_part = jnp.dot(hidden, down_weight, preferred_element_type=jnp.float32)
    in_part = lax.dot_general(
        gate_slopes, gate_weight, contract_last, preferred_element_type=jnp.float32
    ) + lax.dot_general(up_slopes, up_weight, contract_last, preferred_element_type=jnp.float32)
    finished = scatter_sum_rows(
        jnp.concatenate([out_part, in_part], axis=1), "tensor", n_tensor, TENSOR_LINK
    ).astype(jnp.bfloat16)
    return (finished[:, :model_width], finished[:, model_width:])


def solution(mesh):
    in_specs = (
        P(("dp", "tensor"), "pipe"),
        P(("dp", "tensor"), "pipe"),
        P(("dp", "pipe"), "tensor"),
        P(("dp", "pipe"), "tensor"),
        P("pipe", "tensor"),
        P("pipe", "tensor"),
        P("tensor", "pipe"),
    )
    out_specs = (P(("dp", "tensor"), "pipe"), P(("dp", "tensor"), "pipe"))
    return jax.shard_map(
        per_device, mesh=mesh, in_specs=in_specs, out_specs=out_specs, check_vma=False
    )
```

```python
import functools

import jax
import jax.numpy as jnp
from jax import lax
from jax.experimental import pallas as pl
from jax.experimental.pallas import tpu as pltpu
from jax.sharding import PartitionSpec as P

PIPE_LINK = jnp.float32
TENSOR_LINK = jnp.bfloat16
MESH = pl.DeviceIdType.MESH


def make_slopes(hidden_grad, gate_vals, up_vals):
    gate_wide = gate_vals.astype(jnp.float32)
    up_wide = up_vals.astype(jnp.float32)
    sigma = jax.nn.sigmoid(gate_wide)
    gate_slope = (hidden_grad * up_wide * sigma * (1.0 + gate_wide * (1.0 - sigma))).astype(
        jnp.bfloat16
    )
    up_slope = (hidden_grad * gate_wide * sigma).astype(jnp.bfloat16)
    return jnp.concatenate([gate_slope, up_slope], axis=1)


def gather_rows(block, axis, count):
    sent = jnp.broadcast_to(block[None], (count,) + block.shape)
    got = lax.all_to_all(sent, axis, 0, 0, tiled=False)
    return got.reshape((count * block.shape[0],) + block.shape[1:])


def scatter_sum_rows(partial, axis, count, link_dtype):
    rows = partial.shape[0] // count
    sent = partial.reshape((count, rows) + partial.shape[1:]).astype(link_dtype)
    got = lax.all_to_all(sent, axis, 0, 0, tiled=False)
    return got.astype(jnp.float32).sum(axis=0)


def _ring_gather_kernel(axis, outer, inner, ring_on_inner, halves, x_ref, first_ref, second_ref, send_sems, recv_sems, swap_sems, local_sems):
    me = lax.axis_index(axis)
    o = me // inner
    i = me % inner
    if ring_on_inner:
        ring = inner
        pos, other = i, o
        def at(p, q):
            return q * inner + p
    else:
        ring = outer
        pos, other = o, i
        def at(p, q):
            return p * inner + q
    partner = at(pos, 1 - other)
    up = at(lax.rem(pos + 1, ring), other)
    down = at(lax.rem(pos + ring - 1, ring), other)
    rows = x_ref.shape[1]
    part = rows // halves

    barrier = pltpu.get_barrier_semaphore()
    for peer in (partner, up, down):
        pl.semaphore_signal(barrier, inc=1, device_id={axis: peer}, device_id_type=MESH)
    pl.semaphore_wait(barrier, 3)

    outs = (first_ref, second_ref)
    locals_ = []
    swaps = []
    for d in range(2):
        c = pltpu.make_async_copy(x_ref.at[d], outs[d].at[other, pos], local_sems.at[d])
        c.start()
        locals_.append(c)
        s = pltpu.make_async_remote_copy(
            src_ref=x_ref.at[d], dst_ref=outs[d].at[other, pos],
            send_sem=swap_sems.at[0, d], recv_sem=swap_sems.at[1, d],
            device_id={axis: partner}, device_id_type=MESH)
        s.start()
        swaps.append(s)

    targets = (up, down)
    copies = {}

    def chunk_copy(d, step, which, r):
        slot = lax.rem(pos - step + 1 + ring, ring) if d == 0 else lax.rem(pos + step - 1, ring)
        half = other if which == 0 else 1 - other
        rs = pl.ds(r * part, part)
        if step == 1 and which == 0:
            src = x_ref.at[d, rs]
        else:
            src = outs[d].at[half, slot, rs]
        k = ((d * (ring - 1) + step - 1) * 2 + which) * halves + r
        return pltpu.make_async_remote_copy(
            src_ref=src, dst_ref=outs[d].at[half, slot, rs],
            send_sem=send_sems.at[k], recv_sem=recv_sems.at[k],
            device_id={axis: targets[d]}, device_id_type=MESH)

    for step in range(1, ring):
        for which in range(2):
            if step == 1 and which == 1:
                for s in swaps:
                    s.wait_recv()
            for r in range(halves):
                for d in range(2):
                    if step > 1:
                        copies[(d, step - 1, which, r)].wait_recv()
                    c = chunk_copy(d, step, which, r)
                    c.start()
                    copies[(d, step, which, r)] = c
    for which in range(2):
        for r in range(halves):
            for d in range(2):
                copies[(d, ring - 1, which, r)].wait_recv()
    for c in locals_:
        c.wait()
    for s in swaps:
        s.wait_send()
    for c in copies.values():
        c.wait_send()


def ring_gather(first, second, axis, outer, inner, ring_on_inner, cid, halves=2):
    rows, width = first.shape
    ring = inner if ring_on_inner else outer
    shape = (2, ring, rows, width)
    x = jnp.stack([first, second])
    n_copies = 2 * (ring - 1) * 2 * halves
    f, s = pl.pallas_call(
        functools.partial(_ring_gather_kernel, axis, outer, inner, ring_on_inner, halves),
        out_shape=(jax.ShapeDtypeStruct(shape, first.dtype), jax.ShapeDtypeStruct(shape, second.dtype)),
        in_specs=[pl.BlockSpec(memory_space=pltpu.VMEM)],
        out_specs=(pl.BlockSpec(memory_space=pltpu.VMEM), pl.BlockSpec(memory_space=pltpu.VMEM)),
        scratch_shapes=[
            pltpu.SemaphoreType.DMA((n_copies,)),
            pltpu.SemaphoreType.DMA((n_copies,)),
            pltpu.SemaphoreType.DMA((2, 2)),
            pltpu.SemaphoreType.DMA((2,)),
        ],
        compiler_params=pltpu.CompilerParams(collective_id=cid, has_side_effects=True),
    )(x)
    if ring_on_inner:
        return f.reshape(2 * ring * rows, width), s.reshape(2 * ring * rows, width)
    return (f.transpose(1, 0, 2, 3).reshape(2 * ring * rows, width),
            s.transpose(1, 0, 2, 3).reshape(2 * ring * rows, width))


def per_device(
    forward_acts, backward_grad, stored_gate, stored_up, gate_weight, up_weight, down_weight
):
    n_pipe = lax.axis_size("pipe")
    n_tensor = lax.axis_size("tensor")
    hidden_width = gate_weight.shape[1]
    model_width = forward_acts.shape[1]
    contract_last = (((1,), (1,)), ((), ()))

    whole_acts, whole_grad = ring_gather(
        forward_acts, backward_grad, "tensor", 2, n_tensor // 2, True, 0
    )

    gate_part = jnp.dot(whole_acts, gate_weight, preferred_element_type=jnp.float32)
    up_part = jnp.dot(whole_acts, up_weight, preferred_element_type=jnp.float32)
    grad_part = lax.dot_general(
        whole_grad, down_weight, contract_last, preferred_element_type=jnp.float32
    )
    summed = scatter_sum_rows(
        jnp.concatenate([gate_part, up_part, grad_part], axis=1), "pipe", n_pipe, PIPE_LINK
    )
    gate_pre = summed[:, :hidden_width]
    up_pre = summed[:, hidden_width : 2 * hidden_width]
    hidden_grad = summed[:, 2 * hidden_width :]
    hidden_part = (jax.nn.silu(gate_pre) * up_pre).astype(jnp.bfloat16)
    local_slopes = make_slopes(hidden_grad, stored_gate, stored_up)

    rows = gather_rows(jnp.concatenate([hidden_part, local_slopes], axis=1), "pipe", n_pipe)
    hidden = rows[:, :hidden_width]
    gate_slopes = rows[:, hidden_width : 2 * hidden_width]
    up_slopes = rows[:, 2 * hidden_width :]

    out_part = jnp.dot(hidden, down_weight, preferred_element_type=jnp.float32)
    in_part = lax.dot_general(
        gate_slopes, gate_weight, contract_last, preferred_element_type=jnp.float32
    ) + lax.dot_general(up_slopes, up_weight, contract_last, preferred_element_type=jnp.float32)
    finished = scatter_sum_rows(
        jnp.concatenate([out_part, in_part], axis=1), "tensor", n_tensor, TENSOR_LINK
    ).astype(jnp.bfloat16)
    return (finished[:, :model_width], finished[:, model_width:])


def solution(mesh):
    in_specs = (
        P(("dp", "tensor"), "pipe"),
        P(("dp", "tensor"), "pipe"),
        P(("dp", "pipe"), "tensor"),
        P(("dp", "pipe"), "tensor"),
        P("pipe", "tensor"),
        P("pipe", "tensor"),
        P("tensor", "pipe"),
    )
    out_specs = (P(("dp", "tensor"), "pipe"), P(("dp", "tensor"), "pipe"))
    return jax.shard_map(
        per_device, mesh=mesh, in_specs=in_specs, out_specs=out_specs, check_vma=False
    )
```

```python
import functools

import jax
import jax.numpy as jnp
from jax import lax
from jax.experimental import pallas as pl
from jax.experimental.pallas import tpu as pltpu
from jax.sharding import PartitionSpec as P

PIPE_LINK = jnp.float32
TENSOR_LINK = jnp.bfloat16
MESH = pl.DeviceIdType.MESH


def make_slopes(hidden_grad, gate_vals, up_vals):
    gate_wide = gate_vals.astype(jnp.float32)
    up_wide = up_vals.astype(jnp.float32)
    sigma = jax.nn.sigmoid(gate_wide)
    gate_slope = (hidden_grad * up_wide * sigma * (1.0 + gate_wide * (1.0 - sigma))).astype(
        jnp.bfloat16
    )
    up_slope = (hidden_grad * gate_wide * sigma).astype(jnp.bfloat16)
    return jnp.concatenate([gate_slope, up_slope], axis=1)


def _ring_gather_kernel(axis, outer, inner, ring_on_inner, halves, x_ref, first_ref, second_ref, send_sems, recv_sems, swap_sems, local_sems):
    me = lax.axis_index(axis)
    o = me // inner
    i = me % inner
    if ring_on_inner:
        ring = inner
        pos, other = i, o
        def at(p, q):
            return q * inner + p
    else:
        ring = outer
        pos, other = o, i
        def at(p, q):
            return p * inner + q
    partner = at(pos, 1 - other)
    up = at(lax.rem(pos + 1, ring), other)
    down = at(lax.rem(pos + ring - 1, ring), other)
    rows = x_ref.shape[1]
    part = rows // halves

    barrier = pltpu.get_barrier_semaphore()
    for peer in (partner, up, down):
        pl.semaphore_signal(barrier, inc=1, device_id={axis: peer}, device_id_type=MESH)
    pl.semaphore_wait(barrier, 3)

    outs = (first_ref, second_ref)
    locals_ = []
    swaps = []
    for d in range(2):
        c = pltpu.make_async_copy(x_ref.at[d], outs[d].at[other, pos], local_sems.at[d])
        c.start()
        locals_.append(c)
        s = pltpu.make_async_remote_copy(
            src_ref=x_ref.at[d], dst_ref=outs[d].at[other, pos],
            send_sem=swap_sems.at[0, d], recv_sem=swap_sems.at[1, d],
            device_id={axis: partner}, device_id_type=MESH)
        s.start()
        swaps.append(s)

    targets = (up, down)
    copies = {}

    def chunk_copy(d, step, which, r):
        slot = lax.rem(pos - step + 1 + ring, ring) if d == 0 else lax.rem(pos + step - 1, ring)
        half = other if which == 0 else 1 - other
        rs = pl.ds(r * part, part)
        if step == 1 and which == 0:
            src = x_ref.at[d, rs]
        else:
            src = outs[d].at[half, slot, rs]
        k = ((d * (ring - 1) + step - 1) * 2 + which) * halves + r
        return pltpu.make_async_remote_copy(
            src_ref=src, dst_ref=outs[d].at[half, slot, rs],
            send_sem=send_sems.at[k], recv_sem=recv_sems.at[k],
            device_id={axis: targets[d]}, device_id_type=MESH)

    for step in range(1, ring):
        for which in range(2):
            if step == 1 and which == 1:
                for s in swaps:
                    s.wait_recv()
            for r in range(halves):
                for d in range(2):
                    if step > 1:
                        copies[(d, step - 1, which, r)].wait_recv()
                    c = chunk_copy(d, step, which, r)
                    c.start()
                    copies[(d, step, which, r)] = c
    for which in range(2):
        for r in range(halves):
            for d in range(2):
                copies[(d, ring - 1, which, r)].wait_recv()
    for c in locals_:
        c.wait()
    for s in swaps:
        s.wait_send()
    for c in copies.values():
        c.wait_send()


def ring_gather(first, second, axis, outer, inner, ring_on_inner, cid, halves=2):
    rows, width = first.shape
    ring = inner if ring_on_inner else outer
    shape = (2, ring, rows, width)
    x = jnp.stack([first, second])
    n_copies = 2 * (ring - 1) * 2 * halves
    f, s = pl.pallas_call(
        functools.partial(_ring_gather_kernel, axis, outer, inner, ring_on_inner, halves),
        out_shape=(jax.ShapeDtypeStruct(shape, first.dtype), jax.ShapeDtypeStruct(shape, second.dtype)),
        in_specs=[pl.BlockSpec(memory_space=pltpu.VMEM)],
        out_specs=(pl.BlockSpec(memory_space=pltpu.VMEM), pl.BlockSpec(memory_space=pltpu.VMEM)),
        scratch_shapes=[
            pltpu.SemaphoreType.DMA((n_copies,)),
            pltpu.SemaphoreType.DMA((n_copies,)),
            pltpu.SemaphoreType.DMA((2, 2)),
            pltpu.SemaphoreType.DMA((2,)),
        ],
        compiler_params=pltpu.CompilerParams(collective_id=cid, has_side_effects=True),
    )(x)
    if ring_on_inner:
        return f.reshape(2 * ring * rows, width), s.reshape(2 * ring * rows, width)
    return (f.transpose(1, 0, 2, 3).reshape(2 * ring * rows, width),
            s.transpose(1, 0, 2, 3).reshape(2 * ring * rows, width))


def _exchange_kernel(plan, *refs):
    k = len(plan)
    ins, outs = refs[:k], refs[k:2 * k]
    send_sems, recv_sems, local_sems = refs[2 * k:]
    axes = {}
    for axis, count, _ in plan:
        axes[axis] = count
    barrier = pltpu.get_barrier_semaphore()
    total = 0
    for axis, count in axes.items():
        me = lax.axis_index(axis)
        for d in range(1, count):
            pl.semaphore_signal(barrier, inc=1, device_id={axis: lax.rem(me + d, count)}, device_id_type=MESH)
        total += count - 1
    pl.semaphore_wait(barrier, total)
    started = []
    for e, (axis, count, spread) in enumerate(plan):
        me = lax.axis_index(axis)
        src = ins[e] if spread else ins[e].at[me]
        own = pltpu.make_async_copy(src, outs[e].at[me], local_sems.at[e])
        own.start()
        started.append(own)
    remote = []
    for d in range(1, max(c for _, c, _ in plan)):
        for e, (axis, count, spread) in enumerate(plan):
            if d >= count:
                continue
            me = lax.axis_index(axis)
            peer = lax.rem(me + d, count)
            src = ins[e] if spread else ins[e].at[peer]
            c = pltpu.make_async_remote_copy(
                src_ref=src, dst_ref=outs[e].at[me],
                send_sem=send_sems.at[e, d - 1], recv_sem=recv_sems.at[e, d - 1],
                device_id={axis: peer}, device_id_type=MESH)
            c.start()
            remote.append(c)
    for c in started:
        c.wait()
    for c in remote:
        c.wait_recv()
    for c in remote:
        c.wait_send()


def exchange(items, cid):
    plan = tuple((axis, count, spread) for _, axis, count, spread in items)
    shapes = []
    for x, axis, count, spread in items:
        shape = (count,) + x.shape if spread else x.shape
        shapes.append(jax.ShapeDtypeStruct(shape, x.dtype))
    widest = max(count for _, _, count, _ in items)
    return pl.pallas_call(
        functools.partial(_exchange_kernel, plan),
        out_shape=tuple(shapes),
        in_specs=[pl.BlockSpec(memory_space=pl.ANY)] * len(items),
        out_specs=tuple(pl.BlockSpec(memory_space=pl.ANY) for _ in items),
        scratch_shapes=[
            pltpu.SemaphoreType.DMA((len(items), widest - 1)),
            pltpu.SemaphoreType.DMA((len(items), widest - 1)),
            pltpu.SemaphoreType.DMA((len(items),)),
        ],
        compiler_params=pltpu.CompilerParams(collective_id=cid, has_side_effects=True),
    )(*[x for x, _, _, _ in items])


def per_device(
    forward_acts, backward_grad, stored_gate, stored_up, gate_weight, up_weight, down_weight
):
    n_pipe = lax.axis_size("pipe")
    n_tensor = lax.axis_size("tensor")
    hidden_width = gate_weight.shape[1]
    model_width = forward_acts.shape[1]
    half = model_width // 2
    contract_last = (((1,), (1,)), ((), ()))

    def blocks(partial, count, dtype):
        return partial.reshape((count, partial.shape[0] // count) + partial.shape[1:]).astype(dtype)

    acts_low, acts_high = ring_gather(
        forward_acts[:, :half], forward_acts[:, half:], "tensor", 2, n_tensor // 2, True, 0
    )
    whole_acts = jnp.concatenate([acts_low, acts_high], axis=1)
    gate_part = jnp.dot(whole_acts, gate_weight, preferred_element_type=jnp.float32)
    up_part = jnp.dot(whole_acts, up_weight, preferred_element_type=jnp.float32)

    got_proj, got_grad = exchange(
        [
            (blocks(jnp.concatenate([gate_part, up_part], axis=1), n_pipe, PIPE_LINK), "pipe", n_pipe, False),
            (backward_grad, "tensor", n_tensor, True),
        ],
        1,
    )
    summed = got_proj.astype(jnp.float32).sum(axis=0)
    hidden_part = (jax.nn.silu(summed[:, :hidden_width]) * summed[:, hidden_width:]).astype(
        jnp.bfloat16
    )
    whole_grad = got_grad.reshape(n_tensor * backward_grad.shape[0], model_width)
    grad_part = lax.dot_general(
        whole_grad, down_weight, contract_last, preferred_element_type=jnp.float32
    )

    got_hidden, got_hgrad = exchange(
        [
            (hidden_part, "pipe", n_pipe, True),
            (blocks(grad_part, n_pipe, PIPE_LINK), "pipe", n_pipe, False),
        ],
        2,
    )
    hidden = got_hidden.reshape(n_pipe * hidden_part.shape[0], hidden_width)
    hidden_grad = got_hgrad.astype(jnp.float32).sum(axis=0)
    local_slopes = make_slopes(hidden_grad, stored_gate, stored_up)
    out_part = jnp.dot(hidden, down_weight, preferred_element_type=jnp.float32)

    got_out, got_slopes = exchange(
        [
            (blocks(out_part, n_tensor, TENSOR_LINK), "tensor", n_tensor, False),
            (local_slopes, "pipe", n_pipe, True),
        ],
        3,
    )
    layer_output = got_out.astype(jnp.float32).sum(axis=0).astype(jnp.bfloat16)
    all_slopes = got_slopes.reshape(n_pipe * local_slopes.shape[0], 2 * hidden_width)
    in_part = lax.dot_general(
        all_slopes[:, :hidden_width], gate_weight, contract_last, preferred_element_type=jnp.float32
    ) + lax.dot_general(
        all_slopes[:, hidden_width:], up_weight, contract_last, preferred_element_type=jnp.float32
    )

    (got_in,) = exchange([(blocks(in_part, n_tensor, TENSOR_LINK), "tensor", n_tensor, False)], 4)
    input_grad = got_in.astype(jnp.float32).sum(axis=0).astype(jnp.bfloat16)
    return (layer_output, input_grad)


def solution(mesh):
    in_specs = (
        P(("dp", "tensor"), "pipe"),
        P(("dp", "tensor"), "pipe"),
        P(("dp", "pipe"), "tensor"),
        P(("dp", "pipe"), "tensor"),
        P("pipe", "tensor"),
        P("pipe", "tensor"),
        P("tensor", "pipe"),
    )
    out_specs = (P(("dp", "tensor"), "pipe"), P(("dp", "tensor"), "pipe"))
    return jax.shard_map(
        per_device, mesh=mesh, in_specs=in_specs, out_specs=out_specs, check_vma=False
    )
```

```python
import functools

import jax
import jax.numpy as jnp
from jax import lax
from jax.experimental import pallas as pl
from jax.experimental.pallas import tpu as pltpu
from jax.sharding import PartitionSpec as P

PIPE_LINK = jnp.float32
TENSOR_LINK = jnp.bfloat16
MESH = pl.DeviceIdType.MESH


def make_slopes(hidden_grad, gate_vals, up_vals):
    gate_wide = gate_vals.astype(jnp.float32)
    up_wide = up_vals.astype(jnp.float32)
    sigma = jax.nn.sigmoid(gate_wide)
    gate_slope = (hidden_grad * up_wide * sigma * (1.0 + gate_wide * (1.0 - sigma))).astype(
        jnp.bfloat16
    )
    up_slope = (hidden_grad * gate_wide * sigma).astype(jnp.bfloat16)
    return jnp.concatenate([gate_slope, up_slope], axis=1)


def gather_rows(block, axis, count):
    sent = jnp.broadcast_to(block[None], (count,) + block.shape)
    got = lax.all_to_all(sent, axis, 0, 0, tiled=False)
    return got.reshape((count * block.shape[0],) + block.shape[1:])


def scatter_sum_rows(partial, axis, count, link_dtype):
    rows = partial.shape[0] // count
    sent = partial.reshape((count, rows) + partial.shape[1:]).astype(link_dtype)
    got = lax.all_to_all(sent, axis, 0, 0, tiled=False)
    return got.astype(jnp.float32).sum(axis=0)


def _ring_gather_kernel(axis, outer, inner, ring_on_inner, halves, x_ref, first_ref, second_ref, send_sems, recv_sems, swap_sems, local_sems):
    me = lax.axis_index(axis)
    o = me // inner
    i = me % inner
    if ring_on_inner:
        ring = inner
        pos, other = i, o
        def at(p, q):
            return q * inner + p
    else:
        ring = outer
        pos, other = o, i
        def at(p, q):
            return p * inner + q
    partner = at(pos, 1 - other)
    up = at(lax.rem(pos + 1, ring), other)
    down = at(lax.rem(pos + ring - 1, ring), other)
    rows = x_ref.shape[1]
    part = rows // halves
    steps = (ring // 2, (ring - 1) // 2)

    barrier = pltpu.get_barrier_semaphore()
    for peer in (partner, up, down):
        pl.semaphore_signal(barrier, inc=1, device_id={axis: peer}, device_id_type=MESH)
    pl.semaphore_wait(barrier, 3)

    outs = (first_ref, second_ref)
    locals_ = []
    swaps = []
    for a in range(2):
        c = pltpu.make_async_copy(x_ref.at[a], outs[a].at[other, pos], local_sems.at[a])
        c.start()
        locals_.append(c)
        s = pltpu.make_async_remote_copy(
            src_ref=x_ref.at[a], dst_ref=outs[a].at[other, pos],
            send_sem=swap_sems.at[0, a], recv_sem=swap_sems.at[1, a],
            device_id={axis: partner}, device_id_type=MESH)
        s.start()
        swaps.append(s)

    targets = (up, down)
    copies = {}

    def chunk_copy(d, step, which, r, a):
        slot = lax.rem(pos - step + 1 + ring, ring) if d == 0 else lax.rem(pos + step - 1, ring)
        half = other if which == 0 else 1 - other
        rs = pl.ds(r * part, part)
        if step == 1 and which == 0:
            src = x_ref.at[a, rs]
        else:
            src = outs[a].at[half, slot, rs]
        k = (((d * ring + step - 1) * 2 + which) * halves + r) * 2 + a
        return pltpu.make_async_remote_copy(
            src_ref=src, dst_ref=outs[a].at[half, slot, rs],
            send_sem=send_sems.at[k], recv_sem=recv_sems.at[k],
            device_id={axis: targets[d]}, device_id_type=MESH)

    for step in range(1, steps[0] + 1):
        for which in range(2):
            if step == 1 and which == 1:
                for s in swaps:
                    s.wait_recv()
            for r in range(halves):
                for a in range(2):
                    for d in range(2):
                        if step > steps[d]:
                            continue
                        if step > 1:
                            copies[(d, step - 1, which, r, a)].wait_recv()
                        c = chunk_copy(d, step, which, r, a)
                        c.start()
                        copies[(d, step, which, r, a)] = c
    for d in range(2):
        if steps[d] == 0:
            continue
        for which in range(2):
            for r in range(halves):
                for a in range(2):
                    copies[(d, steps[d], which, r, a)].wait_recv()
    for c in locals_:
        c.wait()
    for s in swaps:
        s.wait_send()
    for c in copies.values():
        c.wait_send()


def ring_gather(first, second, axis, outer, inner, ring_on_inner, cid, halves=2):
    rows, width = first.shape
    ring = inner if ring_on_inner else outer
    shape = (2, ring, rows, width)
    x = jnp.stack([first, second])
    n_copies = 2 * ring * 2 * halves * 2
    f, s = pl.pallas_call(
        functools.partial(_ring_gather_kernel, axis, outer, inner, ring_on_inner, halves),
        out_shape=(jax.ShapeDtypeStruct(shape, first.dtype), jax.ShapeDtypeStruct(shape, second.dtype)),
        in_specs=[pl.BlockSpec(memory_space=pltpu.VMEM)],
        out_specs=(pl.BlockSpec(memory_space=pltpu.VMEM), pl.BlockSpec(memory_space=pltpu.VMEM)),
        scratch_shapes=[
            pltpu.SemaphoreType.DMA((n_copies,)),
            pltpu.SemaphoreType.DMA((n_copies,)),
            pltpu.SemaphoreType.DMA((2, 2)),
            pltpu.SemaphoreType.DMA((2,)),
        ],
        compiler_params=pltpu.CompilerParams(collective_id=cid, has_side_effects=True),
    )(x)
    if ring_on_inner:
        return f.reshape(2 * ring * rows, width), s.reshape(2 * ring * rows, width)
    return (f.transpose(1, 0, 2, 3).reshape(2 * ring * rows, width),
            s.transpose(1, 0, 2, 3).reshape(2 * ring * rows, width))


def per_device(
    forward_acts, backward_grad, stored_gate, stored_up, gate_weight, up_weight, down_weight
):
    n_pipe = lax.axis_size("pipe")
    n_tensor = lax.axis_size("tensor")
    hidden_width = gate_weight.shape[1]
    model_width = forward_acts.shape[1]
    contract_last = (((1,), (1,)), ((), ()))

    whole_acts, whole_grad = ring_gather(
        forward_acts, backward_grad, "tensor", 2, n_tensor // 2, True, 0
    )

    gate_part = jnp.dot(whole_acts, gate_weight, preferred_element_type=jnp.float32)
    up_part = jnp.dot(whole_acts, up_weight, preferred_element_type=jnp.float32)
    grad_part = lax.dot_general(
        whole_grad, down_weight, contract_last, preferred_element_type=jnp.float32
    )
    summed = scatter_sum_rows(
        jnp.concatenate([gate_part, up_part, grad_part], axis=1), "pipe", n_pipe, PIPE_LINK
    )
    gate_pre = summed[:, :hidden_width]
    up_pre = summed[:, hidden_width : 2 * hidden_width]
    hidden_grad = summed[:, 2 * hidden_width :]
    hidden_part = (jax.nn.silu(gate_pre) * up_pre).astype(jnp.bfloat16)
    local_slopes = make_slopes(hidden_grad, stored_gate, stored_up)

    rows = gather_rows(jnp.concatenate([hidden_part, local_slopes], axis=1), "pipe", n_pipe)
    hidden = rows[:, :hidden_width]
    gate_slopes = rows[:, hidden_width : 2 * hidden_width]
    up_slopes = rows[:, 2 * hidden_width :]

    out_part = jnp.dot(hidden, down_weight, preferred_element_type=jnp.float32)
    in_part = lax.dot_general(
        gate_slopes, gate_weight, contract_last, preferred_element_type=jnp.float32
    ) + lax.dot_general(up_slopes, up_weight, contract_last, preferred_element_type=jnp.float32)
    finished = scatter_sum_rows(
        jnp.concatenate([out_part, in_part], axis=1), "tensor", n_tensor, TENSOR_LINK
    ).astype(jnp.bfloat16)
    return (finished[:, :model_width], finished[:, model_width:])


def solution(mesh):
    in_specs = (
        P(("dp", "tensor"), "pipe"),
        P(("dp", "tensor"), "pipe"),
        P(("dp", "pipe"), "tensor"),
        P(("dp", "pipe"), "tensor"),
        P("pipe", "tensor"),
        P("pipe", "tensor"),
        P("tensor", "pipe"),
    )
    out_specs = (P(("dp", "tensor"), "pipe"), P(("dp", "tensor"), "pipe"))
    return jax.shard_map(
        per_device, mesh=mesh, in_specs=in_specs, out_specs=out_specs, check_vma=False
    )
```

```python
import functools

import jax
import jax.numpy as jnp
from jax import lax
from jax.experimental import pallas as pl
from jax.experimental.pallas import tpu as pltpu
from jax.sharding import PartitionSpec as P

PIPE_LINK = jnp.float32
TENSOR_LINK = jnp.bfloat16
MESH = pl.DeviceIdType.MESH


def make_slopes(hidden_grad, gate_vals, up_vals):
    gate_wide = gate_vals.astype(jnp.float32)
    up_wide = up_vals.astype(jnp.float32)
    sigma = jax.nn.sigmoid(gate_wide)
    gate_slope = (hidden_grad * up_wide * sigma * (1.0 + gate_wide * (1.0 - sigma))).astype(
        jnp.bfloat16
    )
    up_slope = (hidden_grad * gate_wide * sigma).astype(jnp.bfloat16)
    return jnp.concatenate([gate_slope, up_slope], axis=1)


def gather_rows(block, axis, count):
    sent = jnp.broadcast_to(block[None], (count,) + block.shape)
    got = lax.all_to_all(sent, axis, 0, 0, tiled=False)
    return got.reshape((count * block.shape[0],) + block.shape[1:])


def scatter_sum_rows(partial, axis, count, link_dtype):
    rows = partial.shape[0] // count
    sent = partial.reshape((count, rows) + partial.shape[1:]).astype(link_dtype)
    got = lax.all_to_all(sent, axis, 0, 0, tiled=False)
    return got.astype(jnp.float32).sum(axis=0)


def _ring_gather_kernel(axis, outer, inner, ring_on_inner, halves, x_ref, first_ref, second_ref, send_sems, recv_sems, swap_sems, local_sems):
    me = lax.axis_index(axis)
    o = me // inner
    i = me % inner
    if ring_on_inner:
        ring = inner
        pos, other = i, o
        def at(p, q):
            return q * inner + p
    else:
        ring = outer
        pos, other = o, i
        def at(p, q):
            return p * inner + q
    partner = at(pos, 1 - other)
    up = at(lax.rem(pos + 1, ring), other)
    down = at(lax.rem(pos + ring - 1, ring), other)
    rows = x_ref.shape[1]
    part = rows // halves
    steps = (ring // 2, (ring - 1) // 2)

    barrier = pltpu.get_barrier_semaphore()
    for peer in (partner, up, down):
        pl.semaphore_signal(barrier, inc=1, device_id={axis: peer}, device_id_type=MESH)
    pl.semaphore_wait(barrier, 3)

    outs = (first_ref, second_ref)
    locals_ = []
    swaps = []
    for a in range(2):
        c = pltpu.make_async_copy(x_ref.at[a], outs[a].at[other, pos], local_sems.at[a])
        c.start()
        locals_.append(c)
        s = pltpu.make_async_remote_copy(
            src_ref=x_ref.at[a], dst_ref=outs[a].at[other, pos],
            send_sem=swap_sems.at[0, a], recv_sem=swap_sems.at[1, a],
            device_id={axis: partner}, device_id_type=MESH)
        s.start()
        swaps.append(s)

    targets = (up, down)
    copies = {}

    def chunk_copy(d, step, which, r, a):
        slot = lax.rem(pos - step + 1 + ring, ring) if d == 0 else lax.rem(pos + step - 1, ring)
        half = other if which == 0 else 1 - other
        rs = pl.ds(r * part, part)
        if step == 1 and which == 0:
            src = x_ref.at[a, rs]
        else:
            src = outs[a].at[half, slot, rs]
        k = (((d * ring + step - 1) * 2 + which) * halves + r) * 2 + a
        return pltpu.make_async_remote_copy(
            src_ref=src, dst_ref=outs[a].at[half, slot, rs],
            send_sem=send_sems.at[k], recv_sem=recv_sems.at[k],
            device_id={axis: targets[d]}, device_id_type=MESH)

    for step in range(1, steps[0] + 1):
        for which in range(2):
            if step == 1 and which == 1:
                for s in swaps:
                    s.wait_recv()
            for r in range(halves):
                for a in range(2):
                    for d in range(2):
                        if step > steps[d]:
                            continue
                        if step > 1:
                            copies[(d, step - 1, which, r, a)].wait_recv()
                        c = chunk_copy(d, step, which, r, a)
                        c.start()
                        copies[(d, step, which, r, a)] = c
    for d in range(2):
        if steps[d] == 0:
            continue
        for which in range(2):
            for r in range(halves):
                for a in range(2):
                    copies[(d, steps[d], which, r, a)].wait_recv()
    for c in locals_:
        c.wait()
    for s in swaps:
        s.wait_send()
    for c in copies.values():
        c.wait_send()


def ring_gather(first, second, axis, outer, inner, ring_on_inner, cid, halves=2):
    rows, width = first.shape
    ring = inner if ring_on_inner else outer
    shape = (2, ring, rows, width)
    x = jnp.stack([first, second])
    n_copies = 2 * ring * 2 * halves * 2
    f, s = pl.pallas_call(
        functools.partial(_ring_gather_kernel, axis, outer, inner, ring_on_inner, halves),
        out_shape=(jax.ShapeDtypeStruct(shape, first.dtype), jax.ShapeDtypeStruct(shape, second.dtype)),
        in_specs=[pl.BlockSpec(memory_space=pltpu.VMEM)],
        out_specs=(pl.BlockSpec(memory_space=pltpu.VMEM), pl.BlockSpec(memory_space=pltpu.VMEM)),
        scratch_shapes=[
            pltpu.SemaphoreType.DMA((n_copies,)),
            pltpu.SemaphoreType.DMA((n_copies,)),
            pltpu.SemaphoreType.DMA((2, 2)),
            pltpu.SemaphoreType.DMA((2,)),
        ],
        compiler_params=pltpu.CompilerParams(collective_id=cid, has_side_effects=True),
    )(x)
    if ring_on_inner:
        return f.reshape(2 * ring * rows, width), s.reshape(2 * ring * rows, width)
    return (f.transpose(1, 0, 2, 3).reshape(2 * ring * rows, width),
            s.transpose(1, 0, 2, 3).reshape(2 * ring * rows, width))


def _ring_sum_kernel(axis, outer, chunks, x_ref, out_ref, send_buf, recv_buf, swap_buf, send_sems, recv_sems, swap_sems):
    me = lax.axis_index(axis)
    y = me // 2
    x = me % 2
    ring = outer
    up = lax.rem(y + 1, ring) * 2 + x
    down = lax.rem(y + ring - 1, ring) * 2 + x
    partner = y * 2 + 1 - x
    rows = x_ref.shape[1]
    half = rows // 2
    part = half // chunks

    barrier = pltpu.get_barrier_semaphore()
    for peer in (partner, up, down):
        pl.semaphore_signal(barrier, inc=1, device_id={axis: peer}, device_id_type=MESH)
    pl.semaphore_wait(barrier, 3)

    targets = (up, down)
    copies = {}

    def dest(d, step):
        return lax.rem(y - step + ring, ring) if d == 0 else lax.rem(y + step, ring)

    for step in range(1, ring):
        for c in range(chunks):
            for d in range(2):
                rs = pl.ds(d * half + c * part, part)
                blocks = pl.ds(dest(d, step) * 2, 2)
                if step == 1:
                    src = x_ref.at[blocks, rs]
                else:
                    copies[(d, step - 1, c)].wait_recv()
                    send_buf[d, step, :, pl.ds(c * part, part)] = (
                        recv_buf[d, step - 1, :, pl.ds(c * part, part)] + x_ref[blocks, rs]
                    )
                    src = send_buf.at[d, step, :, pl.ds(c * part, part)]
                cp = pltpu.make_async_remote_copy(
                    src_ref=src, dst_ref=recv_buf.at[d, step, :, pl.ds(c * part, part)],
                    send_sem=send_sems.at[d, step, c], recv_sem=recv_sems.at[d, step, c],
                    device_id={axis: targets[d]}, device_id_type=MESH)
                cp.start()
                copies[(d, step, c)] = cp
    swaps = []
    for c in range(chunks):
        for d in range(2):
            rs = pl.ds(d * half + c * part, part)
            local = pl.ds(c * part, part)
            copies[(d, ring - 1, c)].wait_recv()
            swap_buf[0, d, local] = recv_buf[d, ring - 1, 1 - x, local] + x_ref[y * 2 + 1 - x, rs]
            out_ref[rs] = recv_buf[d, ring - 1, x, local] + x_ref[y * 2 + x, rs]
            sw = pltpu.make_async_remote_copy(
                src_ref=swap_buf.at[0, d, local], dst_ref=swap_buf.at[1, d, local],
                send_sem=swap_sems.at[0, d, c], recv_sem=swap_sems.at[1, d, c],
                device_id={axis: partner}, device_id_type=MESH)
            sw.start()
            swaps.append((d, c, sw))
    for d, c, sw in swaps:
        rs = pl.ds(d * half + c * part, part)
        sw.wait_recv()
        out_ref[rs] = out_ref[rs] + swap_buf[1, d, pl.ds(c * part, part)]
    for d, c, sw in swaps:
        sw.wait_send()
    for cp in copies.values():
        cp.wait_send()


def ring_sum(partial, axis, outer, cid, chunks=2):
    count, rows, width = partial.shape
    half = rows // 2
    return pl.pallas_call(
        functools.partial(_ring_sum_kernel, axis, outer, chunks),
        out_shape=jax.ShapeDtypeStruct((rows, width), jnp.float32),
        in_specs=[pl.BlockSpec(memory_space=pltpu.VMEM)],
        out_specs=pl.BlockSpec(memory_space=pltpu.VMEM),
        scratch_shapes=[
            pltpu.VMEM((2, outer, 2, half, width), jnp.float32),
            pltpu.VMEM((2, outer, 2, half, width), jnp.float32),
            pltpu.VMEM((2, 2, half, width), jnp.float32),
            pltpu.SemaphoreType.DMA((2, outer, chunks)),
            pltpu.SemaphoreType.DMA((2, outer, chunks)),
            pltpu.SemaphoreType.DMA((2, 2, chunks)),
        ],
        compiler_params=pltpu.CompilerParams(collective_id=cid, has_side_effects=True, vmem_limit_bytes=60 * 1024 * 1024),
    )(partial)


def per_device(
    forward_acts, backward_grad, stored_gate, stored_up, gate_weight, up_weight, down_weight
):
    n_pipe = lax.axis_size("pipe")
    n_tensor = lax.axis_size("tensor")
    hidden_width = gate_weight.shape[1]
    model_width = forward_acts.shape[1]
    contract_last = (((1,), (1,)), ((), ()))

    whole_acts, whole_grad = ring_gather(
        forward_acts, backward_grad, "tensor", 2, n_tensor // 2, True, 0
    )

    gate_part = jnp.dot(whole_acts, gate_weight, preferred_element_type=jnp.float32)
    up_part = jnp.dot(whole_acts, up_weight, preferred_element_type=jnp.float32)
    grad_part = lax.dot_general(
        whole_grad, down_weight, contract_last, preferred_element_type=jnp.float32
    )
    partials = jnp.concatenate([gate_part, up_part, grad_part], axis=1)
    summed = ring_sum(
        partials.reshape((n_pipe, partials.shape[0] // n_pipe, partials.shape[1])),
        "pipe",
        n_pipe // 2,
        1,
    )
    gate_pre = summed[:, :hidden_width]
    up_pre = summed[:, hidden_width : 2 * hidden_width]
    hidden_grad = summed[:, 2 * hidden_width :]
    hidden_part = (jax.nn.silu(gate_pre) * up_pre).astype(jnp.bfloat16)
    local_slopes = make_slopes(hidden_grad, stored_gate, stored_up)

    rows = gather_rows(jnp.concatenate([hidden_part, local_slopes], axis=1), "pipe", n_pipe)
    hidden = rows[:, :hidden_width]
    gate_slopes = rows[:, hidden_width : 2 * hidden_width]
    up_slopes = rows[:, 2 * hidden_width :]

    out_part = jnp.dot(hidden, down_weight, preferred_element_type=jnp.float32)
    in_part = lax.dot_general(
        gate_slopes, gate_weight, contract_last, preferred_element_type=jnp.float32
    ) + lax.dot_general(up_slopes, up_weight, contract_last, preferred_element_type=jnp.float32)
    finished = scatter_sum_rows(
        jnp.concatenate([out_part, in_part], axis=1), "tensor", n_tensor, TENSOR_LINK
    ).astype(jnp.bfloat16)
    return (finished[:, :model_width], finished[:, model_width:])


def solution(mesh):
    in_specs = (
        P(("dp", "tensor"), "pipe"),
        P(("dp", "tensor"), "pipe"),
        P(("dp", "pipe"), "tensor"),
        P(("dp", "pipe"), "tensor"),
        P("pipe", "tensor"),
        P("pipe", "tensor"),
        P("tensor", "pipe"),
    )
    out_specs = (P(("dp", "tensor"), "pipe"), P(("dp", "tensor"), "pipe"))
    return jax.shard_map(
        per_device, mesh=mesh, in_specs=in_specs, out_specs=out_specs, check_vma=False
    )
```

```python
import functools

import jax
import jax.numpy as jnp
from jax import lax
from jax.experimental import pallas as pl
from jax.experimental.pallas import tpu as pltpu
from jax.sharding import PartitionSpec as P

PIPE_LINK = jnp.float32
TENSOR_LINK = jnp.bfloat16
MESH = pl.DeviceIdType.MESH


def make_slopes(hidden_grad, gate_vals, up_vals):
    gate_wide = gate_vals.astype(jnp.float32)
    up_wide = up_vals.astype(jnp.float32)
    sigma = jax.nn.sigmoid(gate_wide)
    gate_slope = (hidden_grad * up_wide * sigma * (1.0 + gate_wide * (1.0 - sigma))).astype(
        jnp.bfloat16
    )
    up_slope = (hidden_grad * gate_wide * sigma).astype(jnp.bfloat16)
    return jnp.concatenate([gate_slope, up_slope], axis=1)


def gather_rows(block, axis, count):
    sent = jnp.broadcast_to(block[None], (count,) + block.shape)
    got = lax.all_to_all(sent, axis, 0, 0, tiled=False)
    return got.reshape((count * block.shape[0],) + block.shape[1:])


def scatter_sum_rows(partial, axis, count, link_dtype):
    rows = partial.shape[0] // count
    sent = partial.reshape((count, rows) + partial.shape[1:]).astype(link_dtype)
    got = lax.all_to_all(sent, axis, 0, 0, tiled=False)
    return got.astype(jnp.float32).sum(axis=0)


def _ring_gather_kernel(axis, outer, inner, ring_on_inner, halves, x_ref, first_ref, second_ref, send_sems, recv_sems, swap_sems, local_sems):
    me = lax.axis_index(axis)
    o = me // inner
    i = me % inner
    if ring_on_inner:
        ring = inner
        pos, other = i, o
        def at(p, q):
            return q * inner + p
    else:
        ring = outer
        pos, other = o, i
        def at(p, q):
            return p * inner + q
    partner = at(pos, 1 - other)
    up = at(lax.rem(pos + 1, ring), other)
    down = at(lax.rem(pos + ring - 1, ring), other)
    rows = x_ref.shape[1]
    part = rows // halves
    steps = (ring // 2, (ring - 1) // 2)

    barrier = pltpu.get_barrier_semaphore()
    for peer in (partner, up, down):
        pl.semaphore_signal(barrier, inc=1, device_id={axis: peer}, device_id_type=MESH)
    pl.semaphore_wait(barrier, 3)

    outs = (first_ref, second_ref)
    locals_ = []
    swaps = []
    for a in range(2):
        c = pltpu.make_async_copy(x_ref.at[a], outs[a].at[other, pos], local_sems.at[a])
        c.start()
        locals_.append(c)
        s = pltpu.make_async_remote_copy(
            src_ref=x_ref.at[a], dst_ref=outs[a].at[other, pos],
            send_sem=swap_sems.at[0, a], recv_sem=swap_sems.at[1, a],
            device_id={axis: partner}, device_id_type=MESH)
        s.start()
        swaps.append(s)

    targets = (up, down)
    copies = {}

    def chunk_copy(d, step, which, r, a):
        slot = lax.rem(pos - step + 1 + ring, ring) if d == 0 else lax.rem(pos + step - 1, ring)
        half = other if which == 0 else 1 - other
        rs = pl.ds(r * part, part)
        if step == 1 and which == 0:
            src = x_ref.at[a, rs]
        else:
            src = outs[a].at[half, slot, rs]
        k = (((d * ring + step - 1) * 2 + which) * halves + r) * 2 + a
        return pltpu.make_async_remote_copy(
            src_ref=src, dst_ref=outs[a].at[half, slot, rs],
            send_sem=send_sems.at[k], recv_sem=recv_sems.at[k],
            device_id={axis: targets[d]}, device_id_type=MESH)

    for step in range(1, steps[0] + 1):
        for which in range(2):
            if step == 1 and which == 1:
                for s in swaps:
                    s.wait_recv()
            for r in range(halves):
                for a in range(2):
                    for d in range(2):
                        if step > steps[d]:
                            continue
                        if step > 1:
                            copies[(d, step - 1, which, r, a)].wait_recv()
                        c = chunk_copy(d, step, which, r, a)
                        c.start()
                        copies[(d, step, which, r, a)] = c
    for d in range(2):
        if steps[d] == 0:
            continue
        for which in range(2):
            for r in range(halves):
                for a in range(2):
                    copies[(d, steps[d], which, r, a)].wait_recv()
    for c in locals_:
        c.wait()
    for s in swaps:
        s.wait_send()
    for c in copies.values():
        c.wait_send()


def ring_gather(first, second, axis, outer, inner, ring_on_inner, cid, halves=2):
    rows, width = first.shape
    ring = inner if ring_on_inner else outer
    shape = (2, ring, rows, width)
    x = jnp.stack([first, second])
    n_copies = 2 * ring * 2 * halves * 2
    f, s = pl.pallas_call(
        functools.partial(_ring_gather_kernel, axis, outer, inner, ring_on_inner, halves),
        out_shape=(jax.ShapeDtypeStruct(shape, first.dtype), jax.ShapeDtypeStruct(shape, second.dtype)),
        in_specs=[pl.BlockSpec(memory_space=pltpu.VMEM)],
        out_specs=(pl.BlockSpec(memory_space=pltpu.VMEM), pl.BlockSpec(memory_space=pltpu.VMEM)),
        scratch_shapes=[
            pltpu.SemaphoreType.DMA((n_copies,)),
            pltpu.SemaphoreType.DMA((n_copies,)),
            pltpu.SemaphoreType.DMA((2, 2)),
            pltpu.SemaphoreType.DMA((2,)),
        ],
        compiler_params=pltpu.CompilerParams(collective_id=cid, has_side_effects=True),
    )(x)
    if ring_on_inner:
        return f.reshape(2 * ring * rows, width), s.reshape(2 * ring * rows, width)
    return (f.transpose(1, 0, 2, 3).reshape(2 * ring * rows, width),
            s.transpose(1, 0, 2, 3).reshape(2 * ring * rows, width))


def _ring_sum_kernel(axis, outer, chunks, x_ref, out_ref, send_buf, recv_buf, swap_buf, send_sems, recv_sems, swap_sems):
    me = lax.axis_index(axis)
    y = me // 2
    x = me % 2
    ring = outer
    up = lax.rem(y + 1, ring) * 2 + x
    down = lax.rem(y + ring - 1, ring) * 2 + x
    partner = y * 2 + 1 - x
    rows = x_ref.shape[1]
    half = rows // 2
    part = half // chunks

    barrier = pltpu.get_barrier_semaphore()
    for peer in (partner, up, down):
        pl.semaphore_signal(barrier, inc=1, device_id={axis: peer}, device_id_type=MESH)
    pl.semaphore_wait(barrier, 3)

    targets = (up, down)
    copies = {}

    def dest(d, step):
        return lax.rem(y - step + ring, ring) if d == 0 else lax.rem(y + step, ring)

    for step in range(1, ring):
        for c in range(chunks):
            for d in range(2):
                rs = pl.ds(d * half + c * part, part)
                blocks = pl.ds(dest(d, step) * 2, 2)
                if step == 1:
                    src = x_ref.at[blocks, rs]
                else:
                    copies[(d, step - 1, c)].wait_recv()
                    send_buf[d, step, :, pl.ds(c * part, part)] = (
                        recv_buf[d, step - 1, :, pl.ds(c * part, part)] + x_ref[blocks, rs]
                    )
                    src = send_buf.at[d, step, :, pl.ds(c * part, part)]
                cp = pltpu.make_async_remote_copy(
                    src_ref=src, dst_ref=recv_buf.at[d, step, :, pl.ds(c * part, part)],
                    send_sem=send_sems.at[d, step, c], recv_sem=recv_sems.at[d, step, c],
                    device_id={axis: targets[d]}, device_id_type=MESH)
                cp.start()
                copies[(d, step, c)] = cp
    swaps = []
    for c in range(chunks):
        for d in range(2):
            rs = pl.ds(d * half + c * part, part)
            local = pl.ds(c * part, part)
            copies[(d, ring - 1, c)].wait_recv()
            swap_buf[0, d, local] = recv_buf[d, ring - 1, 1 - x, local] + x_ref[y * 2 + 1 - x, rs]
            out_ref[rs] = recv_buf[d, ring - 1, x, local] + x_ref[y * 2 + x, rs]
            sw = pltpu.make_async_remote_copy(
                src_ref=swap_buf.at[0, d, local], dst_ref=swap_buf.at[1, d, local],
                send_sem=swap_sems.at[0, d, c], recv_sem=swap_sems.at[1, d, c],
                device_id={axis: partner}, device_id_type=MESH)
            sw.start()
            swaps.append((d, c, sw))
    for d, c, sw in swaps:
        rs = pl.ds(d * half + c * part, part)
        sw.wait_recv()
        out_ref[rs] = out_ref[rs] + swap_buf[1, d, pl.ds(c * part, part)]
    for d, c, sw in swaps:
        sw.wait_send()
    for cp in copies.values():
        cp.wait_send()


def ring_sum(partial, axis, outer, cid, chunks=4):
    count, rows, width = partial.shape
    half = rows // 2
    return pl.pallas_call(
        functools.partial(_ring_sum_kernel, axis, outer, chunks),
        out_shape=jax.ShapeDtypeStruct((rows, width), jnp.float32),
        in_specs=[pl.BlockSpec(memory_space=pltpu.VMEM)],
        out_specs=pl.BlockSpec(memory_space=pltpu.VMEM),
        scratch_shapes=[
            pltpu.VMEM((2, outer, 2, half, width), jnp.float32),
            pltpu.VMEM((2, outer, 2, half, width), jnp.float32),
            pltpu.VMEM((2, 2, half, width), jnp.float32),
            pltpu.SemaphoreType.DMA((2, outer, chunks)),
            pltpu.SemaphoreType.DMA((2, outer, chunks)),
            pltpu.SemaphoreType.DMA((2, 2, chunks)),
        ],
        compiler_params=pltpu.CompilerParams(collective_id=cid, has_side_effects=True, vmem_limit_bytes=60 * 1024 * 1024),
    )(partial)


def per_device(
    forward_acts, backward_grad, stored_gate, stored_up, gate_weight, up_weight, down_weight
):
    n_pipe = lax.axis_size("pipe")
    n_tensor = lax.axis_size("tensor")
    hidden_width = gate_weight.shape[1]
    model_width = forward_acts.shape[1]
    contract_last = (((1,), (1,)), ((), ()))

    whole_acts, whole_grad = ring_gather(
        forward_acts, backward_grad, "tensor", 2, n_tensor // 2, True, 0
    )

    gate_part = jnp.dot(whole_acts, gate_weight, preferred_element_type=jnp.float32)
    up_part = jnp.dot(whole_acts, up_weight, preferred_element_type=jnp.float32)
    grad_part = lax.dot_general(
        whole_grad, down_weight, contract_last, preferred_element_type=jnp.float32
    )
    partials = jnp.concatenate([gate_part, up_part, grad_part], axis=1)
    summed = ring_sum(
        partials.reshape((n_pipe, partials.shape[0] // n_pipe, partials.shape[1])),
        "pipe",
        n_pipe // 2,
        1,
    )
    gate_pre = summed[:, :hidden_width]
    up_pre = summed[:, hidden_width : 2 * hidden_width]
    hidden_grad = summed[:, 2 * hidden_width :]
    hidden_part = (jax.nn.silu(gate_pre) * up_pre).astype(jnp.bfloat16)
    local_slopes = make_slopes(hidden_grad, stored_gate, stored_up)

    rows = gather_rows(jnp.concatenate([hidden_part, local_slopes], axis=1), "pipe", n_pipe)
    hidden = rows[:, :hidden_width]
    gate_slopes = rows[:, hidden_width : 2 * hidden_width]
    up_slopes = rows[:, 2 * hidden_width :]

    out_part = jnp.dot(hidden, down_weight, preferred_element_type=jnp.float32)
    in_part = lax.dot_general(
        gate_slopes, gate_weight, contract_last, preferred_element_type=jnp.float32
    ) + lax.dot_general(up_slopes, up_weight, contract_last, preferred_element_type=jnp.float32)
    finished = scatter_sum_rows(
        jnp.concatenate([out_part, in_part], axis=1), "tensor", n_tensor, TENSOR_LINK
    ).astype(jnp.bfloat16)
    return (finished[:, :model_width], finished[:, model_width:])


def solution(mesh):
    in_specs = (
        P(("dp", "tensor"), "pipe"),
        P(("dp", "tensor"), "pipe"),
        P(("dp", "pipe"), "tensor"),
        P(("dp", "pipe"), "tensor"),
        P("pipe", "tensor"),
        P("pipe", "tensor"),
        P("tensor", "pipe"),
    )
    out_specs = (P(("dp", "tensor"), "pipe"), P(("dp", "tensor"), "pipe"))
    return jax.shard_map(
        per_device, mesh=mesh, in_specs=in_specs, out_specs=out_specs, check_vma=False
    )
```

```python
import functools

import jax
import jax.numpy as jnp
from jax import lax
from jax.experimental import pallas as pl
from jax.experimental.pallas import tpu as pltpu
from jax.sharding import PartitionSpec as P

PIPE_LINK = jnp.float32
TENSOR_LINK = jnp.bfloat16
MESH = pl.DeviceIdType.MESH


def make_slopes(hidden_grad, gate_vals, up_vals):
    gate_wide = gate_vals.astype(jnp.float32)
    up_wide = up_vals.astype(jnp.float32)
    sigma = jax.nn.sigmoid(gate_wide)
    gate_slope = (hidden_grad * up_wide * sigma * (1.0 + gate_wide * (1.0 - sigma))).astype(
        jnp.bfloat16
    )
    up_slope = (hidden_grad * gate_wide * sigma).astype(jnp.bfloat16)
    return jnp.concatenate([gate_slope, up_slope], axis=1)


def gather_rows(block, axis, count):
    sent = jnp.broadcast_to(block[None], (count,) + block.shape)
    got = lax.all_to_all(sent, axis, 0, 0, tiled=False)
    return got.reshape((count * block.shape[0],) + block.shape[1:])


def scatter_sum_rows(partial, axis, count, link_dtype):
    rows = partial.shape[0] // count
    sent = partial.reshape((count, rows) + partial.shape[1:]).astype(link_dtype)
    got = lax.all_to_all(sent, axis, 0, 0, tiled=False)
    return got.astype(jnp.float32).sum(axis=0)


def _ring_gather_kernel(axis, outer, inner, ring_on_inner, halves, first_in, second_in, first_ref, second_ref, send_sems, recv_sems, swap_sems, local_sems):
    me = lax.axis_index(axis)
    o = me // inner
    i = me % inner
    if ring_on_inner:
        ring = inner
        pos, other = i, o
        def at(p, q):
            return q * inner + p
    else:
        ring = outer
        pos, other = o, i
        def at(p, q):
            return p * inner + q
    partner = at(pos, 1 - other)
    up = at(lax.rem(pos + 1, ring), other)
    down = at(lax.rem(pos + ring - 1, ring), other)
    ins = (first_in, second_in)
    rows = first_in.shape[0]
    part = rows // halves
    steps = (ring // 2, (ring - 1) // 2)

    barrier = pltpu.get_barrier_semaphore()
    for peer in (partner, up, down):
        pl.semaphore_signal(barrier, inc=1, device_id={axis: peer}, device_id_type=MESH)
    pl.semaphore_wait(barrier, 3)

    outs = (first_ref, second_ref)
    locals_ = []
    swaps = []
    for a in range(2):
        c = pltpu.make_async_copy(ins[a], outs[a].at[other, pos], local_sems.at[a])
        c.start()
        locals_.append(c)
        s = pltpu.make_async_remote_copy(
            src_ref=ins[a], dst_ref=outs[a].at[other, pos],
            send_sem=swap_sems.at[0, a], recv_sem=swap_sems.at[1, a],
            device_id={axis: partner}, device_id_type=MESH)
        s.start()
        swaps.append(s)

    targets = (up, down)
    copies = {}

    def chunk_copy(d, step, which, r, a):
        slot = lax.rem(pos - step + 1 + ring, ring) if d == 0 else lax.rem(pos + step - 1, ring)
        half = other if which == 0 else 1 - other
        rs = pl.ds(r * part, part)
        if step == 1 and which == 0:
            src = ins[a].at[rs]
        else:
            src = outs[a].at[half, slot, rs]
        k = (((d * ring + step - 1) * 2 + which) * halves + r) * 2 + a
        return pltpu.make_async_remote_copy(
            src_ref=src, dst_ref=outs[a].at[half, slot, rs],
            send_sem=send_sems.at[k], recv_sem=recv_sems.at[k],
            device_id={axis: targets[d]}, device_id_type=MESH)

    for step in range(1, steps[0] + 1):
        for which in range(2):
            if step == 1 and which == 1:
                for s in swaps:
                    s.wait_recv()
            for r in range(halves):
                for a in range(2):
                    for d in range(2):
                        if step > steps[d]:
                            continue
                        if step > 1:
                            copies[(d, step - 1, which, r, a)].wait_recv()
                        c = chunk_copy(d, step, which, r, a)
                        c.start()
                        copies[(d, step, which, r, a)] = c
    for d in range(2):
        if steps[d] == 0:
            continue
        for which in range(2):
            for r in range(halves):
                for a in range(2):
                    copies[(d, steps[d], which, r, a)].wait_recv()
    for c in locals_:
        c.wait()
    for s in swaps:
        s.wait_send()
    for c in copies.values():
        c.wait_send()


def ring_gather(first, second, axis, outer, inner, ring_on_inner, cid, halves=2):
    rows, width = first.shape
    ring = inner if ring_on_inner else outer
    shape = (2, ring, rows, width)
    n_copies = 2 * ring * 2 * halves * 2
    f, s = pl.pallas_call(
        functools.partial(_ring_gather_kernel, axis, outer, inner, ring_on_inner, halves),
        out_shape=(jax.ShapeDtypeStruct(shape, first.dtype), jax.ShapeDtypeStruct(shape, second.dtype)),
        in_specs=[pl.BlockSpec(memory_space=pltpu.VMEM)] * 2,
        out_specs=(pl.BlockSpec(memory_space=pltpu.VMEM), pl.BlockSpec(memory_space=pltpu.VMEM)),
        scratch_shapes=[
            pltpu.SemaphoreType.DMA((n_copies,)),
            pltpu.SemaphoreType.DMA((n_copies,)),
            pltpu.SemaphoreType.DMA((2, 2)),
            pltpu.SemaphoreType.DMA((2,)),
        ],
        compiler_params=pltpu.CompilerParams(collective_id=cid, has_side_effects=True),
    )(first, second)
    if ring_on_inner:
        return f.reshape(2 * ring * rows, width), s.reshape(2 * ring * rows, width)
    return (f.transpose(1, 0, 2, 3).reshape(2 * ring * rows, width),
            s.transpose(1, 0, 2, 3).reshape(2 * ring * rows, width))


def _ring_sum_kernel(axis, outer, chunks, x_ref, out_ref, send_buf, recv_buf, swap_buf, send_sems, recv_sems, swap_sems):
    me = lax.axis_index(axis)
    y = me // 2
    x = me % 2
    ring = outer
    up = lax.rem(y + 1, ring) * 2 + x
    down = lax.rem(y + ring - 1, ring) * 2 + x
    partner = y * 2 + 1 - x
    rows = x_ref.shape[1]
    half = rows // 2
    part = half // chunks

    barrier = pltpu.get_barrier_semaphore()
    for peer in (partner, up, down):
        pl.semaphore_signal(barrier, inc=1, device_id={axis: peer}, device_id_type=MESH)
    pl.semaphore_wait(barrier, 3)

    targets = (up, down)
    copies = {}

    def dest(d, step):
        return lax.rem(y - step + ring, ring) if d == 0 else lax.rem(y + step, ring)

    for step in range(1, ring):
        for c in range(chunks):
            for d in range(2):
                rs = pl.ds(d * half + c * part, part)
                blocks = pl.ds(dest(d, step) * 2, 2)
                if step == 1:
                    src = x_ref.at[blocks, rs]
                else:
                    copies[(d, step - 1, c)].wait_recv()
                    send_buf[d, step, :, pl.ds(c * part, part)] = (
                        recv_buf[d, step - 1, :, pl.ds(c * part, part)] + x_ref[blocks, rs]
                    )
                    src = send_buf.at[d, step, :, pl.ds(c * part, part)]
                cp = pltpu.make_async_remote_copy(
                    src_ref=src, dst_ref=recv_buf.at[d, step, :, pl.ds(c * part, part)],
                    send_sem=send_sems.at[d, step, c], recv_sem=recv_sems.at[d, step, c],
                    device_id={axis: targets[d]}, device_id_type=MESH)
                cp.start()
                copies[(d, step, c)] = cp
    swaps = []
    for c in range(chunks):
        for d in range(2):
            rs = pl.ds(d * half + c * part, part)
            local = pl.ds(c * part, part)
            copies[(d, ring - 1, c)].wait_recv()
            swap_buf[0, d, local] = recv_buf[d, ring - 1, 1 - x, local] + x_ref[y * 2 + 1 - x, rs]
            out_ref[rs] = recv_buf[d, ring - 1, x, local] + x_ref[y * 2 + x, rs]
            sw = pltpu.make_async_remote_copy(
                src_ref=swap_buf.at[0, d, local], dst_ref=swap_buf.at[1, d, local],
                send_sem=swap_sems.at[0, d, c], recv_sem=swap_sems.at[1, d, c],
                device_id={axis: partner}, device_id_type=MESH)
            sw.start()
            swaps.append((d, c, sw))
    for d, c, sw in swaps:
        rs = pl.ds(d * half + c * part, part)
        sw.wait_recv()
        out_ref[rs] = out_ref[rs] + swap_buf[1, d, pl.ds(c * part, part)]
    for d, c, sw in swaps:
        sw.wait_send()
    for cp in copies.values():
        cp.wait_send()


def ring_sum(partial, axis, outer, cid, chunks=4):
    count, rows, width = partial.shape
    half = rows // 2
    return pl.pallas_call(
        functools.partial(_ring_sum_kernel, axis, outer, chunks),
        out_shape=jax.ShapeDtypeStruct((rows, width), jnp.float32),
        in_specs=[pl.BlockSpec(memory_space=pltpu.VMEM)],
        out_specs=pl.BlockSpec(memory_space=pltpu.VMEM),
        scratch_shapes=[
            pltpu.VMEM((2, outer, 2, half, width), jnp.float32),
            pltpu.VMEM((2, outer, 2, half, width), jnp.float32),
            pltpu.VMEM((2, 2, half, width), jnp.float32),
            pltpu.SemaphoreType.DMA((2, outer, chunks)),
            pltpu.SemaphoreType.DMA((2, outer, chunks)),
            pltpu.SemaphoreType.DMA((2, 2, chunks)),
        ],
        compiler_params=pltpu.CompilerParams(collective_id=cid, has_side_effects=True, vmem_limit_bytes=60 * 1024 * 1024),
    )(partial)


def _exchange_kernel(plan, *refs):
    k = len(plan)
    ins, outs = refs[:k], refs[k:2 * k]
    send_sems, recv_sems, local_sems = refs[2 * k:]
    axes = {}
    for axis, count, _ in plan:
        axes[axis] = count
    barrier = pltpu.get_barrier_semaphore()
    total = 0
    for axis, count in axes.items():
        me = lax.axis_index(axis)
        for d in range(1, count):
            pl.semaphore_signal(barrier, inc=1, device_id={axis: lax.rem(me + d, count)}, device_id_type=MESH)
        total += count - 1
    pl.semaphore_wait(barrier, total)
    started = []
    for e, (axis, count, spread) in enumerate(plan):
        me = lax.axis_index(axis)
        src = ins[e] if spread else ins[e].at[me]
        own = pltpu.make_async_copy(src, outs[e].at[me], local_sems.at[e])
        own.start()
        started.append(own)
    remote = []
    for d in range(1, max(c for _, c, _ in plan)):
        for e, (axis, count, spread) in enumerate(plan):
            if d >= count:
                continue
            me = lax.axis_index(axis)
            peer = lax.rem(me + d, count)
            src = ins[e] if spread else ins[e].at[peer]
            c = pltpu.make_async_remote_copy(
                src_ref=src, dst_ref=outs[e].at[me],
                send_sem=send_sems.at[e, d - 1], recv_sem=recv_sems.at[e, d - 1],
                device_id={axis: peer}, device_id_type=MESH)
            c.start()
            remote.append(c)
    for c in started:
        c.wait()
    for c in remote:
        c.wait_recv()
    for c in remote:
        c.wait_send()


def exchange(items, cid):
    plan = tuple((axis, count, spread) for _, axis, count, spread in items)
    shapes = []
    for x, axis, count, spread in items:
        shape = (count,) + x.shape if spread else x.shape
        shapes.append(jax.ShapeDtypeStruct(shape, x.dtype))
    widest = max(count for _, _, count, _ in items)
    return pl.pallas_call(
        functools.partial(_exchange_kernel, plan),
        out_shape=tuple(shapes),
        in_specs=[pl.BlockSpec(memory_space=pl.ANY)] * len(items),
        out_specs=tuple(pl.BlockSpec(memory_space=pl.ANY) for _ in items),
        scratch_shapes=[
            pltpu.SemaphoreType.DMA((len(items), widest - 1)),
            pltpu.SemaphoreType.DMA((len(items), widest - 1)),
            pltpu.SemaphoreType.DMA((len(items),)),
        ],
        compiler_params=pltpu.CompilerParams(collective_id=cid, has_side_effects=True),
    )(*[x for x, _, _, _ in items])


def per_device(
    forward_acts, backward_grad, stored_gate, stored_up, gate_weight, up_weight, down_weight
):
    n_pipe = lax.axis_size("pipe")
    n_tensor = lax.axis_size("tensor")
    hidden_width = gate_weight.shape[1]
    model_width = forward_acts.shape[1]
    contract_last = (((1,), (1,)), ((), ()))

    whole_acts, whole_grad = ring_gather(
        forward_acts, backward_grad, "tensor", 2, n_tensor // 2, True, 0
    )

    gate_part = jnp.dot(whole_acts, gate_weight, preferred_element_type=jnp.float32)
    up_part = jnp.dot(whole_acts, up_weight, preferred_element_type=jnp.float32)
    grad_part = lax.dot_general(
        whole_grad, down_weight, contract_last, preferred_element_type=jnp.float32
    )
    partials = jnp.concatenate([gate_part, up_part, grad_part], axis=1)
    summed = ring_sum(
        partials.reshape((n_pipe, partials.shape[0] // n_pipe, partials.shape[1])),
        "pipe",
        n_pipe // 2,
        1,
    )
    gate_pre = summed[:, :hidden_width]
    up_pre = summed[:, hidden_width : 2 * hidden_width]
    hidden_grad = summed[:, 2 * hidden_width :]
    hidden_part = (jax.nn.silu(gate_pre) * up_pre).astype(jnp.bfloat16)
    local_slopes = make_slopes(hidden_grad, stored_gate, stored_up)

    local_rows = jnp.concatenate([hidden_part, local_slopes], axis=1)
    (rows,) = exchange([(local_rows, "pipe", n_pipe, True)], 2)
    rows = rows.reshape(n_pipe * local_rows.shape[0], local_rows.shape[1])
    hidden = rows[:, :hidden_width]
    gate_slopes = rows[:, hidden_width : 2 * hidden_width]
    up_slopes = rows[:, 2 * hidden_width :]

    out_part = jnp.dot(hidden, down_weight, preferred_element_type=jnp.float32)
    in_part = lax.dot_general(
        gate_slopes, gate_weight, contract_last, preferred_element_type=jnp.float32
    ) + lax.dot_general(up_slopes, up_weight, contract_last, preferred_element_type=jnp.float32)
    finishing = jnp.concatenate([out_part, in_part], axis=1)
    (got,) = exchange(
        [
            (
                finishing.reshape((n_tensor, finishing.shape[0] // n_tensor, finishing.shape[1])).astype(
                    TENSOR_LINK
                ),
                "tensor",
                n_tensor,
                False,
            )
        ],
        3,
    )
    finished = got.astype(jnp.float32).sum(axis=0).astype(jnp.bfloat16)
    return (finished[:, :model_width], finished[:, model_width:])


def solution(mesh):
    in_specs = (
        P(("dp", "tensor"), "pipe"),
        P(("dp", "tensor"), "pipe"),
        P(("dp", "pipe"), "tensor"),
        P(("dp", "pipe"), "tensor"),
        P("pipe", "tensor"),
        P("pipe", "tensor"),
        P("tensor", "pipe"),
    )
    out_specs = (P(("dp", "tensor"), "pipe"), P(("dp", "tensor"), "pipe"))
    return jax.shard_map(
        per_device, mesh=mesh, in_specs=in_specs, out_specs=out_specs, check_vma=False
    )
```

```python
import functools

import jax
import jax.numpy as jnp
from jax import lax
from jax.experimental import pallas as pl
from jax.experimental.pallas import tpu as pltpu
from jax.sharding import PartitionSpec as P

TENSOR_LINK = jnp.bfloat16
MESH = pl.DeviceIdType.MESH


def make_slopes(hidden_grad, gate_vals, up_vals):
    gate_wide = gate_vals.astype(jnp.float32)
    up_wide = up_vals.astype(jnp.float32)
    sigma = jax.nn.sigmoid(gate_wide)
    gate_slope = (hidden_grad * up_wide * sigma * (1.0 + gate_wide * (1.0 - sigma))).astype(
        jnp.bfloat16
    )
    up_slope = (hidden_grad * gate_wide * sigma).astype(jnp.bfloat16)
    return jnp.concatenate([gate_slope, up_slope], axis=1)


def _ring_gather_kernel(axis, outer, inner, ring_on_inner, halves, first_in, second_in, first_ref, second_ref, send_sems, recv_sems, swap_sems, local_sems):
    me = lax.axis_index(axis)
    o = me // inner
    i = me % inner
    if ring_on_inner:
        ring = inner
        pos, other = i, o
        def at(p, q):
            return q * inner + p
    else:
        ring = outer
        pos, other = o, i
        def at(p, q):
            return p * inner + q
    partner = at(pos, 1 - other)
    up = at(lax.rem(pos + 1, ring), other)
    down = at(lax.rem(pos + ring - 1, ring), other)
    ins = (first_in, second_in)
    rows = first_in.shape[0]
    part = rows // halves
    steps = (ring // 2, (ring - 1) // 2)

    barrier = pltpu.get_barrier_semaphore()
    for peer in (partner, up, down):
        pl.semaphore_signal(barrier, inc=1, device_id={axis: peer}, device_id_type=MESH)
    pl.semaphore_wait(barrier, 3)

    outs = (first_ref, second_ref)
    locals_ = []
    swaps = []
    for a in range(2):
        c = pltpu.make_async_copy(ins[a], outs[a].at[other, pos], local_sems.at[a])
        c.start()
        locals_.append(c)
        s = pltpu.make_async_remote_copy(
            src_ref=ins[a], dst_ref=outs[a].at[other, pos],
            send_sem=swap_sems.at[0, a], recv_sem=swap_sems.at[1, a],
            device_id={axis: partner}, device_id_type=MESH)
        s.start()
        swaps.append(s)

    targets = (up, down)
    copies = {}

    def chunk_copy(d, step, which, r, a):
        slot = lax.rem(pos - step + 1 + ring, ring) if d == 0 else lax.rem(pos + step - 1, ring)
        half = other if which == 0 else 1 - other
        rs = pl.ds(r * part, part)
        if step == 1 and which == 0:
            src = ins[a].at[rs]
        else:
            src = outs[a].at[half, slot, rs]
        k = (((d * ring + step - 1) * 2 + which) * halves + r) * 2 + a
        return pltpu.make_async_remote_copy(
            src_ref=src, dst_ref=outs[a].at[half, slot, rs],
            send_sem=send_sems.at[k], recv_sem=recv_sems.at[k],
            device_id={axis: targets[d]}, device_id_type=MESH)

    for step in range(1, steps[0] + 1):
        for which in range(2):
            if step == 1 and which == 1:
                for s in swaps:
                    s.wait_recv()
            for r in range(halves):
                for a in range(2):
                    for d in range(2):
                        if step > steps[d]:
                            continue
                        if step > 1:
                            copies[(d, step - 1, which, r, a)].wait_recv()
                        c = chunk_copy(d, step, which, r, a)
                        c.start()
                        copies[(d, step, which, r, a)] = c
    for d in range(2):
        if steps[d] == 0:
            continue
        for which in range(2):
            for r in range(halves):
                for a in range(2):
                    copies[(d, steps[d], which, r, a)].wait_recv()
    for c in locals_:
        c.wait()
    for s in swaps:
        s.wait_send()
    for c in copies.values():
        c.wait_send()


def ring_gather(first, second, axis, outer, inner, ring_on_inner, cid, halves=2):
    rows, width = first.shape
    ring = inner if ring_on_inner else outer
    shape = (2, ring, rows, width)
    n_copies = 2 * ring * 2 * halves * 2
    f, s = pl.pallas_call(
        functools.partial(_ring_gather_kernel, axis, outer, inner, ring_on_inner, halves),
        out_shape=(jax.ShapeDtypeStruct(shape, first.dtype), jax.ShapeDtypeStruct(shape, second.dtype)),
        in_specs=[pl.BlockSpec(memory_space=pltpu.VMEM)] * 2,
        out_specs=(pl.BlockSpec(memory_space=pltpu.VMEM), pl.BlockSpec(memory_space=pltpu.VMEM)),
        scratch_shapes=[
            pltpu.SemaphoreType.DMA((n_copies,)),
            pltpu.SemaphoreType.DMA((n_copies,)),
            pltpu.SemaphoreType.DMA((2, 2)),
            pltpu.SemaphoreType.DMA((2,)),
        ],
        compiler_params=pltpu.CompilerParams(collective_id=cid, has_side_effects=True),
    )(first, second)
    if ring_on_inner:
        return f.reshape(2 * ring * rows, width), s.reshape(2 * ring * rows, width)
    return (f.transpose(1, 0, 2, 3).reshape(2 * ring * rows, width),
            s.transpose(1, 0, 2, 3).reshape(2 * ring * rows, width))


def _ring_sum_kernel(axis, outer, chunks, count, *refs):
    xs = refs[:count]
    outs = refs[count:2 * count]
    send_bufs = refs[2 * count:3 * count]
    recv_bufs = refs[3 * count:4 * count]
    swap_bufs = refs[4 * count:5 * count]
    send_sems, recv_sems, swap_sems = refs[5 * count:]
    me = lax.axis_index(axis)
    y = me // 2
    x = me % 2
    ring = outer
    up = lax.rem(y + 1, ring) * 2 + x
    down = lax.rem(y + ring - 1, ring) * 2 + x
    partner = y * 2 + 1 - x
    rows = xs[0].shape[1]
    half = rows // 2
    part = half // chunks

    barrier = pltpu.get_barrier_semaphore()
    for peer in (partner, up, down):
        pl.semaphore_signal(barrier, inc=1, device_id={axis: peer}, device_id_type=MESH)
    pl.semaphore_wait(barrier, 3)

    targets = (up, down)
    copies = {}

    def dest(d, step):
        return lax.rem(y - step + ring, ring) if d == 0 else lax.rem(y + step, ring)

    for step in range(1, ring):
        for c in range(chunks):
            for d in range(2):
                for t in range(count):
                    rs = pl.ds(d * half + c * part, part)
                    local = pl.ds(c * part, part)
                    blocks = pl.ds(dest(d, step) * 2, 2)
                    if step == 1:
                        src = xs[t].at[blocks, rs]
                    else:
                        copies[(d, step - 1, c, t)].wait_recv()
                        send_bufs[t][d, step, :, local] = (
                            recv_bufs[t][d, step - 1, :, local] + xs[t][blocks, rs]
                        )
                        src = send_bufs[t].at[d, step, :, local]
                    cp = pltpu.make_async_remote_copy(
                        src_ref=src, dst_ref=recv_bufs[t].at[d, step, :, local],
                        send_sem=send_sems.at[t, d, step, c], recv_sem=recv_sems.at[t, d, step, c],
                        device_id={axis: targets[d]}, device_id_type=MESH)
                    cp.start()
                    copies[(d, step, c, t)] = cp
    swaps = []
    for c in range(chunks):
        for d in range(2):
            for t in range(count):
                rs = pl.ds(d * half + c * part, part)
                local = pl.ds(c * part, part)
                copies[(d, ring - 1, c, t)].wait_recv()
                swap_bufs[t][0, d, local] = recv_bufs[t][d, ring - 1, 1 - x, local] + xs[t][y * 2 + 1 - x, rs]
                outs[t][rs] = recv_bufs[t][d, ring - 1, x, local] + xs[t][y * 2 + x, rs]
                sw = pltpu.make_async_remote_copy(
                    src_ref=swap_bufs[t].at[0, d, local], dst_ref=swap_bufs[t].at[1, d, local],
                    send_sem=swap_sems.at[t, 0, d, c], recv_sem=swap_sems.at[t, 1, d, c],
                    device_id={axis: partner}, device_id_type=MESH)
                sw.start()
                swaps.append((d, c, t, sw))
    for d, c, t, sw in swaps:
        rs = pl.ds(d * half + c * part, part)
        sw.wait_recv()
        outs[t][rs] = outs[t][rs] + swap_bufs[t][1, d, pl.ds(c * part, part)]
    for d, c, t, sw in swaps:
        sw.wait_send()
    for cp in copies.values():
        cp.wait_send()


def ring_sum(partials, axis, outer, cid, chunks=4):
    count = len(partials)
    rows = partials[0].shape[1]
    half = rows // 2
    scratch = []
    for kind in range(3):
        for p in partials:
            width = p.shape[2]
            if kind < 2:
                scratch.append(pltpu.VMEM((2, outer, 2, half, width), jnp.float32))
            else:
                scratch.append(pltpu.VMEM((2, 2, half, width), jnp.float32))
    scratch += [
        pltpu.SemaphoreType.DMA((count, 2, outer, chunks)),
        pltpu.SemaphoreType.DMA((count, 2, outer, chunks)),
        pltpu.SemaphoreType.DMA((count, 2, 2, chunks)),
    ]
    return pl.pallas_call(
        functools.partial(_ring_sum_kernel, axis, outer, chunks, count),
        out_shape=tuple(jax.ShapeDtypeStruct((rows, p.shape[2]), jnp.float32) for p in partials),
        in_specs=[pl.BlockSpec(memory_space=pltpu.VMEM)] * count,
        out_specs=tuple(pl.BlockSpec(memory_space=pltpu.VMEM) for _ in partials),
        scratch_shapes=scratch,
        compiler_params=pltpu.CompilerParams(collective_id=cid, has_side_effects=True, vmem_limit_bytes=60 * 1024 * 1024),
    )(*partials)


def _exchange_kernel(plan, *refs):
    k = len(plan)
    ins, outs = refs[:k], refs[k:2 * k]
    send_sems, recv_sems, local_sems = refs[2 * k:]
    axes = {}
    for axis, count, _ in plan:
        axes[axis] = count
    barrier = pltpu.get_barrier_semaphore()
    total = 0
    for axis, count in axes.items():
        me = lax.axis_index(axis)
        for d in range(1, count):
            pl.semaphore_signal(barrier, inc=1, device_id={axis: lax.rem(me + d, count)}, device_id_type=MESH)
        total += count - 1
    pl.semaphore_wait(barrier, total)
    started = []
    for e, (axis, count, spread) in enumerate(plan):
        me = lax.axis_index(axis)
        src = ins[e] if spread else ins[e].at[me]
        own = pltpu.make_async_copy(src, outs[e].at[me], local_sems.at[e])
        own.start()
        started.append(own)
    remote = []
    for d in range(1, max(c for _, c, _ in plan)):
        for e, (axis, count, spread) in enumerate(plan):
            if d >= count:
                continue
            me = lax.axis_index(axis)
            peer = lax.rem(me + d, count)
            src = ins[e] if spread else ins[e].at[peer]
            c = pltpu.make_async_remote_copy(
                src_ref=src, dst_ref=outs[e].at[me],
                send_sem=send_sems.at[e, d - 1], recv_sem=recv_sems.at[e, d - 1],
                device_id={axis: peer}, device_id_type=MESH)
            c.start()
            remote.append(c)
    for c in started:
        c.wait()
    for c in remote:
        c.wait_recv()
    for c in remote:
        c.wait_send()


def exchange(items, cid):
    plan = tuple((axis, count, spread) for _, axis, count, spread in items)
    shapes = []
    for x, axis, count, spread in items:
        shape = (count,) + x.shape if spread else x.shape
        shapes.append(jax.ShapeDtypeStruct(shape, x.dtype))
    widest = max(count for _, _, count, _ in items)
    return pl.pallas_call(
        functools.partial(_exchange_kernel, plan),
        out_shape=tuple(shapes),
        in_specs=[pl.BlockSpec(memory_space=pl.ANY)] * len(items),
        out_specs=tuple(pl.BlockSpec(memory_space=pl.ANY) for _ in items),
        scratch_shapes=[
            pltpu.SemaphoreType.DMA((len(items), widest - 1)),
            pltpu.SemaphoreType.DMA((len(items), widest - 1)),
            pltpu.SemaphoreType.DMA((len(items),)),
        ],
        compiler_params=pltpu.CompilerParams(collective_id=cid, has_side_effects=True),
    )(*[x for x, _, _, _ in items])


def per_device(
    forward_acts, backward_grad, stored_gate, stored_up, gate_weight, up_weight, down_weight
):
    n_pipe = lax.axis_size("pipe")
    n_tensor = lax.axis_size("tensor")
    hidden_width = gate_weight.shape[1]
    model_width = forward_acts.shape[1]
    contract_last = (((1,), (1,)), ((), ()))

    whole_acts, whole_grad = ring_gather(
        forward_acts, backward_grad, "tensor", 2, n_tensor // 2, True, 0
    )

    gate_part = jnp.dot(whole_acts, gate_weight, preferred_element_type=jnp.float32)
    up_part = jnp.dot(whole_acts, up_weight, preferred_element_type=jnp.float32)
    grad_part = lax.dot_general(
        whole_grad, down_weight, contract_last, preferred_element_type=jnp.float32
    )
    gate_pre, up_pre, hidden_grad = ring_sum(
        [p.reshape((n_pipe, p.shape[0] // n_pipe, p.shape[1])) for p in (gate_part, up_part, grad_part)],
        "pipe",
        n_pipe // 2,
        1,
    )
    hidden_part = (jax.nn.silu(gate_pre) * up_pre).astype(jnp.bfloat16)
    local_slopes = make_slopes(hidden_grad, stored_gate, stored_up)

    local_rows = jnp.concatenate([hidden_part, local_slopes], axis=1)
    (rows,) = exchange([(local_rows, "pipe", n_pipe, True)], 2)
    rows = rows.reshape(n_pipe * local_rows.shape[0], local_rows.shape[1])
    hidden = rows[:, :hidden_width]
    gate_slopes = rows[:, hidden_width : 2 * hidden_width]
    up_slopes = rows[:, 2 * hidden_width :]

    out_part = jnp.dot(hidden, down_weight, preferred_element_type=jnp.float32)
    in_part = lax.dot_general(
        gate_slopes, gate_weight, contract_last, preferred_element_type=jnp.float32
    ) + lax.dot_general(up_slopes, up_weight, contract_last, preferred_element_type=jnp.float32)
    finishing = jnp.concatenate([out_part, in_part], axis=1)
    (got,) = exchange(
        [
            (
                finishing.reshape((n_tensor, finishing.shape[0] // n_tensor, finishing.shape[1])).astype(
                    TENSOR_LINK
                ),
                "tensor",
                n_tensor,
                False,
            )
        ],
        3,
    )
    finished = got.astype(jnp.float32).sum(axis=0).astype(jnp.bfloat16)
    return (finished[:, :model_width], finished[:, model_width:])


def solution(mesh):
    in_specs = (
        P(("dp", "tensor"), "pipe"),
        P(("dp", "tensor"), "pipe"),
        P(("dp", "pipe"), "tensor"),
        P(("dp", "pipe"), "tensor"),
        P("pipe", "tensor"),
        P("pipe", "tensor"),
        P("tensor", "pipe"),
    )
    out_specs = (P(("dp", "tensor"), "pipe"), P(("dp", "tensor"), "pipe"))
    return jax.shard_map(
        per_device, mesh=mesh, in_specs=in_specs, out_specs=out_specs, check_vma=False
    )
```

```python
import functools

import jax
import jax.numpy as jnp
from jax import lax
from jax.experimental import pallas as pl
from jax.experimental.pallas import tpu as pltpu
from jax.sharding import PartitionSpec as P

TENSOR_LINK = jnp.bfloat16
MESH = pl.DeviceIdType.MESH


def make_slopes(hidden_grad, gate_vals, up_vals):
    gate_wide = gate_vals.astype(jnp.float32)
    up_wide = up_vals.astype(jnp.float32)
    sigma = jax.nn.sigmoid(gate_wide)
    gate_slope = (hidden_grad * up_wide * sigma * (1.0 + gate_wide * (1.0 - sigma))).astype(
        jnp.bfloat16
    )
    up_slope = (hidden_grad * gate_wide * sigma).astype(jnp.bfloat16)
    return jnp.concatenate([gate_slope, up_slope], axis=1)


def _ring_gather_kernel(axis, outer, inner, ring_on_inner, halves, first_in, second_in, first_ref, second_ref, send_sems, recv_sems, swap_sems, local_sems):
    me = lax.axis_index(axis)
    o = me // inner
    i = me % inner
    if ring_on_inner:
        ring = inner
        pos, other = i, o
        def at(p, q):
            return q * inner + p
    else:
        ring = outer
        pos, other = o, i
        def at(p, q):
            return p * inner + q
    partner = at(pos, 1 - other)
    up = at(lax.rem(pos + 1, ring), other)
    down = at(lax.rem(pos + ring - 1, ring), other)
    ins = (first_in, second_in)
    rows = first_in.shape[0]
    part = rows // halves
    steps = (ring // 2, (ring - 1) // 2)

    barrier = pltpu.get_barrier_semaphore()
    for peer in (partner, up, down):
        pl.semaphore_signal(barrier, inc=1, device_id={axis: peer}, device_id_type=MESH)
    pl.semaphore_wait(barrier, 3)

    outs = (first_ref, second_ref)
    locals_ = []
    swaps = []
    for a in range(2):
        c = pltpu.make_async_copy(ins[a], outs[a].at[other, pos], local_sems.at[a])
        c.start()
        locals_.append(c)
        s = pltpu.make_async_remote_copy(
            src_ref=ins[a], dst_ref=outs[a].at[other, pos],
            send_sem=swap_sems.at[0, a], recv_sem=swap_sems.at[1, a],
            device_id={axis: partner}, device_id_type=MESH)
        s.start()
        swaps.append(s)

    targets = (up, down)
    copies = {}

    def chunk_copy(d, step, which, r, a):
        slot = lax.rem(pos - step + 1 + ring, ring) if d == 0 else lax.rem(pos + step - 1, ring)
        half = other if which == 0 else 1 - other
        rs = pl.ds(r * part, part)
        if step == 1 and which == 0:
            src = ins[a].at[rs]
        else:
            src = outs[a].at[half, slot, rs]
        k = (((d * ring + step - 1) * 2 + which) * halves + r) * 2 + a
        return pltpu.make_async_remote_copy(
            src_ref=src, dst_ref=outs[a].at[half, slot, rs],
            send_sem=send_sems.at[k], recv_sem=recv_sems.at[k],
            device_id={axis: targets[d]}, device_id_type=MESH)

    for step in range(1, steps[0] + 1):
        for which in range(2):
            if step == 1 and which == 1:
                for s in swaps:
                    s.wait_recv()
            for r in range(halves):
                for a in range(2):
                    for d in range(2):
                        if step > steps[d]:
                            continue
                        if step > 1:
                            copies[(d, step - 1, which, r, a)].wait_recv()
                        c = chunk_copy(d, step, which, r, a)
                        c.start()
                        copies[(d, step, which, r, a)] = c
    for d in range(2):
        if steps[d] == 0:
            continue
        for which in range(2):
            for r in range(halves):
                for a in range(2):
                    copies[(d, steps[d], which, r, a)].wait_recv()
    for c in locals_:
        c.wait()
    for s in swaps:
        s.wait_send()
    for c in copies.values():
        c.wait_send()


def ring_gather(first, second, axis, outer, inner, ring_on_inner, cid, halves=2):
    rows, width = first.shape
    ring = inner if ring_on_inner else outer
    shape = (2, ring, rows, width)
    n_copies = 2 * ring * 2 * halves * 2
    f, s = pl.pallas_call(
        functools.partial(_ring_gather_kernel, axis, outer, inner, ring_on_inner, halves),
        out_shape=(jax.ShapeDtypeStruct(shape, first.dtype), jax.ShapeDtypeStruct(shape, second.dtype)),
        in_specs=[pl.BlockSpec(memory_space=pltpu.VMEM)] * 2,
        out_specs=(pl.BlockSpec(memory_space=pltpu.VMEM), pl.BlockSpec(memory_space=pltpu.VMEM)),
        scratch_shapes=[
            pltpu.SemaphoreType.DMA((n_copies,)),
            pltpu.SemaphoreType.DMA((n_copies,)),
            pltpu.SemaphoreType.DMA((2, 2)),
            pltpu.SemaphoreType.DMA((2,)),
        ],
        compiler_params=pltpu.CompilerParams(collective_id=cid, has_side_effects=True),
    )(first, second)
    if ring_on_inner:
        return f.reshape(2 * ring * rows, width), s.reshape(2 * ring * rows, width)
    return (f.transpose(1, 0, 2, 3).reshape(2 * ring * rows, width),
            s.transpose(1, 0, 2, 3).reshape(2 * ring * rows, width))


def _ring_sum_kernel(axis, outer, chunks, x_ref, out_ref, send_buf, recv_buf, swap_buf, send_sems, recv_sems, swap_sems):
    me = lax.axis_index(axis)
    y = me // 2
    x = me % 2
    ring = outer
    up = lax.rem(y + 1, ring) * 2 + x
    down = lax.rem(y + ring - 1, ring) * 2 + x
    partner = y * 2 + 1 - x
    rows = x_ref.shape[1]
    half = rows // 2
    part = half // chunks

    barrier = pltpu.get_barrier_semaphore()
    for peer in (partner, up, down):
        pl.semaphore_signal(barrier, inc=1, device_id={axis: peer}, device_id_type=MESH)
    pl.semaphore_wait(barrier, 3)

    targets = (up, down)
    copies = {}

    def dest(d, step):
        return lax.rem(y - step + ring, ring) if d == 0 else lax.rem(y + step, ring)

    for step in range(1, ring):
        for c in range(chunks):
            for d in range(2):
                rs = pl.ds(d * half + c * part, part)
                blocks = pl.ds(dest(d, step) * 2, 2)
                if step == 1:
                    src = x_ref.at[blocks, rs]
                else:
                    copies[(d, step - 1, c)].wait_recv()
                    send_buf[d, step, :, pl.ds(c * part, part)] = (
                        recv_buf[d, step - 1, :, pl.ds(c * part, part)] + x_ref[blocks, rs]
                    )
                    src = send_buf.at[d, step, :, pl.ds(c * part, part)]
                cp = pltpu.make_async_remote_copy(
                    src_ref=src, dst_ref=recv_buf.at[d, step, :, pl.ds(c * part, part)],
                    send_sem=send_sems.at[d, step, c], recv_sem=recv_sems.at[d, step, c],
                    device_id={axis: targets[d]}, device_id_type=MESH)
                cp.start()
                copies[(d, step, c)] = cp
    swaps = []
    for c in range(chunks):
        for d in range(2):
            rs = pl.ds(d * half + c * part, part)
            local = pl.ds(c * part, part)
            copies[(d, ring - 1, c)].wait_recv()
            swap_buf[0, d, local] = recv_buf[d, ring - 1, 1 - x, local] + x_ref[y * 2 + 1 - x, rs]
            out_ref[rs] = recv_buf[d, ring - 1, x, local] + x_ref[y * 2 + x, rs]
            sw = pltpu.make_async_remote_copy(
                src_ref=swap_buf.at[0, d, local], dst_ref=swap_buf.at[1, d, local],
                send_sem=swap_sems.at[0, d, c], recv_sem=swap_sems.at[1, d, c],
                device_id={axis: partner}, device_id_type=MESH)
            sw.start()
            swaps.append((d, c, sw))
    for d, c, sw in swaps:
        rs = pl.ds(d * half + c * part, part)
        sw.wait_recv()
        out_ref[rs] = out_ref[rs] + swap_buf[1, d, pl.ds(c * part, part)]
    for d, c, sw in swaps:
        sw.wait_send()
    for cp in copies.values():
        cp.wait_send()


def ring_sum(partial, axis, outer, cid, chunks=4):
    count, rows, width = partial.shape
    half = rows // 2
    return pl.pallas_call(
        functools.partial(_ring_sum_kernel, axis, outer, chunks),
        out_shape=jax.ShapeDtypeStruct((rows, width), jnp.float32),
        in_specs=[pl.BlockSpec(memory_space=pltpu.VMEM)],
        out_specs=pl.BlockSpec(memory_space=pltpu.VMEM),
        scratch_shapes=[
            pltpu.VMEM((2, outer, 2, half, width), jnp.float32),
            pltpu.VMEM((2, outer, 2, half, width), jnp.float32),
            pltpu.VMEM((2, 2, half, width), jnp.float32),
            pltpu.SemaphoreType.DMA((2, outer, chunks)),
            pltpu.SemaphoreType.DMA((2, outer, chunks)),
            pltpu.SemaphoreType.DMA((2, 2, chunks)),
        ],
        compiler_params=pltpu.CompilerParams(collective_id=cid, has_side_effects=True, vmem_limit_bytes=60 * 1024 * 1024),
    )(partial)


def _exchange_kernel(plan, *refs):
    k = len(plan)
    ins, outs = refs[:k], refs[k:2 * k]
    send_sems, recv_sems, local_sems = refs[2 * k:]
    axes = {}
    for axis, count, _ in plan:
        axes[axis] = count
    barrier = pltpu.get_barrier_semaphore()
    total = 0
    for axis, count in axes.items():
        me = lax.axis_index(axis)
        for d in range(1, count):
            pl.semaphore_signal(barrier, inc=1, device_id={axis: lax.rem(me + d, count)}, device_id_type=MESH)
        total += count - 1
    pl.semaphore_wait(barrier, total)
    started = []
    for e, (axis, count, spread) in enumerate(plan):
        me = lax.axis_index(axis)
        src = ins[e] if spread else ins[e].at[me]
        own = pltpu.make_async_copy(src, outs[e].at[me], local_sems.at[e])
        own.start()
        started.append(own)
    remote = []
    for d in range(1, max(c for _, c, _ in plan)):
        for e, (axis, count, spread) in enumerate(plan):
            if d >= count:
                continue
            me = lax.axis_index(axis)
            peer = lax.rem(me + d, count)
            src = ins[e] if spread else ins[e].at[peer]
            c = pltpu.make_async_remote_copy(
                src_ref=src, dst_ref=outs[e].at[me],
                send_sem=send_sems.at[e, d - 1], recv_sem=recv_sems.at[e, d - 1],
                device_id={axis: peer}, device_id_type=MESH)
            c.start()
            remote.append(c)
    for c in started:
        c.wait()
    for c in remote:
        c.wait_recv()
    for c in remote:
        c.wait_send()


def exchange(items, cid):
    plan = tuple((axis, count, spread) for _, axis, count, spread in items)
    shapes = []
    for x, axis, count, spread in items:
        shape = (count,) + x.shape if spread else x.shape
        shapes.append(jax.ShapeDtypeStruct(shape, x.dtype))
    widest = max(count for _, _, count, _ in items)
    return pl.pallas_call(
        functools.partial(_exchange_kernel, plan),
        out_shape=tuple(shapes),
        in_specs=[pl.BlockSpec(memory_space=pl.ANY)] * len(items),
        out_specs=tuple(pl.BlockSpec(memory_space=pl.ANY) for _ in items),
        scratch_shapes=[
            pltpu.SemaphoreType.DMA((len(items), widest - 1)),
            pltpu.SemaphoreType.DMA((len(items), widest - 1)),
            pltpu.SemaphoreType.DMA((len(items),)),
        ],
        compiler_params=pltpu.CompilerParams(collective_id=cid, has_side_effects=True),
    )(*[x for x, _, _, _ in items])


def per_device(
    forward_acts, backward_grad, stored_gate, stored_up, gate_weight, up_weight, down_weight
):
    n_pipe = lax.axis_size("pipe")
    n_tensor = lax.axis_size("tensor")
    hidden_width = gate_weight.shape[1]
    model_width = forward_acts.shape[1]
    contract_last = (((1,), (1,)), ((), ()))

    whole_acts, whole_grad = ring_gather(
        forward_acts, backward_grad, "tensor", 2, n_tensor // 2, True, 0
    )

    gate_part = jnp.dot(whole_acts, gate_weight, preferred_element_type=jnp.float32)
    up_part = jnp.dot(whole_acts, up_weight, preferred_element_type=jnp.float32)
    grad_part = lax.dot_general(
        whole_grad, down_weight, contract_last, preferred_element_type=jnp.float32
    )
    partials = jnp.concatenate([gate_part, up_part, grad_part], axis=1)
    summed = ring_sum(
        partials.reshape((n_pipe, partials.shape[0] // n_pipe, partials.shape[1])),
        "pipe",
        n_pipe // 2,
        1,
    )
    gate_pre = summed[:, :hidden_width]
    up_pre = summed[:, hidden_width : 2 * hidden_width]
    hidden_grad = summed[:, 2 * hidden_width :]
    hidden_part = (jax.nn.silu(gate_pre) * up_pre).astype(jnp.bfloat16)
    local_slopes = make_slopes(hidden_grad, stored_gate, stored_up)

    got_hidden, got_slopes = exchange(
        [(hidden_part, "pipe", n_pipe, True), (local_slopes, "pipe", n_pipe, True)], 2
    )
    hidden = got_hidden.reshape(n_pipe * hidden_part.shape[0], hidden_width)
    all_slopes = got_slopes.reshape(n_pipe * local_slopes.shape[0], 2 * hidden_width)
    gate_slopes = all_slopes[:, :hidden_width]
    up_slopes = all_slopes[:, hidden_width:]

    out_part = jnp.dot(hidden, down_weight, preferred_element_type=jnp.float32)
    in_part = lax.dot_general(
        gate_slopes, gate_weight, contract_last, preferred_element_type=jnp.float32
    ) + lax.dot_general(up_slopes, up_weight, contract_last, preferred_element_type=jnp.float32)
    def blocks(partial):
        return partial.reshape((n_tensor, partial.shape[0] // n_tensor, partial.shape[1])).astype(
            TENSOR_LINK
        )

    got_out, got_in = exchange(
        [(blocks(out_part), "tensor", n_tensor, False), (blocks(in_part), "tensor", n_tensor, False)], 3
    )
    layer_output = got_out.astype(jnp.float32).sum(axis=0).astype(jnp.bfloat16)
    input_grad = got_in.astype(jnp.float32).sum(axis=0).astype(jnp.bfloat16)
    return (layer_output, input_grad)


def solution(mesh):
    in_specs = (
        P(("dp", "tensor"), "pipe"),
        P(("dp", "tensor"), "pipe"),
        P(("dp", "pipe"), "tensor"),
        P(("dp", "pipe"), "tensor"),
        P("pipe", "tensor"),
        P("pipe", "tensor"),
        P("tensor", "pipe"),
    )
    out_specs = (P(("dp", "tensor"), "pipe"), P(("dp", "tensor"), "pipe"))
    return jax.shard_map(
        per_device, mesh=mesh, in_specs=in_specs, out_specs=out_specs, check_vma=False
    )
```

```python
import functools

import jax
import jax.numpy as jnp
from jax import lax
from jax.experimental import pallas as pl
from jax.experimental.pallas import tpu as pltpu
from jax.sharding import PartitionSpec as P

PIPE_LINK = jnp.float32
TENSOR_LINK = jnp.bfloat16
MESH = pl.DeviceIdType.MESH


def make_slopes(hidden_grad, gate_vals, up_vals):
    gate_wide = gate_vals.astype(jnp.float32)
    up_wide = up_vals.astype(jnp.float32)
    sigma = jax.nn.sigmoid(gate_wide)
    gate_slope = (hidden_grad * up_wide * sigma * (1.0 + gate_wide * (1.0 - sigma))).astype(
        jnp.bfloat16
    )
    up_slope = (hidden_grad * gate_wide * sigma).astype(jnp.bfloat16)
    return jnp.concatenate([gate_slope, up_slope], axis=1)


def gather_rows(block, axis, count):
    sent = jnp.broadcast_to(block[None], (count,) + block.shape)
    got = lax.all_to_all(sent, axis, 0, 0, tiled=False)
    return got.reshape((count * block.shape[0],) + block.shape[1:])


def scatter_sum_rows(partial, axis, count, link_dtype):
    rows = partial.shape[0] // count
    sent = partial.reshape((count, rows) + partial.shape[1:]).astype(link_dtype)
    got = lax.all_to_all(sent, axis, 0, 0, tiled=False)
    return got.astype(jnp.float32).sum(axis=0)


def _ring_gather_kernel(axis, outer, inner, ring_on_inner, halves, x_ref, first_ref, second_ref, send_sems, recv_sems, swap_sems, local_sems):
    me = lax.axis_index(axis)
    o = me // inner
    i = me % inner
    if ring_on_inner:
        ring = inner
        pos, other = i, o
        def at(p, q):
            return q * inner + p
    else:
        ring = outer
        pos, other = o, i
        def at(p, q):
            return p * inner + q
    partner = at(pos, 1 - other)
    up = at(lax.rem(pos + 1, ring), other)
    down = at(lax.rem(pos + ring - 1, ring), other)
    rows = x_ref.shape[1]
    part = rows // halves
    steps = (ring // 2, ring // 2)

    def carries(d, step, r):
        if ring % 2 == 1 or step < ring // 2:
            return True
        return (r < halves // 2) == (d == 0)

    barrier = pltpu.get_barrier_semaphore()
    for peer in (partner, up, down):
        pl.semaphore_signal(barrier, inc=1, device_id={axis: peer}, device_id_type=MESH)
    pl.semaphore_wait(barrier, 3)

    outs = (first_ref, second_ref)
    locals_ = []
    swaps = []
    for a in range(2):
        c = pltpu.make_async_copy(x_ref.at[a], outs[a].at[other, pos], local_sems.at[a])
        c.start()
        locals_.append(c)
        s = pltpu.make_async_remote_copy(
            src_ref=x_ref.at[a], dst_ref=outs[a].at[other, pos],
            send_sem=swap_sems.at[0, a], recv_sem=swap_sems.at[1, a],
            device_id={axis: partner}, device_id_type=MESH)
        s.start()
        swaps.append(s)

    targets = (up, down)
    copies = {}

    def chunk_copy(d, step, which, r, a):
        slot = lax.rem(pos - step + 1 + ring, ring) if d == 0 else lax.rem(pos + step - 1, ring)
        half = other if which == 0 else 1 - other
        rs = pl.ds(r * part, part)
        if step == 1 and which == 0:
            src = x_ref.at[a, rs]
        else:
            src = outs[a].at[half, slot, rs]
        k = (((d * ring + step - 1) * 2 + which) * halves + r) * 2 + a
        return pltpu.make_async_remote_copy(
            src_ref=src, dst_ref=outs[a].at[half, slot, rs],
            send_sem=send_sems.at[k], recv_sem=recv_sems.at[k],
            device_id={axis: targets[d]}, device_id_type=MESH)

    last = {}
    for step in range(1, steps[0] + 1):
        for which in range(2):
            if step == 1 and which == 1:
                for s in swaps:
                    s.wait_recv()
            for r in range(halves):
                for a in range(2):
                    for d in range(2):
                        if not carries(d, step, r):
                            continue
                        if step > 1:
                            last[(d, which, r, a)].wait_recv()
                        c = chunk_copy(d, step, which, r, a)
                        c.start()
                        copies[(d, step, which, r, a)] = c
                        last[(d, which, r, a)] = c
    for c in last.values():
        c.wait_recv()
    for c in locals_:
        c.wait()
    for s in swaps:
        s.wait_send()
    for c in copies.values():
        c.wait_send()


def ring_gather(first, second, axis, outer, inner, ring_on_inner, cid, halves=2):
    rows, width = first.shape
    ring = inner if ring_on_inner else outer
    shape = (2, ring, rows, width)
    x = jnp.stack([first, second])
    n_copies = 2 * ring * 2 * halves * 2
    f, s = pl.pallas_call(
        functools.partial(_ring_gather_kernel, axis, outer, inner, ring_on_inner, halves),
        out_shape=(jax.ShapeDtypeStruct(shape, first.dtype), jax.ShapeDtypeStruct(shape, second.dtype)),
        in_specs=[pl.BlockSpec(memory_space=pltpu.VMEM)],
        out_specs=(pl.BlockSpec(memory_space=pltpu.VMEM), pl.BlockSpec(memory_space=pltpu.VMEM)),
        scratch_shapes=[
            pltpu.SemaphoreType.DMA((n_copies,)),
            pltpu.SemaphoreType.DMA((n_copies,)),
            pltpu.SemaphoreType.DMA((2, 2)),
            pltpu.SemaphoreType.DMA((2,)),
        ],
        compiler_params=pltpu.CompilerParams(collective_id=cid, has_side_effects=True),
    )(x)
    if ring_on_inner:
        return f.reshape(2 * ring * rows, width), s.reshape(2 * ring * rows, width)
    return (f.transpose(1, 0, 2, 3).reshape(2 * ring * rows, width),
            s.transpose(1, 0, 2, 3).reshape(2 * ring * rows, width))


def _ring_sum_kernel(axis, outer, chunks, x_ref, out_ref, send_buf, recv_buf, swap_buf, send_sems, recv_sems, swap_sems):
    me = lax.axis_index(axis)
    y = me // 2
    x = me % 2
    ring = outer
    up = lax.rem(y + 1, ring) * 2 + x
    down = lax.rem(y + ring - 1, ring) * 2 + x
    partner = y * 2 + 1 - x
    rows = x_ref.shape[1]
    half = rows // 2
    part = half // chunks

    barrier = pltpu.get_barrier_semaphore()
    for peer in (partner, up, down):
        pl.semaphore_signal(barrier, inc=1, device_id={axis: peer}, device_id_type=MESH)
    pl.semaphore_wait(barrier, 3)

    targets = (up, down)
    copies = {}

    def dest(d, step):
        return lax.rem(y - step + ring, ring) if d == 0 else lax.rem(y + step, ring)

    for step in range(1, ring):
        for c in range(chunks):
            for d in range(2):
                rs = pl.ds(d * half + c * part, part)
                blocks = pl.ds(dest(d, step) * 2, 2)
                if step == 1:
                    src = x_ref.at[blocks, rs]
                else:
                    copies[(d, step - 1, c)].wait_recv()
                    send_buf[d, step, :, pl.ds(c * part, part)] = (
                        recv_buf[d, step - 1, :, pl.ds(c * part, part)] + x_ref[blocks, rs]
                    )
                    src = send_buf.at[d, step, :, pl.ds(c * part, part)]
                cp = pltpu.make_async_remote_copy(
                    src_ref=src, dst_ref=recv_buf.at[d, step, :, pl.ds(c * part, part)],
                    send_sem=send_sems.at[d, step, c], recv_sem=recv_sems.at[d, step, c],
                    device_id={axis: targets[d]}, device_id_type=MESH)
                cp.start()
                copies[(d, step, c)] = cp
    swaps = []
    for c in range(chunks):
        for d in range(2):
            rs = pl.ds(d * half + c * part, part)
            local = pl.ds(c * part, part)
            copies[(d, ring - 1, c)].wait_recv()
            swap_buf[0, d, local] = recv_buf[d, ring - 1, 1 - x, local] + x_ref[y * 2 + 1 - x, rs]
            out_ref[rs] = recv_buf[d, ring - 1, x, local] + x_ref[y * 2 + x, rs]
            sw = pltpu.make_async_remote_copy(
                src_ref=swap_buf.at[0, d, local], dst_ref=swap_buf.at[1, d, local],
                send_sem=swap_sems.at[0, d, c], recv_sem=swap_sems.at[1, d, c],
                device_id={axis: partner}, device_id_type=MESH)
            sw.start()
            swaps.append((d, c, sw))
    for d, c, sw in swaps:
        rs = pl.ds(d * half + c * part, part)
        sw.wait_recv()
        out_ref[rs] = out_ref[rs] + swap_buf[1, d, pl.ds(c * part, part)]
    for d, c, sw in swaps:
        sw.wait_send()
    for cp in copies.values():
        cp.wait_send()


def ring_sum(partial, axis, outer, cid, chunks=4):
    count, rows, width = partial.shape
    half = rows // 2
    return pl.pallas_call(
        functools.partial(_ring_sum_kernel, axis, outer, chunks),
        out_shape=jax.ShapeDtypeStruct((rows, width), jnp.float32),
        in_specs=[pl.BlockSpec(memory_space=pltpu.VMEM)],
        out_specs=pl.BlockSpec(memory_space=pltpu.VMEM),
        scratch_shapes=[
            pltpu.VMEM((2, outer, 2, half, width), jnp.float32),
            pltpu.VMEM((2, outer, 2, half, width), jnp.float32),
            pltpu.VMEM((2, 2, half, width), jnp.float32),
            pltpu.SemaphoreType.DMA((2, outer, chunks)),
            pltpu.SemaphoreType.DMA((2, outer, chunks)),
            pltpu.SemaphoreType.DMA((2, 2, chunks)),
        ],
        compiler_params=pltpu.CompilerParams(collective_id=cid, has_side_effects=True, vmem_limit_bytes=60 * 1024 * 1024),
    )(partial)


def per_device(
    forward_acts, backward_grad, stored_gate, stored_up, gate_weight, up_weight, down_weight
):
    n_pipe = lax.axis_size("pipe")
    n_tensor = lax.axis_size("tensor")
    hidden_width = gate_weight.shape[1]
    model_width = forward_acts.shape[1]
    contract_last = (((1,), (1,)), ((), ()))

    whole_acts, whole_grad = ring_gather(
        forward_acts, backward_grad, "tensor", 2, n_tensor // 2, True, 0
    )

    gate_part = jnp.dot(whole_acts, gate_weight, preferred_element_type=jnp.float32)
    up_part = jnp.dot(whole_acts, up_weight, preferred_element_type=jnp.float32)
    grad_part = lax.dot_general(
        whole_grad, down_weight, contract_last, preferred_element_type=jnp.float32
    )
    partials = jnp.concatenate([gate_part, up_part, grad_part], axis=1)
    summed = ring_sum(
        partials.reshape((n_pipe, partials.shape[0] // n_pipe, partials.shape[1])),
        "pipe",
        n_pipe // 2,
        1,
    )
    gate_pre = summed[:, :hidden_width]
    up_pre = summed[:, hidden_width : 2 * hidden_width]
    hidden_grad = summed[:, 2 * hidden_width :]
    hidden_part = (jax.nn.silu(gate_pre) * up_pre).astype(jnp.bfloat16)
    local_slopes = make_slopes(hidden_grad, stored_gate, stored_up)

    rows = gather_rows(jnp.concatenate([hidden_part, local_slopes], axis=1), "pipe", n_pipe)
    hidden = rows[:, :hidden_width]
    gate_slopes = rows[:, hidden_width : 2 * hidden_width]
    up_slopes = rows[:, 2 * hidden_width :]

    out_part = jnp.dot(hidden, down_weight, preferred_element_type=jnp.float32)
    in_part = lax.dot_general(
        gate_slopes, gate_weight, contract_last, preferred_element_type=jnp.float32
    ) + lax.dot_general(up_slopes, up_weight, contract_last, preferred_element_type=jnp.float32)
    finished = scatter_sum_rows(
        jnp.concatenate([out_part, in_part], axis=1), "tensor", n_tensor, TENSOR_LINK
    ).astype(jnp.bfloat16)
    return (finished[:, :model_width], finished[:, model_width:])


def solution(mesh):
    in_specs = (
        P(("dp", "tensor"), "pipe"),
        P(("dp", "tensor"), "pipe"),
        P(("dp", "pipe"), "tensor"),
        P(("dp", "pipe"), "tensor"),
        P("pipe", "tensor"),
        P("pipe", "tensor"),
        P("tensor", "pipe"),
    )
    out_specs = (P(("dp", "tensor"), "pipe"), P(("dp", "tensor"), "pipe"))
    return jax.shard_map(
        per_device, mesh=mesh, in_specs=in_specs, out_specs=out_specs, check_vma=False
    )
```

```python
import functools

import jax
import jax.numpy as jnp
from jax import lax
from jax.experimental import pallas as pl
from jax.experimental.pallas import tpu as pltpu
from jax.sharding import PartitionSpec as P

TENSOR_LINK = jnp.bfloat16
MESH = pl.DeviceIdType.MESH


def make_slopes(hidden_grad, gate_vals, up_vals):
    gate_wide = gate_vals.astype(jnp.float32)
    up_wide = up_vals.astype(jnp.float32)
    sigma = jax.nn.sigmoid(gate_wide)
    gate_slope = (hidden_grad * up_wide * sigma * (1.0 + gate_wide * (1.0 - sigma))).astype(
        jnp.bfloat16
    )
    up_slope = (hidden_grad * gate_wide * sigma).astype(jnp.bfloat16)
    return jnp.concatenate([gate_slope, up_slope], axis=1)


def scatter_sum_rows(partial, axis, count, link_dtype):
    rows = partial.shape[0] // count
    sent = partial.reshape((count, rows) + partial.shape[1:]).astype(link_dtype)
    got = lax.all_to_all(sent, axis, 0, 0, tiled=False)
    return got.astype(jnp.float32).sum(axis=0)


def _ring_gather_kernel(axis, outer, inner, ring_on_inner, halves, x_ref, first_ref, second_ref, send_sems, recv_sems, swap_sems, local_sems):
    me = lax.axis_index(axis)
    o = me // inner
    i = me % inner
    if ring_on_inner:
        ring = inner
        pos, other = i, o
        def at(p, q):
            return q * inner + p
    else:
        ring = outer
        pos, other = o, i
        def at(p, q):
            return p * inner + q
    partner = at(pos, 1 - other)
    up = at(lax.rem(pos + 1, ring), other)
    down = at(lax.rem(pos + ring - 1, ring), other)
    rows = x_ref.shape[1]
    part = rows // halves
    steps = (ring // 2, ring // 2)

    def carries(d, step, r):
        if ring % 2 == 1 or step < ring // 2:
            return True
        return (r < halves // 2) == (d == 0)

    barrier = pltpu.get_barrier_semaphore()
    for peer in (partner, up, down):
        pl.semaphore_signal(barrier, inc=1, device_id={axis: peer}, device_id_type=MESH)
    pl.semaphore_wait(barrier, 3)

    outs = (first_ref, second_ref)
    locals_ = []
    swaps = []
    for a in range(2):
        c = pltpu.make_async_copy(x_ref.at[a], outs[a].at[other, pos], local_sems.at[a])
        c.start()
        locals_.append(c)
        s = pltpu.make_async_remote_copy(
            src_ref=x_ref.at[a], dst_ref=outs[a].at[other, pos],
            send_sem=swap_sems.at[0, a], recv_sem=swap_sems.at[1, a],
            device_id={axis: partner}, device_id_type=MESH)
        s.start()
        swaps.append(s)

    targets = (up, down)
    copies = {}

    def chunk_copy(d, step, which, r, a):
        slot = lax.rem(pos - step + 1 + ring, ring) if d == 0 else lax.rem(pos + step - 1, ring)
        half = other if which == 0 else 1 - other
        rs = pl.ds(r * part, part)
        if step == 1 and which == 0:
            src = x_ref.at[a, rs]
        else:
            src = outs[a].at[half, slot, rs]
        k = (((d * ring + step - 1) * 2 + which) * halves + r) * 2 + a
        return pltpu.make_async_remote_copy(
            src_ref=src, dst_ref=outs[a].at[half, slot, rs],
            send_sem=send_sems.at[k], recv_sem=recv_sems.at[k],
            device_id={axis: targets[d]}, device_id_type=MESH)

    last = {}
    for step in range(1, steps[0] + 1):
        for which in range(2):
            if step == 1 and which == 1:
                for s in swaps:
                    s.wait_recv()
            for r in range(halves):
                for a in range(2):
                    for d in range(2):
                        if not carries(d, step, r):
                            continue
                        if step > 1:
                            last[(d, which, r, a)].wait_recv()
                        c = chunk_copy(d, step, which, r, a)
                        c.start()
                        copies[(d, step, which, r, a)] = c
                        last[(d, which, r, a)] = c
    for c in last.values():
        c.wait_recv()
    for c in locals_:
        c.wait()
    for s in swaps:
        s.wait_send()
    for c in copies.values():
        c.wait_send()


def ring_gather(first, second, axis, outer, inner, ring_on_inner, cid, halves=2):
    rows, width = first.shape
    ring = inner if ring_on_inner else outer
    shape = (2, ring, rows, width)
    x = jnp.stack([first, second])
    n_copies = 2 * ring * 2 * halves * 2
    f, s = pl.pallas_call(
        functools.partial(_ring_gather_kernel, axis, outer, inner, ring_on_inner, halves),
        out_shape=(jax.ShapeDtypeStruct(shape, first.dtype), jax.ShapeDtypeStruct(shape, second.dtype)),
        in_specs=[pl.BlockSpec(memory_space=pltpu.VMEM)],
        out_specs=(pl.BlockSpec(memory_space=pltpu.VMEM), pl.BlockSpec(memory_space=pltpu.VMEM)),
        scratch_shapes=[
            pltpu.SemaphoreType.DMA((n_copies,)),
            pltpu.SemaphoreType.DMA((n_copies,)),
            pltpu.SemaphoreType.DMA((2, 2)),
            pltpu.SemaphoreType.DMA((2,)),
        ],
        compiler_params=pltpu.CompilerParams(collective_id=cid, has_side_effects=True),
    )(x)
    if ring_on_inner:
        return f.reshape(2 * ring * rows, width), s.reshape(2 * ring * rows, width)
    return (f.transpose(1, 0, 2, 3).reshape(2 * ring * rows, width),
            s.transpose(1, 0, 2, 3).reshape(2 * ring * rows, width))


def _ring_sum_kernel(axis, outer, chunks, x_ref, out_ref, send_buf, recv_buf, swap_buf, send_sems, recv_sems, swap_sems):
    me = lax.axis_index(axis)
    y = me // 2
    x = me % 2
    ring = outer
    up = lax.rem(y + 1, ring) * 2 + x
    down = lax.rem(y + ring - 1, ring) * 2 + x
    partner = y * 2 + 1 - x
    rows = x_ref.shape[1]
    half = rows // 2
    part = half // chunks

    barrier = pltpu.get_barrier_semaphore()
    for peer in (partner, up, down):
        pl.semaphore_signal(barrier, inc=1, device_id={axis: peer}, device_id_type=MESH)
    pl.semaphore_wait(barrier, 3)

    targets = (up, down)
    copies = {}

    def dest(d, step):
        return lax.rem(y - step + ring, ring) if d == 0 else lax.rem(y + step, ring)

    for step in range(1, ring):
        for c in range(chunks):
            for d in range(2):
                rs = pl.ds(d * half + c * part, part)
                blocks = pl.ds(dest(d, step) * 2, 2)
                if step == 1:
                    src = x_ref.at[blocks, rs]
                else:
                    copies[(d, step - 1, c)].wait_recv()
                    send_buf[d, step, :, pl.ds(c * part, part)] = (
                        recv_buf[d, step - 1, :, pl.ds(c * part, part)] + x_ref[blocks, rs]
                    )
                    src = send_buf.at[d, step, :, pl.ds(c * part, part)]
                cp = pltpu.make_async_remote_copy(
                    src_ref=src, dst_ref=recv_buf.at[d, step, :, pl.ds(c * part, part)],
                    send_sem=send_sems.at[d, step, c], recv_sem=recv_sems.at[d, step, c],
                    device_id={axis: targets[d]}, device_id_type=MESH)
                cp.start()
                copies[(d, step, c)] = cp
    swaps = []
    for c in range(chunks):
        for d in range(2):
            rs = pl.ds(d * half + c * part, part)
            local = pl.ds(c * part, part)
            copies[(d, ring - 1, c)].wait_recv()
            swap_buf[0, d, local] = recv_buf[d, ring - 1, 1 - x, local] + x_ref[y * 2 + 1 - x, rs]
            out_ref[rs] = recv_buf[d, ring - 1, x, local] + x_ref[y * 2 + x, rs]
            sw = pltpu.make_async_remote_copy(
                src_ref=swap_buf.at[0, d, local], dst_ref=swap_buf.at[1, d, local],
                send_sem=swap_sems.at[0, d, c], recv_sem=swap_sems.at[1, d, c],
                device_id={axis: partner}, device_id_type=MESH)
            sw.start()
            swaps.append((d, c, sw))
    for d, c, sw in swaps:
        rs = pl.ds(d * half + c * part, part)
        sw.wait_recv()
        out_ref[rs] = out_ref[rs] + swap_buf[1, d, pl.ds(c * part, part)]
    for d, c, sw in swaps:
        sw.wait_send()
    for cp in copies.values():
        cp.wait_send()


def ring_sum(partial, axis, outer, cid, chunks=4):
    count, rows, width = partial.shape
    half = rows // 2
    return pl.pallas_call(
        functools.partial(_ring_sum_kernel, axis, outer, chunks),
        out_shape=jax.ShapeDtypeStruct((rows, width), jnp.float32),
        in_specs=[pl.BlockSpec(memory_space=pltpu.VMEM)],
        out_specs=pl.BlockSpec(memory_space=pltpu.VMEM),
        scratch_shapes=[
            pltpu.VMEM((2, outer, 2, half, width), jnp.float32),
            pltpu.VMEM((2, outer, 2, half, width), jnp.float32),
            pltpu.VMEM((2, 2, half, width), jnp.float32),
            pltpu.SemaphoreType.DMA((2, outer, chunks)),
            pltpu.SemaphoreType.DMA((2, outer, chunks)),
            pltpu.SemaphoreType.DMA((2, 2, chunks)),
        ],
        compiler_params=pltpu.CompilerParams(collective_id=cid, has_side_effects=True, vmem_limit_bytes=60 * 1024 * 1024),
    )(partial)


def _exchange_kernel(plan, *refs):
    k = len(plan)
    ins, outs = refs[:k], refs[k:2 * k]
    send_sems, recv_sems, local_sems = refs[2 * k:]
    axes = {}
    for axis, count, _ in plan:
        axes[axis] = count
    barrier = pltpu.get_barrier_semaphore()
    total = 0
    for axis, count in axes.items():
        me = lax.axis_index(axis)
        for d in range(1, count):
            pl.semaphore_signal(barrier, inc=1, device_id={axis: lax.rem(me + d, count)}, device_id_type=MESH)
        total += count - 1
    pl.semaphore_wait(barrier, total)
    started = []
    for e, (axis, count, spread) in enumerate(plan):
        me = lax.axis_index(axis)
        src = ins[e] if spread else ins[e].at[me]
        own = pltpu.make_async_copy(src, outs[e].at[me], local_sems.at[e])
        own.start()
        started.append(own)
    remote = []
    for d in range(1, max(c for _, c, _ in plan)):
        for e, (axis, count, spread) in enumerate(plan):
            if d >= count:
                continue
            me = lax.axis_index(axis)
            peer = lax.rem(me + d, count)
            src = ins[e] if spread else ins[e].at[peer]
            c = pltpu.make_async_remote_copy(
                src_ref=src, dst_ref=outs[e].at[me],
                send_sem=send_sems.at[e, d - 1], recv_sem=recv_sems.at[e, d - 1],
                device_id={axis: peer}, device_id_type=MESH)
            c.start()
            remote.append(c)
    for c in started:
        c.wait()
    for c in remote:
        c.wait_recv()
    for c in remote:
        c.wait_send()


def exchange(items, cid):
    plan = tuple((axis, count, spread) for _, axis, count, spread in items)
    shapes = []
    for x, axis, count, spread in items:
        shape = (count,) + x.shape if spread else x.shape
        shapes.append(jax.ShapeDtypeStruct(shape, x.dtype))
    widest = max(count for _, _, count, _ in items)
    return pl.pallas_call(
        functools.partial(_exchange_kernel, plan),
        out_shape=tuple(shapes),
        in_specs=[pl.BlockSpec(memory_space=pl.ANY)] * len(items),
        out_specs=tuple(pl.BlockSpec(memory_space=pl.ANY) for _ in items),
        scratch_shapes=[
            pltpu.SemaphoreType.DMA((len(items), widest - 1)),
            pltpu.SemaphoreType.DMA((len(items), widest - 1)),
            pltpu.SemaphoreType.DMA((len(items),)),
        ],
        compiler_params=pltpu.CompilerParams(collective_id=cid, has_side_effects=True),
    )(*[x for x, _, _, _ in items])


def per_device(
    forward_acts, backward_grad, stored_gate, stored_up, gate_weight, up_weight, down_weight
):
    n_pipe = lax.axis_size("pipe")
    n_tensor = lax.axis_size("tensor")
    hidden_width = gate_weight.shape[1]
    model_width = forward_acts.shape[1]
    contract_last = (((1,), (1,)), ((), ()))

    whole_acts, whole_grad = ring_gather(
        forward_acts, backward_grad, "tensor", 2, n_tensor // 2, True, 0
    )

    gate_part = jnp.dot(whole_acts, gate_weight, preferred_element_type=jnp.float32)
    up_part = jnp.dot(whole_acts, up_weight, preferred_element_type=jnp.float32)
    grad_part = lax.dot_general(
        whole_grad, down_weight, contract_last, preferred_element_type=jnp.float32
    )
    partials = jnp.concatenate([gate_part, up_part, grad_part], axis=1)
    summed = ring_sum(
        partials.reshape((n_pipe, partials.shape[0] // n_pipe, partials.shape[1])),
        "pipe",
        n_pipe // 2,
        1,
    )
    gate_pre = summed[:, :hidden_width]
    up_pre = summed[:, hidden_width : 2 * hidden_width]
    hidden_grad = summed[:, 2 * hidden_width :]
    hidden_part = (jax.nn.silu(gate_pre) * up_pre).astype(jnp.bfloat16)
    local_slopes = make_slopes(hidden_grad, stored_gate, stored_up)

    local_rows = jnp.concatenate([hidden_part, local_slopes], axis=1)
    (rows,) = exchange([(local_rows, "pipe", n_pipe, True)], 2)
    rows = rows.reshape(n_pipe * local_rows.shape[0], local_rows.shape[1])
    hidden = rows[:, :hidden_width]
    gate_slopes = rows[:, hidden_width : 2 * hidden_width]
    up_slopes = rows[:, 2 * hidden_width :]

    out_part = jnp.dot(hidden, down_weight, preferred_element_type=jnp.float32)
    in_part = lax.dot_general(
        gate_slopes, gate_weight, contract_last, preferred_element_type=jnp.float32
    ) + lax.dot_general(up_slopes, up_weight, contract_last, preferred_element_type=jnp.float32)
    finished = scatter_sum_rows(
        jnp.concatenate([out_part, in_part], axis=1), "tensor", n_tensor, TENSOR_LINK
    ).astype(jnp.bfloat16)
    return (finished[:, :model_width], finished[:, model_width:])


def solution(mesh):
    in_specs = (
        P(("dp", "tensor"), "pipe"),
        P(("dp", "tensor"), "pipe"),
        P(("dp", "pipe"), "tensor"),
        P(("dp", "pipe"), "tensor"),
        P("pipe", "tensor"),
        P("pipe", "tensor"),
        P("tensor", "pipe"),
    )
    out_specs = (P(("dp", "tensor"), "pipe"), P(("dp", "tensor"), "pipe"))
    return jax.shard_map(
        per_device, mesh=mesh, in_specs=in_specs, out_specs=out_specs, check_vma=False
    )
```

```python
import functools

import jax
import jax.numpy as jnp
from jax import lax
from jax.experimental import pallas as pl
from jax.experimental.pallas import tpu as pltpu
from jax.sharding import PartitionSpec as P

PIPE_LINK = jnp.float32
TENSOR_LINK = jnp.bfloat16
MESH = pl.DeviceIdType.MESH


def make_slopes(hidden_grad, gate_vals, up_vals):
    gate_wide = gate_vals.astype(jnp.float32)
    up_wide = up_vals.astype(jnp.float32)
    sigma = jax.nn.sigmoid(gate_wide)
    gate_slope = (hidden_grad * up_wide * sigma * (1.0 + gate_wide * (1.0 - sigma))).astype(
        jnp.bfloat16
    )
    up_slope = (hidden_grad * gate_wide * sigma).astype(jnp.bfloat16)
    return jnp.concatenate([gate_slope, up_slope], axis=1)


def gather_rows(block, axis, count):
    sent = jnp.broadcast_to(block[None], (count,) + block.shape)
    got = lax.all_to_all(sent, axis, 0, 0, tiled=False)
    return got.reshape((count * block.shape[0],) + block.shape[1:])


def scatter_sum_rows(partial, axis, count, link_dtype):
    rows = partial.shape[0] // count
    sent = partial.reshape((count, rows) + partial.shape[1:]).astype(link_dtype)
    got = lax.all_to_all(sent, axis, 0, 0, tiled=False)
    return got.astype(jnp.float32).sum(axis=0)


def _ring_gather_kernel(axis, outer, inner, ring_on_inner, halves, x_ref, first_ref, second_ref, send_sems, recv_sems, swap_sems, local_sems):
    me = lax.axis_index(axis)
    o = me // inner
    i = me % inner
    if ring_on_inner:
        ring = inner
        pos, other = i, o
        def at(p, q):
            return q * inner + p
    else:
        ring = outer
        pos, other = o, i
        def at(p, q):
            return p * inner + q
    partner = at(pos, 1 - other)
    up = at(lax.rem(pos + 1, ring), other)
    down = at(lax.rem(pos + ring - 1, ring), other)
    rows = x_ref.shape[1]
    part = rows // halves
    steps = (ring // 2, ring // 2)

    def carries(d, step, r):
        if ring % 2 == 1 or step < ring // 2:
            return True
        return (r < halves // 2) == (d == 0)

    barrier = pltpu.get_barrier_semaphore()
    for peer in (partner, up, down):
        pl.semaphore_signal(barrier, inc=1, device_id={axis: peer}, device_id_type=MESH)
    pl.semaphore_wait(barrier, 3)

    outs = (first_ref, second_ref)
    locals_ = []
    swaps = []
    for a in range(2):
        c = pltpu.make_async_copy(x_ref.at[a], outs[a].at[other, pos], local_sems.at[a])
        c.start()
        locals_.append(c)
        s = pltpu.make_async_remote_copy(
            src_ref=x_ref.at[a], dst_ref=outs[a].at[other, pos],
            send_sem=swap_sems.at[0, a], recv_sem=swap_sems.at[1, a],
            device_id={axis: partner}, device_id_type=MESH)
        s.start()
        swaps.append(s)

    targets = (up, down)
    copies = {}

    def chunk_copy(d, step, which, r, a):
        slot = lax.rem(pos - step + 1 + ring, ring) if d == 0 else lax.rem(pos + step - 1, ring)
        half = other if which == 0 else 1 - other
        rs = pl.ds(r * part, part)
        if step == 1 and which == 0:
            src = x_ref.at[a, rs]
        else:
            src = outs[a].at[half, slot, rs]
        k = (((d * ring + step - 1) * 2 + which) * halves + r) * 2 + a
        return pltpu.make_async_remote_copy(
            src_ref=src, dst_ref=outs[a].at[half, slot, rs],
            send_sem=send_sems.at[k], recv_sem=recv_sems.at[k],
            device_id={axis: targets[d]}, device_id_type=MESH)

    last = {}
    for step in range(1, steps[0] + 1):
        for which in range(2):
            if step == 1 and which == 1:
                for s in swaps:
                    s.wait_recv()
            for r in range(halves):
                for a in range(2):
                    for d in range(2):
                        if not carries(d, step, r):
                            continue
                        if step > 1:
                            last[(d, which, r, a)].wait_recv()
                        c = chunk_copy(d, step, which, r, a)
                        c.start()
                        copies[(d, step, which, r, a)] = c
                        last[(d, which, r, a)] = c
    for c in last.values():
        c.wait_recv()
    for c in locals_:
        c.wait()
    for s in swaps:
        s.wait_send()
    for c in copies.values():
        c.wait_send()


def ring_gather(first, second, axis, outer, inner, ring_on_inner, cid, halves=4):
    rows, width = first.shape
    ring = inner if ring_on_inner else outer
    shape = (2, ring, rows, width)
    x = jnp.stack([first, second])
    n_copies = 2 * ring * 2 * halves * 2
    f, s = pl.pallas_call(
        functools.partial(_ring_gather_kernel, axis, outer, inner, ring_on_inner, halves),
        out_shape=(jax.ShapeDtypeStruct(shape, first.dtype), jax.ShapeDtypeStruct(shape, second.dtype)),
        in_specs=[pl.BlockSpec(memory_space=pltpu.VMEM)],
        out_specs=(pl.BlockSpec(memory_space=pltpu.VMEM), pl.BlockSpec(memory_space=pltpu.VMEM)),
        scratch_shapes=[
            pltpu.SemaphoreType.DMA((n_copies,)),
            pltpu.SemaphoreType.DMA((n_copies,)),
            pltpu.SemaphoreType.DMA((2, 2)),
            pltpu.SemaphoreType.DMA((2,)),
        ],
        compiler_params=pltpu.CompilerParams(collective_id=cid, has_side_effects=True),
    )(x)
    if ring_on_inner:
        return f.reshape(2 * ring * rows, width), s.reshape(2 * ring * rows, width)
    return (f.transpose(1, 0, 2, 3).reshape(2 * ring * rows, width),
            s.transpose(1, 0, 2, 3).reshape(2 * ring * rows, width))


def _ring_sum_kernel(axis, outer, chunks, x_ref, out_ref, send_buf, recv_buf, swap_buf, send_sems, recv_sems, swap_sems):
    me = lax.axis_index(axis)
    y = me // 2
    x = me % 2
    ring = outer
    up = lax.rem(y + 1, ring) * 2 + x
    down = lax.rem(y + ring - 1, ring) * 2 + x
    partner = y * 2 + 1 - x
    rows = x_ref.shape[1]
    half = rows // 2
    part = half // chunks

    barrier = pltpu.get_barrier_semaphore()
    for peer in (partner, up, down):
        pl.semaphore_signal(barrier, inc=1, device_id={axis: peer}, device_id_type=MESH)
    pl.semaphore_wait(barrier, 3)

    targets = (up, down)
    copies = {}

    def dest(d, step):
        return lax.rem(y - step + ring, ring) if d == 0 else lax.rem(y + step, ring)

    for step in range(1, ring):
        for c in range(chunks):
            for d in range(2):
                rs = pl.ds(d * half + c * part, part)
                blocks = pl.ds(dest(d, step) * 2, 2)
                if step == 1:
                    src = x_ref.at[blocks, rs]
                else:
                    copies[(d, step - 1, c)].wait_recv()
                    send_buf[d, step, :, pl.ds(c * part, part)] = (
                        recv_buf[d, step - 1, :, pl.ds(c * part, part)] + x_ref[blocks, rs]
                    )
                    src = send_buf.at[d, step, :, pl.ds(c * part, part)]
                cp = pltpu.make_async_remote_copy(
                    src_ref=src, dst_ref=recv_buf.at[d, step, :, pl.ds(c * part, part)],
                    send_sem=send_sems.at[d, step, c], recv_sem=recv_sems.at[d, step, c],
                    device_id={axis: targets[d]}, device_id_type=MESH)
                cp.start()
                copies[(d, step, c)] = cp
    swaps = []
    for c in range(chunks):
        for d in range(2):
            rs = pl.ds(d * half + c * part, part)
            local = pl.ds(c * part, part)
            copies[(d, ring - 1, c)].wait_recv()
            swap_buf[0, d, local] = recv_buf[d, ring - 1, 1 - x, local] + x_ref[y * 2 + 1 - x, rs]
            out_ref[rs] = recv_buf[d, ring - 1, x, local] + x_ref[y * 2 + x, rs]
            sw = pltpu.make_async_remote_copy(
                src_ref=swap_buf.at[0, d, local], dst_ref=swap_buf.at[1, d, local],
                send_sem=swap_sems.at[0, d, c], recv_sem=swap_sems.at[1, d, c],
                device_id={axis: partner}, device_id_type=MESH)
            sw.start()
            swaps.append((d, c, sw))
    for d, c, sw in swaps:
        rs = pl.ds(d * half + c * part, part)
        sw.wait_recv()
        out_ref[rs] = out_ref[rs] + swap_buf[1, d, pl.ds(c * part, part)]
    for d, c, sw in swaps:
        sw.wait_send()
    for cp in copies.values():
        cp.wait_send()


def ring_sum(partial, axis, outer, cid, chunks=4):
    count, rows, width = partial.shape
    half = rows // 2
    return pl.pallas_call(
        functools.partial(_ring_sum_kernel, axis, outer, chunks),
        out_shape=jax.ShapeDtypeStruct((rows, width), jnp.float32),
        in_specs=[pl.BlockSpec(memory_space=pltpu.VMEM)],
        out_specs=pl.BlockSpec(memory_space=pltpu.VMEM),
        scratch_shapes=[
            pltpu.VMEM((2, outer, 2, half, width), jnp.float32),
            pltpu.VMEM((2, outer, 2, half, width), jnp.float32),
            pltpu.VMEM((2, 2, half, width), jnp.float32),
            pltpu.SemaphoreType.DMA((2, outer, chunks)),
            pltpu.SemaphoreType.DMA((2, outer, chunks)),
            pltpu.SemaphoreType.DMA((2, 2, chunks)),
        ],
        compiler_params=pltpu.CompilerParams(collective_id=cid, has_side_effects=True, vmem_limit_bytes=60 * 1024 * 1024),
    )(partial)


def per_device(
    forward_acts, backward_grad, stored_gate, stored_up, gate_weight, up_weight, down_weight
):
    n_pipe = lax.axis_size("pipe")
    n_tensor = lax.axis_size("tensor")
    hidden_width = gate_weight.shape[1]
    model_width = forward_acts.shape[1]
    contract_last = (((1,), (1,)), ((), ()))

    whole_acts, whole_grad = ring_gather(
        forward_acts, backward_grad, "tensor", 2, n_tensor // 2, True, 0
    )

    gate_part = jnp.dot(whole_acts, gate_weight, preferred_element_type=jnp.float32)
    up_part = jnp.dot(whole_acts, up_weight, preferred_element_type=jnp.float32)
    grad_part = lax.dot_general(
        whole_grad, down_weight, contract_last, preferred_element_type=jnp.float32
    )
    partials = jnp.concatenate([gate_part, up_part, grad_part], axis=1)
    summed = ring_sum(
        partials.reshape((n_pipe, partials.shape[0] // n_pipe, partials.shape[1])),
        "pipe",
        n_pipe // 2,
        1,
    )
    gate_pre = summed[:, :hidden_width]
    up_pre = summed[:, hidden_width : 2 * hidden_width]
    hidden_grad = summed[:, 2 * hidden_width :]
    hidden_part = (jax.nn.silu(gate_pre) * up_pre).astype(jnp.bfloat16)
    local_slopes = make_slopes(hidden_grad, stored_gate, stored_up)

    rows = gather_rows(jnp.concatenate([hidden_part, local_slopes], axis=1), "pipe", n_pipe)
    hidden = rows[:, :hidden_width]
    gate_slopes = rows[:, hidden_width : 2 * hidden_width]
    up_slopes = rows[:, 2 * hidden_width :]

    out_part = jnp.dot(hidden, down_weight, preferred_element_type=jnp.float32)
    in_part = lax.dot_general(
        gate_slopes, gate_weight, contract_last, preferred_element_type=jnp.float32
    ) + lax.dot_general(up_slopes, up_weight, contract_last, preferred_element_type=jnp.float32)
    finished = scatter_sum_rows(
        jnp.concatenate([out_part, in_part], axis=1), "tensor", n_tensor, TENSOR_LINK
    ).astype(jnp.bfloat16)
    return (finished[:, :model_width], finished[:, model_width:])


def solution(mesh):
    in_specs = (
        P(("dp", "tensor"), "pipe"),
        P(("dp", "tensor"), "pipe"),
        P(("dp", "pipe"), "tensor"),
        P(("dp", "pipe"), "tensor"),
        P("pipe", "tensor"),
        P("pipe", "tensor"),
        P("tensor", "pipe"),
    )
    out_specs = (P(("dp", "tensor"), "pipe"), P(("dp", "tensor"), "pipe"))
    return jax.shard_map(
        per_device, mesh=mesh, in_specs=in_specs, out_specs=out_specs, check_vma=False
    )
```

```python
import functools

import jax
import jax.numpy as jnp
from jax import lax
from jax.experimental import pallas as pl
from jax.experimental.pallas import tpu as pltpu
from jax.sharding import PartitionSpec as P

PIPE_LINK = jnp.float32
TENSOR_LINK = jnp.bfloat16
MESH = pl.DeviceIdType.MESH


def make_slopes(hidden_grad, gate_vals, up_vals):
    gate_wide = gate_vals.astype(jnp.float32)
    up_wide = up_vals.astype(jnp.float32)
    sigma = jax.nn.sigmoid(gate_wide)
    gate_slope = (hidden_grad * up_wide * sigma * (1.0 + gate_wide * (1.0 - sigma))).astype(
        jnp.bfloat16
    )
    up_slope = (hidden_grad * gate_wide * sigma).astype(jnp.bfloat16)
    return jnp.concatenate([gate_slope, up_slope], axis=1)


def gather_rows(block, axis, count):
    sent = jnp.broadcast_to(block[None], (count,) + block.shape)
    got = lax.all_to_all(sent, axis, 0, 0, tiled=False)
    return got.reshape((count * block.shape[0],) + block.shape[1:])


def scatter_sum_rows(partial, axis, count, link_dtype):
    rows = partial.shape[0] // count
    sent = partial.reshape((count, rows) + partial.shape[1:]).astype(link_dtype)
    got = lax.all_to_all(sent, axis, 0, 0, tiled=False)
    return got.astype(jnp.float32).sum(axis=0)


def _ring_gather_kernel(axis, outer, inner, ring_on_inner, halves, first_in, second_in, first_ref, second_ref, send_sems, recv_sems, swap_sems, local_sems):
    me = lax.axis_index(axis)
    o = me // inner
    i = me % inner
    if ring_on_inner:
        ring = inner
        pos, other = i, o
        def at(p, q):
            return q * inner + p
    else:
        ring = outer
        pos, other = o, i
        def at(p, q):
            return p * inner + q
    partner = at(pos, 1 - other)
    up = at(lax.rem(pos + 1, ring), other)
    down = at(lax.rem(pos + ring - 1, ring), other)
    ins = (first_in, second_in)
    rows = first_in.shape[0]
    part = rows // halves
    steps = (ring // 2, ring // 2)

    def carries(d, step, r):
        if ring % 2 == 1 or step < ring // 2:
            return True
        return (r < halves // 2) == (d == 0)

    barrier = pltpu.get_barrier_semaphore()
    for peer in (partner, up, down):
        pl.semaphore_signal(barrier, inc=1, device_id={axis: peer}, device_id_type=MESH)
    pl.semaphore_wait(barrier, 3)

    outs = (first_ref, second_ref)
    locals_ = []
    swaps = []
    for a in range(2):
        c = pltpu.make_async_copy(ins[a], outs[a].at[other, pos], local_sems.at[a])
        c.start()
        locals_.append(c)
        s = pltpu.make_async_remote_copy(
            src_ref=ins[a], dst_ref=outs[a].at[other, pos],
            send_sem=swap_sems.at[0, a], recv_sem=swap_sems.at[1, a],
            device_id={axis: partner}, device_id_type=MESH)
        s.start()
        swaps.append(s)

    targets = (up, down)
    copies = {}

    def chunk_copy(d, step, which, r, a):
        slot = lax.rem(pos - step + 1 + ring, ring) if d == 0 else lax.rem(pos + step - 1, ring)
        half = other if which == 0 else 1 - other
        rs = pl.ds(r * part, part)
        if step == 1 and which == 0:
            src = ins[a].at[rs]
        else:
            src = outs[a].at[half, slot, rs]
        k = (((d * ring + step - 1) * 2 + which) * halves + r) * 2 + a
        return pltpu.make_async_remote_copy(
            src_ref=src, dst_ref=outs[a].at[half, slot, rs],
            send_sem=send_sems.at[k], recv_sem=recv_sems.at[k],
            device_id={axis: targets[d]}, device_id_type=MESH)

    last = {}
    for step in range(1, steps[0] + 1):
        for which in range(2):
            if step == 1 and which == 1:
                for s in swaps:
                    s.wait_recv()
            for r in range(halves):
                for a in range(2):
                    for d in range(2):
                        if not carries(d, step, r):
                            continue
                        if step > 1:
                            last[(d, which, r, a)].wait_recv()
                        c = chunk_copy(d, step, which, r, a)
                        c.start()
                        copies[(d, step, which, r, a)] = c
                        last[(d, which, r, a)] = c
    for c in last.values():
        c.wait_recv()
    for c in locals_:
        c.wait()
    for s in swaps:
        s.wait_send()
    for c in copies.values():
        c.wait_send()


def ring_gather(first, second, axis, outer, inner, ring_on_inner, cid, halves=2):
    rows, width = first.shape
    ring = inner if ring_on_inner else outer
    shape = (2, ring, rows, width)
    n_copies = 2 * ring * 2 * halves * 2
    f, s = pl.pallas_call(
        functools.partial(_ring_gather_kernel, axis, outer, inner, ring_on_inner, halves),
        out_shape=(jax.ShapeDtypeStruct(shape, first.dtype), jax.ShapeDtypeStruct(shape, second.dtype)),
        in_specs=[pl.BlockSpec(memory_space=pltpu.VMEM)] * 2,
        out_specs=(pl.BlockSpec(memory_space=pltpu.VMEM), pl.BlockSpec(memory_space=pltpu.VMEM)),
        scratch_shapes=[
            pltpu.SemaphoreType.DMA((n_copies,)),
            pltpu.SemaphoreType.DMA((n_copies,)),
            pltpu.SemaphoreType.DMA((2, 2)),
            pltpu.SemaphoreType.DMA((2,)),
        ],
        compiler_params=pltpu.CompilerParams(collective_id=cid, has_side_effects=True),
    )(first, second)
    if ring_on_inner:
        return f.reshape(2 * ring * rows, width), s.reshape(2 * ring * rows, width)
    return (f.transpose(1, 0, 2, 3).reshape(2 * ring * rows, width),
            s.transpose(1, 0, 2, 3).reshape(2 * ring * rows, width))


def _ring_sum_kernel(axis, outer, chunks, x_ref, out_ref, send_buf, recv_buf, swap_buf, send_sems, recv_sems, swap_sems):
    me = lax.axis_index(axis)
    y = me // 2
    x = me % 2
    ring = outer
    up = lax.rem(y + 1, ring) * 2 + x
    down = lax.rem(y + ring - 1, ring) * 2 + x
    partner = y * 2 + 1 - x
    rows = x_ref.shape[1]
    half = rows // 2
    part = half // chunks

    barrier = pltpu.get_barrier_semaphore()
    for peer in (partner, up, down):
        pl.semaphore_signal(barrier, inc=1, device_id={axis: peer}, device_id_type=MESH)
    pl.semaphore_wait(barrier, 3)

    targets = (up, down)
    copies = {}

    def dest(d, step):
        return lax.rem(y - step + ring, ring) if d == 0 else lax.rem(y + step, ring)

    for step in range(1, ring):
        for c in range(chunks):
            for d in range(2):
                rs = pl.ds(d * half + c * part, part)
                blocks = pl.ds(dest(d, step) * 2, 2)
                if step == 1:
                    src = x_ref.at[blocks, rs]
                else:
                    copies[(d, step - 1, c)].wait_recv()
                    send_buf[d, step, :, pl.ds(c * part, part)] = (
                        recv_buf[d, step - 1, :, pl.ds(c * part, part)] + x_ref[blocks, rs]
                    )
                    src = send_buf.at[d, step, :, pl.ds(c * part, part)]
                cp = pltpu.make_async_remote_copy(
                    src_ref=src, dst_ref=recv_buf.at[d, step, :, pl.ds(c * part, part)],
                    send_sem=send_sems.at[d, step, c], recv_sem=recv_sems.at[d, step, c],
                    device_id={axis: targets[d]}, device_id_type=MESH)
                cp.start()
                copies[(d, step, c)] = cp
    swaps = []
    for c in range(chunks):
        for d in range(2):
            rs = pl.ds(d * half + c * part, part)
            local = pl.ds(c * part, part)
            copies[(d, ring - 1, c)].wait_recv()
            swap_buf[0, d, local] = recv_buf[d, ring - 1, 1 - x, local] + x_ref[y * 2 + 1 - x, rs]
            out_ref[rs] = recv_buf[d, ring - 1, x, local] + x_ref[y * 2 + x, rs]
            sw = pltpu.make_async_remote_copy(
                src_ref=swap_buf.at[0, d, local], dst_ref=swap_buf.at[1, d, local],
                send_sem=swap_sems.at[0, d, c], recv_sem=swap_sems.at[1, d, c],
                device_id={axis: partner}, device_id_type=MESH)
            sw.start()
            swaps.append((d, c, sw))
    for d, c, sw in swaps:
        rs = pl.ds(d * half + c * part, part)
        sw.wait_recv()
        out_ref[rs] = out_ref[rs] + swap_buf[1, d, pl.ds(c * part, part)]
    for d, c, sw in swaps:
        sw.wait_send()
    for cp in copies.values():
        cp.wait_send()


def ring_sum(partial, axis, outer, cid, chunks=4):
    count, rows, width = partial.shape
    half = rows // 2
    return pl.pallas_call(
        functools.partial(_ring_sum_kernel, axis, outer, chunks),
        out_shape=jax.ShapeDtypeStruct((rows, width), jnp.float32),
        in_specs=[pl.BlockSpec(memory_space=pltpu.VMEM)],
        out_specs=pl.BlockSpec(memory_space=pltpu.VMEM),
        scratch_shapes=[
            pltpu.VMEM((2, outer, 2, half, width), jnp.float32),
            pltpu.VMEM((2, outer, 2, half, width), jnp.float32),
            pltpu.VMEM((2, 2, half, width), jnp.float32),
            pltpu.SemaphoreType.DMA((2, outer, chunks)),
            pltpu.SemaphoreType.DMA((2, outer, chunks)),
            pltpu.SemaphoreType.DMA((2, 2, chunks)),
        ],
        compiler_params=pltpu.CompilerParams(collective_id=cid, has_side_effects=True, vmem_limit_bytes=60 * 1024 * 1024),
    )(partial)


def per_device(
    forward_acts, backward_grad, stored_gate, stored_up, gate_weight, up_weight, down_weight
):
    n_pipe = lax.axis_size("pipe")
    n_tensor = lax.axis_size("tensor")
    hidden_width = gate_weight.shape[1]
    model_width = forward_acts.shape[1]
    contract_last = (((1,), (1,)), ((), ()))

    whole_acts, whole_grad = ring_gather(
        forward_acts, backward_grad, "tensor", 2, n_tensor // 2, True, 0
    )

    gate_part = jnp.dot(whole_acts, gate_weight, preferred_element_type=jnp.float32)
    up_part = jnp.dot(whole_acts, up_weight, preferred_element_type=jnp.float32)
    grad_part = lax.dot_general(
        whole_grad, down_weight, contract_last, preferred_element_type=jnp.float32
    )
    partials = jnp.concatenate([gate_part, up_part, grad_part], axis=1)
    summed = ring_sum(
        partials.reshape((n_pipe, partials.shape[0] // n_pipe, partials.shape[1])),
        "pipe",
        n_pipe // 2,
        1,
    )
    gate_pre = summed[:, :hidden_width]
    up_pre = summed[:, hidden_width : 2 * hidden_width]
    hidden_grad = summed[:, 2 * hidden_width :]
    hidden_part = (jax.nn.silu(gate_pre) * up_pre).astype(jnp.bfloat16)
    local_slopes = make_slopes(hidden_grad, stored_gate, stored_up)

    rows = gather_rows(jnp.concatenate([hidden_part, local_slopes], axis=1), "pipe", n_pipe)
    hidden = rows[:, :hidden_width]
    gate_slopes = rows[:, hidden_width : 2 * hidden_width]
    up_slopes = rows[:, 2 * hidden_width :]

    out_part = jnp.dot(hidden, down_weight, preferred_element_type=jnp.float32)
    in_part = lax.dot_general(
        gate_slopes, gate_weight, contract_last, preferred_element_type=jnp.float32
    ) + lax.dot_general(up_slopes, up_weight, contract_last, preferred_element_type=jnp.float32)
    finished = scatter_sum_rows(
        jnp.concatenate([out_part, in_part], axis=1), "tensor", n_tensor, TENSOR_LINK
    ).astype(jnp.bfloat16)
    return (finished[:, :model_width], finished[:, model_width:])


def solution(mesh):
    in_specs = (
        P(("dp", "tensor"), "pipe"),
        P(("dp", "tensor"), "pipe"),
        P(("dp", "pipe"), "tensor"),
        P(("dp", "pipe"), "tensor"),
        P("pipe", "tensor"),
        P("pipe", "tensor"),
        P("tensor", "pipe"),
    )
    out_specs = (P(("dp", "tensor"), "pipe"), P(("dp", "tensor"), "pipe"))
    return jax.shard_map(
        per_device, mesh=mesh, in_specs=in_specs, out_specs=out_specs, check_vma=False
    )
```

```python
import functools

import jax
import jax.numpy as jnp
from jax import lax
from jax.experimental import pallas as pl
from jax.experimental.pallas import tpu as pltpu
from jax.sharding import PartitionSpec as P

PIPE_LINK = jnp.float32
TENSOR_LINK = jnp.bfloat16
MESH = pl.DeviceIdType.MESH


def make_slopes(hidden_grad, gate_vals, up_vals):
    gate_wide = gate_vals.astype(jnp.float32)
    up_wide = up_vals.astype(jnp.float32)
    sigma = jax.nn.sigmoid(gate_wide)
    gate_slope = (hidden_grad * up_wide * sigma * (1.0 + gate_wide * (1.0 - sigma))).astype(
        jnp.bfloat16
    )
    up_slope = (hidden_grad * gate_wide * sigma).astype(jnp.bfloat16)
    return jnp.concatenate([gate_slope, up_slope], axis=1)


def scatter_sum_rows(partial, axis, count, link_dtype):
    rows = partial.shape[0] // count
    sent = partial.reshape((count, rows) + partial.shape[1:]).astype(link_dtype)
    got = lax.all_to_all(sent, axis, 0, 0, tiled=False)
    return got.astype(jnp.float32).sum(axis=0)


def _ring_gather_kernel(axis, outer, inner, ring_on_inner, halves, first_in, second_in, first_ref, second_ref, send_sems, recv_sems, swap_sems, local_sems):
    me = lax.axis_index(axis)
    o = me // inner
    i = me % inner
    if ring_on_inner:
        ring = inner
        pos, other = i, o
        def at(p, q):
            return q * inner + p
    else:
        ring = outer
        pos, other = o, i
        def at(p, q):
            return p * inner + q
    partner = at(pos, 1 - other)
    up = at(lax.rem(pos + 1, ring), other)
    down = at(lax.rem(pos + ring - 1, ring), other)
    ins = (first_in, second_in)
    rows = first_in.shape[0]
    part = rows // halves
    steps = (ring // 2, ring // 2)

    def carries(d, step, r):
        if ring % 2 == 1 or step < ring // 2:
            return True
        return (r < halves // 2) == (d == 0)

    barrier = pltpu.get_barrier_semaphore()
    for peer in (partner, up, down):
        pl.semaphore_signal(barrier, inc=1, device_id={axis: peer}, device_id_type=MESH)
    pl.semaphore_wait(barrier, 3)

    outs = (first_ref, second_ref)
    locals_ = []
    swaps = []
    for a in range(2):
        c = pltpu.make_async_copy(ins[a], outs[a].at[other, pos], local_sems.at[a])
        c.start()
        locals_.append(c)
        s = pltpu.make_async_remote_copy(
            src_ref=ins[a], dst_ref=outs[a].at[other, pos],
            send_sem=swap_sems.at[0, a], recv_sem=swap_sems.at[1, a],
            device_id={axis: partner}, device_id_type=MESH)
        s.start()
        swaps.append(s)

    targets = (up, down)
    copies = {}

    def chunk_copy(d, step, which, r, a):
        slot = lax.rem(pos - step + 1 + ring, ring) if d == 0 else lax.rem(pos + step - 1, ring)
        half = other if which == 0 else 1 - other
        rs = pl.ds(r * part, part)
        if step == 1 and which == 0:
            src = ins[a].at[rs]
        else:
            src = outs[a].at[half, slot, rs]
        k = (((d * ring + step - 1) * 2 + which) * halves + r) * 2 + a
        return pltpu.make_async_remote_copy(
            src_ref=src, dst_ref=outs[a].at[half, slot, rs],
            send_sem=send_sems.at[k], recv_sem=recv_sems.at[k],
            device_id={axis: targets[d]}, device_id_type=MESH)

    last = {}
    for step in range(1, steps[0] + 1):
        for which in range(2):
            if step == 1 and which == 1:
                for s in swaps:
                    s.wait_recv()
            for r in range(halves):
                for a in range(2):
                    for d in range(2):
                        if not carries(d, step, r):
                            continue
                        if step > 1:
                            last[(d, which, r, a)].wait_recv()
                        c = chunk_copy(d, step, which, r, a)
                        c.start()
                        copies[(d, step, which, r, a)] = c
                        last[(d, which, r, a)] = c
    for c in last.values():
        c.wait_recv()
    for c in locals_:
        c.wait()
    for s in swaps:
        s.wait_send()
    for c in copies.values():
        c.wait_send()


def ring_gather(first, second, axis, outer, inner, ring_on_inner, cid, halves=2):
    rows, width = first.shape
    ring = inner if ring_on_inner else outer
    shape = (2, ring, rows, width)
    n_copies = 2 * ring * 2 * halves * 2
    f, s = pl.pallas_call(
        functools.partial(_ring_gather_kernel, axis, outer, inner, ring_on_inner, halves),
        out_shape=(jax.ShapeDtypeStruct(shape, first.dtype), jax.ShapeDtypeStruct(shape, second.dtype)),
        in_specs=[pl.BlockSpec(memory_space=pltpu.VMEM)] * 2,
        out_specs=(pl.BlockSpec(memory_space=pltpu.VMEM), pl.BlockSpec(memory_space=pltpu.VMEM)),
        scratch_shapes=[
            pltpu.SemaphoreType.DMA((n_copies,)),
            pltpu.SemaphoreType.DMA((n_copies,)),
            pltpu.SemaphoreType.DMA((2, 2)),
            pltpu.SemaphoreType.DMA((2,)),
        ],
        compiler_params=pltpu.CompilerParams(collective_id=cid, has_side_effects=True),
    )(first, second)
    if ring_on_inner:
        return f.reshape(2 * ring * rows, width), s.reshape(2 * ring * rows, width)
    return (f.transpose(1, 0, 2, 3).reshape(2 * ring * rows, width),
            s.transpose(1, 0, 2, 3).reshape(2 * ring * rows, width))


def _ring_sum_kernel(axis, outer, chunks, x_ref, out_ref, send_buf, recv_buf, swap_buf, send_sems, recv_sems, swap_sems):
    me = lax.axis_index(axis)
    y = me // 2
    x = me % 2
    ring = outer
    up = lax.rem(y + 1, ring) * 2 + x
    down = lax.rem(y + ring - 1, ring) * 2 + x
    partner = y * 2 + 1 - x
    rows = x_ref.shape[1]
    half = rows // 2
    part = half // chunks

    barrier = pltpu.get_barrier_semaphore()
    for peer in (partner, up, down):
        pl.semaphore_signal(barrier, inc=1, device_id={axis: peer}, device_id_type=MESH)
    pl.semaphore_wait(barrier, 3)

    targets = (up, down)
    copies = {}

    def dest(d, step):
        return lax.rem(y - step + ring, ring) if d == 0 else lax.rem(y + step, ring)

    for step in range(1, ring):
        for c in range(chunks):
            for d in range(2):
                rs = pl.ds(d * half + c * part, part)
                blocks = pl.ds(dest(d, step) * 2, 2)
                if step == 1:
                    src = x_ref.at[blocks, rs]
                else:
                    copies[(d, step - 1, c)].wait_recv()
                    send_buf[d, step, :, pl.ds(c * part, part)] = (
                        recv_buf[d, step - 1, :, pl.ds(c * part, part)] + x_ref[blocks, rs]
                    )
                    src = send_buf.at[d, step, :, pl.ds(c * part, part)]
                cp = pltpu.make_async_remote_copy(
                    src_ref=src, dst_ref=recv_buf.at[d, step, :, pl.ds(c * part, part)],
                    send_sem=send_sems.at[d, step, c], recv_sem=recv_sems.at[d, step, c],
                    device_id={axis: targets[d]}, device_id_type=MESH)
                cp.start()
                copies[(d, step, c)] = cp
    swaps = []
    for c in range(chunks):
        for d in range(2):
            rs = pl.ds(d * half + c * part, part)
            local = pl.ds(c * part, part)
            copies[(d, ring - 1, c)].wait_recv()
            swap_buf[0, d, local] = recv_buf[d, ring - 1, 1 - x, local] + x_ref[y * 2 + 1 - x, rs]
            out_ref[rs] = recv_buf[d, ring - 1, x, local] + x_ref[y * 2 + x, rs]
            sw = pltpu.make_async_remote_copy(
                src_ref=swap_buf.at[0, d, local], dst_ref=swap_buf.at[1, d, local],
                send_sem=swap_sems.at[0, d, c], recv_sem=swap_sems.at[1, d, c],
                device_id={axis: partner}, device_id_type=MESH)
            sw.start()
            swaps.append((d, c, sw))
    for d, c, sw in swaps:
        rs = pl.ds(d * half + c * part, part)
        sw.wait_recv()
        out_ref[rs] = out_ref[rs] + swap_buf[1, d, pl.ds(c * part, part)]
    for d, c, sw in swaps:
        sw.wait_send()
    for cp in copies.values():
        cp.wait_send()


def ring_sum(partial, axis, outer, cid, chunks=4):
    count, rows, width = partial.shape
    half = rows // 2
    return pl.pallas_call(
        functools.partial(_ring_sum_kernel, axis, outer, chunks),
        out_shape=jax.ShapeDtypeStruct((rows, width), jnp.float32),
        in_specs=[pl.BlockSpec(memory_space=pltpu.VMEM)],
        out_specs=pl.BlockSpec(memory_space=pltpu.VMEM),
        scratch_shapes=[
            pltpu.VMEM((2, outer, 2, half, width), jnp.float32),
            pltpu.VMEM((2, outer, 2, half, width), jnp.float32),
            pltpu.VMEM((2, 2, half, width), jnp.float32),
            pltpu.SemaphoreType.DMA((2, outer, chunks)),
            pltpu.SemaphoreType.DMA((2, outer, chunks)),
            pltpu.SemaphoreType.DMA((2, 2, chunks)),
        ],
        compiler_params=pltpu.CompilerParams(collective_id=cid, has_side_effects=True, vmem_limit_bytes=60 * 1024 * 1024),
    )(partial)


def per_device(
    forward_acts, backward_grad, stored_gate, stored_up, gate_weight, up_weight, down_weight
):
    n_pipe = lax.axis_size("pipe")
    n_tensor = lax.axis_size("tensor")
    hidden_width = gate_weight.shape[1]
    model_width = forward_acts.shape[1]
    contract_last = (((1,), (1,)), ((), ()))

    whole_acts, whole_grad = ring_gather(
        forward_acts, backward_grad, "tensor", 2, n_tensor // 2, True, 0
    )

    gate_part = jnp.dot(whole_acts, gate_weight, preferred_element_type=jnp.float32)
    up_part = jnp.dot(whole_acts, up_weight, preferred_element_type=jnp.float32)
    grad_part = lax.dot_general(
        whole_grad, down_weight, contract_last, preferred_element_type=jnp.float32
    )
    partials = jnp.concatenate([gate_part, up_part, grad_part], axis=1)
    summed = ring_sum(
        partials.reshape((n_pipe, partials.shape[0] // n_pipe, partials.shape[1])),
        "pipe",
        n_pipe // 2,
        1,
    )
    gate_pre = summed[:, :hidden_width]
    up_pre = summed[:, hidden_width : 2 * hidden_width]
    hidden_grad = summed[:, 2 * hidden_width :]
    hidden_part = (jax.nn.silu(gate_pre) * up_pre).astype(jnp.bfloat16)
    local_slopes = make_slopes(hidden_grad, stored_gate, stored_up)

    local_rows = jnp.concatenate([hidden_part, local_slopes], axis=1)
    split = local_rows.shape[1] // 2
    rows_low, rows_high = ring_gather(
        local_rows[:, :split], local_rows[:, split:], "pipe", n_pipe // 2, 2, False, 2
    )
    rows = jnp.concatenate([rows_low, rows_high], axis=1)
    hidden = rows[:, :hidden_width]
    gate_slopes = rows[:, hidden_width : 2 * hidden_width]
    up_slopes = rows[:, 2 * hidden_width :]

    out_part = jnp.dot(hidden, down_weight, preferred_element_type=jnp.float32)
    in_part = lax.dot_general(
        gate_slopes, gate_weight, contract_last, preferred_element_type=jnp.float32
    ) + lax.dot_general(up_slopes, up_weight, contract_last, preferred_element_type=jnp.float32)
    finished = scatter_sum_rows(
        jnp.concatenate([out_part, in_part], axis=1), "tensor", n_tensor, TENSOR_LINK
    ).astype(jnp.bfloat16)
    return (finished[:, :model_width], finished[:, model_width:])


def solution(mesh):
    in_specs = (
        P(("dp", "tensor"), "pipe"),
        P(("dp", "tensor"), "pipe"),
        P(("dp", "pipe"), "tensor"),
        P(("dp", "pipe"), "tensor"),
        P("pipe", "tensor"),
        P("pipe", "tensor"),
        P("tensor", "pipe"),
    )
    out_specs = (P(("dp", "tensor"), "pipe"), P(("dp", "tensor"), "pipe"))
    return jax.shard_map(
        per_device, mesh=mesh, in_specs=in_specs, out_specs=out_specs, check_vma=False
    )
```

```python
import functools

import jax
import jax.numpy as jnp
from jax import lax
from jax.experimental import pallas as pl
from jax.experimental.pallas import tpu as pltpu
from jax.sharding import PartitionSpec as P

PIPE_LINK = jnp.float32
TENSOR_LINK = jnp.bfloat16
MESH = pl.DeviceIdType.MESH


def make_slopes(hidden_grad, gate_vals, up_vals):
    gate_wide = gate_vals.astype(jnp.float32)
    up_wide = up_vals.astype(jnp.float32)
    sigma = jax.nn.sigmoid(gate_wide)
    gate_slope = (hidden_grad * up_wide * sigma * (1.0 + gate_wide * (1.0 - sigma))).astype(
        jnp.bfloat16
    )
    up_slope = (hidden_grad * gate_wide * sigma).astype(jnp.bfloat16)
    return jnp.concatenate([gate_slope, up_slope], axis=1)


def scatter_sum_rows(partial, axis, count, link_dtype):
    rows = partial.shape[0] // count
    sent = partial.reshape((count, rows) + partial.shape[1:]).astype(link_dtype)
    got = lax.all_to_all(sent, axis, 0, 0, tiled=False)
    return got.astype(jnp.float32).sum(axis=0)


def _ring_gather_kernel(axis, outer, inner, ring_on_inner, halves, first_in, second_in, first_ref, second_ref, send_sems, recv_sems, swap_sems, local_sems):
    me = lax.axis_index(axis)
    o = me // inner
    i = me % inner
    if ring_on_inner:
        ring = inner
        pos, other = i, o
        def at(p, q):
            return q * inner + p
    else:
        ring = outer
        pos, other = o, i
        def at(p, q):
            return p * inner + q
    partner = at(pos, 1 - other)
    up = at(lax.rem(pos + 1, ring), other)
    down = at(lax.rem(pos + ring - 1, ring), other)
    ins = (first_in, second_in)
    rows = first_in.shape[0]
    part = rows // halves
    steps = (ring // 2, ring // 2)

    def carries(d, step, r):
        if ring % 2 == 1 or step < ring // 2:
            return True
        return (r < halves // 2) == (d == 0)

    barrier = pltpu.get_barrier_semaphore()
    for peer in (partner, up, down):
        pl.semaphore_signal(barrier, inc=1, device_id={axis: peer}, device_id_type=MESH)
    pl.semaphore_wait(barrier, 3)

    outs = (first_ref, second_ref)

    def slot_of(a, half, slot):
        return outs[a].at[half, slot] if ring_on_inner else outs[a].at[slot, half]
    locals_ = []
    swaps = []
    for a in range(2):
        c = pltpu.make_async_copy(ins[a], slot_of(a, other, pos), local_sems.at[a])
        c.start()
        locals_.append(c)
        s = pltpu.make_async_remote_copy(
            src_ref=ins[a], dst_ref=slot_of(a, other, pos),
            send_sem=swap_sems.at[0, a], recv_sem=swap_sems.at[1, a],
            device_id={axis: partner}, device_id_type=MESH)
        s.start()
        swaps.append(s)

    targets = (up, down)
    copies = {}

    def chunk_copy(d, step, which, r, a):
        slot = lax.rem(pos - step + 1 + ring, ring) if d == 0 else lax.rem(pos + step - 1, ring)
        half = other if which == 0 else 1 - other
        rs = pl.ds(r * part, part)
        if step == 1 and which == 0:
            src = ins[a].at[rs]
        else:
            src = slot_of(a, half, slot).at[rs]
        k = (((d * ring + step - 1) * 2 + which) * halves + r) * 2 + a
        return pltpu.make_async_remote_copy(
            src_ref=src, dst_ref=slot_of(a, half, slot).at[rs],
            send_sem=send_sems.at[k], recv_sem=recv_sems.at[k],
            device_id={axis: targets[d]}, device_id_type=MESH)

    last = {}
    for step in range(1, steps[0] + 1):
        for which in range(2):
            if step == 1 and which == 1:
                for s in swaps:
                    s.wait_recv()
            for r in range(halves):
                for a in range(2):
                    for d in range(2):
                        if not carries(d, step, r):
                            continue
                        if step > 1:
                            last[(d, which, r, a)].wait_recv()
                        c = chunk_copy(d, step, which, r, a)
                        c.start()
                        copies[(d, step, which, r, a)] = c
                        last[(d, which, r, a)] = c
    for c in last.values():
        c.wait_recv()
    for c in locals_:
        c.wait()
    for s in swaps:
        s.wait_send()
    for c in copies.values():
        c.wait_send()


def ring_gather(first, second, axis, outer, inner, ring_on_inner, cid, halves=2):
    rows, width = first.shape
    ring = inner if ring_on_inner else outer
    shape = (2, ring, rows, width) if ring_on_inner else (ring, 2, rows, width)
    n_copies = 2 * ring * 2 * halves * 2
    f, s = pl.pallas_call(
        functools.partial(_ring_gather_kernel, axis, outer, inner, ring_on_inner, halves),
        out_shape=(jax.ShapeDtypeStruct(shape, first.dtype), jax.ShapeDtypeStruct(shape, second.dtype)),
        in_specs=[pl.BlockSpec(memory_space=pltpu.VMEM)] * 2,
        out_specs=(pl.BlockSpec(memory_space=pltpu.VMEM), pl.BlockSpec(memory_space=pltpu.VMEM)),
        scratch_shapes=[
            pltpu.SemaphoreType.DMA((n_copies,)),
            pltpu.SemaphoreType.DMA((n_copies,)),
            pltpu.SemaphoreType.DMA((2, 2)),
            pltpu.SemaphoreType.DMA((2,)),
        ],
        compiler_params=pltpu.CompilerParams(collective_id=cid, has_side_effects=True),
    )(first, second)
    return f.reshape(2 * ring * rows, width), s.reshape(2 * ring * rows, width)


def _ring_sum_kernel(axis, outer, chunks, x_ref, out_ref, send_buf, recv_buf, swap_buf, send_sems, recv_sems, swap_sems):
    me = lax.axis_index(axis)
    y = me // 2
    x = me % 2
    ring = outer
    up = lax.rem(y + 1, ring) * 2 + x
    down = lax.rem(y + ring - 1, ring) * 2 + x
    partner = y * 2 + 1 - x
    rows = x_ref.shape[1]
    half = rows // 2
    part = half // chunks

    barrier = pltpu.get_barrier_semaphore()
    for peer in (partner, up, down):
        pl.semaphore_signal(barrier, inc=1, device_id={axis: peer}, device_id_type=MESH)
    pl.semaphore_wait(barrier, 3)

    targets = (up, down)
    copies = {}

    def dest(d, step):
        return lax.rem(y - step + ring, ring) if d == 0 else lax.rem(y + step, ring)

    for step in range(1, ring):
        for c in range(chunks):
            for d in range(2):
                rs = pl.ds(d * half + c * part, part)
                blocks = pl.ds(dest(d, step) * 2, 2)
                if step == 1:
                    src = x_ref.at[blocks, rs]
                else:
                    copies[(d, step - 1, c)].wait_recv()
                    send_buf[d, step, :, pl.ds(c * part, part)] = (
                        recv_buf[d, step - 1, :, pl.ds(c * part, part)] + x_ref[blocks, rs]
                    )
                    src = send_buf.at[d, step, :, pl.ds(c * part, part)]
                cp = pltpu.make_async_remote_copy(
                    src_ref=src, dst_ref=recv_buf.at[d, step, :, pl.ds(c * part, part)],
                    send_sem=send_sems.at[d, step, c], recv_sem=recv_sems.at[d, step, c],
                    device_id={axis: targets[d]}, device_id_type=MESH)
                cp.start()
                copies[(d, step, c)] = cp
    swaps = []
    for c in range(chunks):
        for d in range(2):
            rs = pl.ds(d * half + c * part, part)
            local = pl.ds(c * part, part)
            copies[(d, ring - 1, c)].wait_recv()
            swap_buf[0, d, local] = recv_buf[d, ring - 1, 1 - x, local] + x_ref[y * 2 + 1 - x, rs]
            out_ref[rs] = recv_buf[d, ring - 1, x, local] + x_ref[y * 2 + x, rs]
            sw = pltpu.make_async_remote_copy(
                src_ref=swap_buf.at[0, d, local], dst_ref=swap_buf.at[1, d, local],
                send_sem=swap_sems.at[0, d, c], recv_sem=swap_sems.at[1, d, c],
                device_id={axis: partner}, device_id_type=MESH)
            sw.start()
            swaps.append((d, c, sw))
    for d, c, sw in swaps:
        rs = pl.ds(d * half + c * part, part)
        sw.wait_recv()
        out_ref[rs] = out_ref[rs] + swap_buf[1, d, pl.ds(c * part, part)]
    for d, c, sw in swaps:
        sw.wait_send()
    for cp in copies.values():
        cp.wait_send()


def ring_sum(partial, axis, outer, cid, chunks=4):
    count, rows, width = partial.shape
    half = rows // 2
    return pl.pallas_call(
        functools.partial(_ring_sum_kernel, axis, outer, chunks),
        out_shape=jax.ShapeDtypeStruct((rows, width), jnp.float32),
        in_specs=[pl.BlockSpec(memory_space=pltpu.VMEM)],
        out_specs=pl.BlockSpec(memory_space=pltpu.VMEM),
        scratch_shapes=[
            pltpu.VMEM((2, outer, 2, half, width), jnp.float32),
            pltpu.VMEM((2, outer, 2, half, width), jnp.float32),
            pltpu.VMEM((2, 2, half, width), jnp.float32),
            pltpu.SemaphoreType.DMA((2, outer, chunks)),
            pltpu.SemaphoreType.DMA((2, outer, chunks)),
            pltpu.SemaphoreType.DMA((2, 2, chunks)),
        ],
        compiler_params=pltpu.CompilerParams(collective_id=cid, has_side_effects=True, vmem_limit_bytes=60 * 1024 * 1024),
    )(partial)


def per_device(
    forward_acts, backward_grad, stored_gate, stored_up, gate_weight, up_weight, down_weight
):
    n_pipe = lax.axis_size("pipe")
    n_tensor = lax.axis_size("tensor")
    hidden_width = gate_weight.shape[1]
    model_width = forward_acts.shape[1]
    contract_last = (((1,), (1,)), ((), ()))

    whole_acts, whole_grad = ring_gather(
        forward_acts, backward_grad, "tensor", 2, n_tensor // 2, True, 0
    )

    gate_part = jnp.dot(whole_acts, gate_weight, preferred_element_type=jnp.float32)
    up_part = jnp.dot(whole_acts, up_weight, preferred_element_type=jnp.float32)
    grad_part = lax.dot_general(
        whole_grad, down_weight, contract_last, preferred_element_type=jnp.float32
    )
    partials = jnp.concatenate([gate_part, up_part, grad_part], axis=1)
    summed = ring_sum(
        partials.reshape((n_pipe, partials.shape[0] // n_pipe, partials.shape[1])),
        "pipe",
        n_pipe // 2,
        1,
    )
    gate_pre = summed[:, :hidden_width]
    up_pre = summed[:, hidden_width : 2 * hidden_width]
    hidden_grad = summed[:, 2 * hidden_width :]
    hidden_part = (jax.nn.silu(gate_pre) * up_pre).astype(jnp.bfloat16)
    local_slopes = make_slopes(hidden_grad, stored_gate, stored_up)

    local_rows = jnp.concatenate([hidden_part, local_slopes], axis=1)
    split = local_rows.shape[1] // 2
    rows_low, rows_high = ring_gather(
        local_rows[:, :split], local_rows[:, split:], "pipe", n_pipe // 2, 2, False, 2
    )
    rows = jnp.concatenate([rows_low, rows_high], axis=1)
    hidden = rows[:, :hidden_width]
    gate_slopes = rows[:, hidden_width : 2 * hidden_width]
    up_slopes = rows[:, 2 * hidden_width :]

    out_part = jnp.dot(hidden, down_weight, preferred_element_type=jnp.float32)
    in_part = lax.dot_general(
        gate_slopes, gate_weight, contract_last, preferred_element_type=jnp.float32
    ) + lax.dot_general(up_slopes, up_weight, contract_last, preferred_element_type=jnp.float32)
    finished = scatter_sum_rows(
        jnp.concatenate([out_part, in_part], axis=1), "tensor", n_tensor, TENSOR_LINK
    ).astype(jnp.bfloat16)
    return (finished[:, :model_width], finished[:, model_width:])


def solution(mesh):
    in_specs = (
        P(("dp", "tensor"), "pipe"),
        P(("dp", "tensor"), "pipe"),
        P(("dp", "pipe"), "tensor"),
        P(("dp", "pipe"), "tensor"),
        P("pipe", "tensor"),
        P("pipe", "tensor"),
        P("tensor", "pipe"),
    )
    out_specs = (P(("dp", "tensor"), "pipe"), P(("dp", "tensor"), "pipe"))
    return jax.shard_map(
        per_device, mesh=mesh, in_specs=in_specs, out_specs=out_specs, check_vma=False
    )
```

```python
import functools

import jax
import jax.numpy as jnp
from jax import lax
from jax.experimental import pallas as pl
from jax.experimental.pallas import tpu as pltpu
from jax.sharding import PartitionSpec as P

PIPE_LINK = jnp.float32
TENSOR_LINK = jnp.bfloat16
MESH = pl.DeviceIdType.MESH


def make_slopes(hidden_grad, gate_vals, up_vals):
    gate_wide = gate_vals.astype(jnp.float32)
    up_wide = up_vals.astype(jnp.float32)
    sigma = jax.nn.sigmoid(gate_wide)
    gate_slope = (hidden_grad * up_wide * sigma * (1.0 + gate_wide * (1.0 - sigma))).astype(
        jnp.bfloat16
    )
    up_slope = (hidden_grad * gate_wide * sigma).astype(jnp.bfloat16)
    return gate_slope, up_slope


def scatter_sum_rows(partial, axis, count, link_dtype):
    rows = partial.shape[0] // count
    sent = partial.reshape((count, rows) + partial.shape[1:]).astype(link_dtype)
    got = lax.all_to_all(sent, axis, 0, 0, tiled=False)
    return got.astype(jnp.float32).sum(axis=0)


def _ring_gather_kernel(axis, outer, inner, ring_on_inner, halves, count, *refs):
    me = lax.axis_index(axis)
    o = me // inner
    i = me % inner
    if ring_on_inner:
        ring = inner
        pos, other = i, o
        def at(p, q):
            return q * inner + p
    else:
        ring = outer
        pos, other = o, i
        def at(p, q):
            return p * inner + q
    partner = at(pos, 1 - other)
    up = at(lax.rem(pos + 1, ring), other)
    down = at(lax.rem(pos + ring - 1, ring), other)
    ins = refs[:count]
    outs = refs[count:2 * count]
    send_sems, recv_sems, swap_sems, local_sems = refs[2 * count:]
    rows = ins[0].shape[0]
    part = rows // halves
    steps = (ring // 2, ring // 2)

    def carries(d, step, r):
        if ring % 2 == 1 or step < ring // 2:
            return True
        return (r < halves // 2) == (d == 0)

    barrier = pltpu.get_barrier_semaphore()
    for peer in (partner, up, down):
        pl.semaphore_signal(barrier, inc=1, device_id={axis: peer}, device_id_type=MESH)
    pl.semaphore_wait(barrier, 3)


    def slot_of(a, half, slot):
        return outs[a].at[half, slot] if ring_on_inner else outs[a].at[slot, half]
    locals_ = []
    swaps = []
    for a in range(count):
        c = pltpu.make_async_copy(ins[a], slot_of(a, other, pos), local_sems.at[a])
        c.start()
        locals_.append(c)
        s = pltpu.make_async_remote_copy(
            src_ref=ins[a], dst_ref=slot_of(a, other, pos),
            send_sem=swap_sems.at[0, a], recv_sem=swap_sems.at[1, a],
            device_id={axis: partner}, device_id_type=MESH)
        s.start()
        swaps.append(s)

    targets = (up, down)
    copies = {}

    def chunk_copy(d, step, which, r, a):
        slot = lax.rem(pos - step + 1 + ring, ring) if d == 0 else lax.rem(pos + step - 1, ring)
        half = other if which == 0 else 1 - other
        rs = pl.ds(r * part, part)
        if step == 1 and which == 0:
            src = ins[a].at[rs]
        else:
            src = slot_of(a, half, slot).at[rs]
        k = (((d * ring + step - 1) * 2 + which) * halves + r) * count + a
        return pltpu.make_async_remote_copy(
            src_ref=src, dst_ref=slot_of(a, half, slot).at[rs],
            send_sem=send_sems.at[k], recv_sem=recv_sems.at[k],
            device_id={axis: targets[d]}, device_id_type=MESH)

    last = {}
    for step in range(1, steps[0] + 1):
        for which in range(2):
            if step == 1 and which == 1:
                for s in swaps:
                    s.wait_recv()
            for r in range(halves):
                for a in range(count):
                    for d in range(2):
                        if not carries(d, step, r):
                            continue
                        if step > 1:
                            last[(d, which, r, a)].wait_recv()
                        c = chunk_copy(d, step, which, r, a)
                        c.start()
                        copies[(d, step, which, r, a)] = c
                        last[(d, which, r, a)] = c
    for c in last.values():
        c.wait_recv()
    for c in locals_:
        c.wait()
    for s in swaps:
        s.wait_send()
    for c in copies.values():
        c.wait_send()


def ring_gather(arrays, axis, outer, inner, ring_on_inner, cid, halves=2):
    rows = arrays[0].shape[0]
    count = len(arrays)
    ring = inner if ring_on_inner else outer
    shapes = [
        (2, ring, rows, a.shape[1]) if ring_on_inner else (ring, 2, rows, a.shape[1]) for a in arrays
    ]
    n_copies = 2 * ring * 2 * halves * count
    got = pl.pallas_call(
        functools.partial(_ring_gather_kernel, axis, outer, inner, ring_on_inner, halves, count),
        out_shape=tuple(jax.ShapeDtypeStruct(s, a.dtype) for s, a in zip(shapes, arrays)),
        in_specs=[pl.BlockSpec(memory_space=pltpu.VMEM)] * count,
        out_specs=tuple(pl.BlockSpec(memory_space=pltpu.VMEM) for _ in arrays),
        scratch_shapes=[
            pltpu.SemaphoreType.DMA((n_copies,)),
            pltpu.SemaphoreType.DMA((n_copies,)),
            pltpu.SemaphoreType.DMA((2, count)),
            pltpu.SemaphoreType.DMA((count,)),
        ],
        compiler_params=pltpu.CompilerParams(collective_id=cid, has_side_effects=True),
    )(*arrays)
    return [g.reshape(2 * ring * rows, a.shape[1]) for g, a in zip(got, arrays)]


def _ring_sum_kernel(axis, outer, chunks, x_ref, out_ref, send_buf, recv_buf, swap_buf, send_sems, recv_sems, swap_sems):
    me = lax.axis_index(axis)
    y = me // 2
    x = me % 2
    ring = outer
    up = lax.rem(y + 1, ring) * 2 + x
    down = lax.rem(y + ring - 1, ring) * 2 + x
    partner = y * 2 + 1 - x
    rows = x_ref.shape[1]
    half = rows // 2
    part = half // chunks

    barrier = pltpu.get_barrier_semaphore()
    for peer in (partner, up, down):
        pl.semaphore_signal(barrier, inc=1, device_id={axis: peer}, device_id_type=MESH)
    pl.semaphore_wait(barrier, 3)

    targets = (up, down)
    copies = {}

    def dest(d, step):
        return lax.rem(y - step + ring, ring) if d == 0 else lax.rem(y + step, ring)

    for step in range(1, ring):
        for c in range(chunks):
            for d in range(2):
                rs = pl.ds(d * half + c * part, part)
                blocks = pl.ds(dest(d, step) * 2, 2)
                if step == 1:
                    src = x_ref.at[blocks, rs]
                else:
                    copies[(d, step - 1, c)].wait_recv()
                    send_buf[d, step, :, pl.ds(c * part, part)] = (
                        recv_buf[d, step - 1, :, pl.ds(c * part, part)] + x_ref[blocks, rs]
                    )
                    src = send_buf.at[d, step, :, pl.ds(c * part, part)]
                cp = pltpu.make_async_remote_copy(
                    src_ref=src, dst_ref=recv_buf.at[d, step, :, pl.ds(c * part, part)],
                    send_sem=send_sems.at[d, step, c], recv_sem=recv_sems.at[d, step, c],
                    device_id={axis: targets[d]}, device_id_type=MESH)
                cp.start()
                copies[(d, step, c)] = cp
    swaps = []
    for c in range(chunks):
        for d in range(2):
            rs = pl.ds(d * half + c * part, part)
            local = pl.ds(c * part, part)
            copies[(d, ring - 1, c)].wait_recv()
            swap_buf[0, d, local] = recv_buf[d, ring - 1, 1 - x, local] + x_ref[y * 2 + 1 - x, rs]
            out_ref[rs] = recv_buf[d, ring - 1, x, local] + x_ref[y * 2 + x, rs]
            sw = pltpu.make_async_remote_copy(
                src_ref=swap_buf.at[0, d, local], dst_ref=swap_buf.at[1, d, local],
                send_sem=swap_sems.at[0, d, c], recv_sem=swap_sems.at[1, d, c],
                device_id={axis: partner}, device_id_type=MESH)
            sw.start()
            swaps.append((d, c, sw))
    for d, c, sw in swaps:
        rs = pl.ds(d * half + c * part, part)
        sw.wait_recv()
        out_ref[rs] = out_ref[rs] + swap_buf[1, d, pl.ds(c * part, part)]
    for d, c, sw in swaps:
        sw.wait_send()
    for cp in copies.values():
        cp.wait_send()


def ring_sum(partial, axis, outer, cid, chunks=4):
    count, rows, width = partial.shape
    half = rows // 2
    return pl.pallas_call(
        functools.partial(_ring_sum_kernel, axis, outer, chunks),
        out_shape=jax.ShapeDtypeStruct((rows, width), jnp.float32),
        in_specs=[pl.BlockSpec(memory_space=pltpu.VMEM)],
        out_specs=pl.BlockSpec(memory_space=pltpu.VMEM),
        scratch_shapes=[
            pltpu.VMEM((2, outer, 2, half, width), jnp.float32),
            pltpu.VMEM((2, outer, 2, half, width), jnp.float32),
            pltpu.VMEM((2, 2, half, width), jnp.float32),
            pltpu.SemaphoreType.DMA((2, outer, chunks)),
            pltpu.SemaphoreType.DMA((2, outer, chunks)),
            pltpu.SemaphoreType.DMA((2, 2, chunks)),
        ],
        compiler_params=pltpu.CompilerParams(collective_id=cid, has_side_effects=True, vmem_limit_bytes=60 * 1024 * 1024),
    )(partial)


def per_device(
    forward_acts, backward_grad, stored_gate, stored_up, gate_weight, up_weight, down_weight
):
    n_pipe = lax.axis_size("pipe")
    n_tensor = lax.axis_size("tensor")
    hidden_width = gate_weight.shape[1]
    model_width = forward_acts.shape[1]
    contract_last = (((1,), (1,)), ((), ()))

    whole_acts, whole_grad = ring_gather(
        [forward_acts, backward_grad], "tensor", 2, n_tensor // 2, True, 0
    )

    gate_part = jnp.dot(whole_acts, gate_weight, preferred_element_type=jnp.float32)
    up_part = jnp.dot(whole_acts, up_weight, preferred_element_type=jnp.float32)
    grad_part = lax.dot_general(
        whole_grad, down_weight, contract_last, preferred_element_type=jnp.float32
    )
    partials = jnp.concatenate([gate_part, up_part, grad_part], axis=1)
    summed = ring_sum(
        partials.reshape((n_pipe, partials.shape[0] // n_pipe, partials.shape[1])),
        "pipe",
        n_pipe // 2,
        1,
    )
    gate_pre = summed[:, :hidden_width]
    up_pre = summed[:, hidden_width : 2 * hidden_width]
    hidden_grad = summed[:, 2 * hidden_width :]
    hidden_part = (jax.nn.silu(gate_pre) * up_pre).astype(jnp.bfloat16)
    local_gate_slope, local_up_slope = make_slopes(hidden_grad, stored_gate, stored_up)

    hidden, gate_slopes, up_slopes = ring_gather(
        [hidden_part, local_gate_slope, local_up_slope], "pipe", n_pipe // 2, 2, False, 2
    )

    out_part = jnp.dot(hidden, down_weight, preferred_element_type=jnp.float32)
    in_part = lax.dot_general(
        gate_slopes, gate_weight, contract_last, preferred_element_type=jnp.float32
    ) + lax.dot_general(up_slopes, up_weight, contract_last, preferred_element_type=jnp.float32)
    finished = scatter_sum_rows(
        jnp.concatenate([out_part, in_part], axis=1), "tensor", n_tensor, TENSOR_LINK
    ).astype(jnp.bfloat16)
    return (finished[:, :model_width], finished[:, model_width:])


def solution(mesh):
    in_specs = (
        P(("dp", "tensor"), "pipe"),
        P(("dp", "tensor"), "pipe"),
        P(("dp", "pipe"), "tensor"),
        P(("dp", "pipe"), "tensor"),
        P("pipe", "tensor"),
        P("pipe", "tensor"),
        P("tensor", "pipe"),
    )
    out_specs = (P(("dp", "tensor"), "pipe"), P(("dp", "tensor"), "pipe"))
    return jax.shard_map(
        per_device, mesh=mesh, in_specs=in_specs, out_specs=out_specs, check_vma=False
    )
```

```python
import functools

import jax
import jax.numpy as jnp
from jax import lax
from jax.experimental import pallas as pl
from jax.experimental.pallas import tpu as pltpu
from jax.sharding import PartitionSpec as P

PIPE_LINK = jnp.float32
TENSOR_LINK = jnp.bfloat16
MESH = pl.DeviceIdType.MESH


def make_slopes(hidden_grad, gate_vals, up_vals):
    gate_wide = gate_vals.astype(jnp.float32)
    up_wide = up_vals.astype(jnp.float32)
    sigma = jax.nn.sigmoid(gate_wide)
    gate_slope = (hidden_grad * up_wide * sigma * (1.0 + gate_wide * (1.0 - sigma))).astype(
        jnp.bfloat16
    )
    up_slope = (hidden_grad * gate_wide * sigma).astype(jnp.bfloat16)
    return gate_slope, up_slope


def scatter_sum_rows(partial, axis, count, link_dtype):
    rows = partial.shape[0] // count
    sent = partial.reshape((count, rows) + partial.shape[1:]).astype(link_dtype)
    got = lax.all_to_all(sent, axis, 0, 0, tiled=False)
    return got.astype(jnp.float32).sum(axis=0)


def _ring_gather_kernel(axis, outer, inner, ring_on_inner, halves, count, *refs):
    me = lax.axis_index(axis)
    o = me // inner
    i = me % inner
    if ring_on_inner:
        ring = inner
        pos, other = i, o
        def at(p, q):
            return q * inner + p
    else:
        ring = outer
        pos, other = o, i
        def at(p, q):
            return p * inner + q
    partner = at(pos, 1 - other)
    up = at(lax.rem(pos + 1, ring), other)
    down = at(lax.rem(pos + ring - 1, ring), other)
    ins = refs[:count]
    outs = refs[count:2 * count]
    send_sems, recv_sems, swap_sems, local_sems = refs[2 * count:]
    rows = ins[0].shape[0]
    part = rows // halves
    steps = (ring // 2, ring // 2)

    def carries(d, step, r):
        if ring % 2 == 1 or step < ring // 2:
            return True
        return (r < halves // 2) == (d == 0)

    barrier = pltpu.get_barrier_semaphore()
    for peer in (partner, up, down):
        pl.semaphore_signal(barrier, inc=1, device_id={axis: peer}, device_id_type=MESH)
    pl.semaphore_wait(barrier, 3)


    def slot_of(a, half, slot):
        return outs[a].at[half, slot] if ring_on_inner else outs[a].at[slot, half]
    locals_ = []
    swaps = []
    for a in range(count):
        c = pltpu.make_async_copy(ins[a], slot_of(a, other, pos), local_sems.at[a])
        c.start()
        locals_.append(c)
        s = pltpu.make_async_remote_copy(
            src_ref=ins[a], dst_ref=slot_of(a, other, pos),
            send_sem=swap_sems.at[0, a], recv_sem=swap_sems.at[1, a],
            device_id={axis: partner}, device_id_type=MESH)
        s.start()
        swaps.append(s)

    targets = (up, down)
    copies = {}

    def chunk_copy(d, step, which, r, a):
        slot = lax.rem(pos - step + 1 + ring, ring) if d == 0 else lax.rem(pos + step - 1, ring)
        half = other if which == 0 else 1 - other
        rs = pl.ds(r * part, part)
        if step == 1 and which == 0:
            src = ins[a].at[rs]
        else:
            src = slot_of(a, half, slot).at[rs]
        k = (((d * ring + step - 1) * 2 + which) * halves + r) * count + a
        return pltpu.make_async_remote_copy(
            src_ref=src, dst_ref=slot_of(a, half, slot).at[rs],
            send_sem=send_sems.at[k], recv_sem=recv_sems.at[k],
            device_id={axis: targets[d]}, device_id_type=MESH)

    last = {}
    for step in range(1, steps[0] + 1):
        for which in range(2):
            if step == 1 and which == 1:
                for s in swaps:
                    s.wait_recv()
            for r in range(halves):
                for a in range(count):
                    for d in range(2):
                        if not carries(d, step, r):
                            continue
                        if step > 1:
                            last[(d, which, r, a)].wait_recv()
                        c = chunk_copy(d, step, which, r, a)
                        c.start()
                        copies[(d, step, which, r, a)] = c
                        last[(d, which, r, a)] = c
    for c in last.values():
        c.wait_recv()
    for c in locals_:
        c.wait()
    for s in swaps:
        s.wait_send()
    for c in copies.values():
        c.wait_send()


def ring_gather(arrays, axis, outer, inner, ring_on_inner, cid, halves=2):
    rows = arrays[0].shape[0]
    count = len(arrays)
    ring = inner if ring_on_inner else outer
    shapes = [
        (2, ring, rows, a.shape[1]) if ring_on_inner else (ring, 2, rows, a.shape[1]) for a in arrays
    ]
    n_copies = 2 * ring * 2 * halves * count
    got = pl.pallas_call(
        functools.partial(_ring_gather_kernel, axis, outer, inner, ring_on_inner, halves, count),
        out_shape=tuple(jax.ShapeDtypeStruct(s, a.dtype) for s, a in zip(shapes, arrays)),
        in_specs=[pl.BlockSpec(memory_space=pltpu.VMEM)] * count,
        out_specs=tuple(pl.BlockSpec(memory_space=pltpu.VMEM) for _ in arrays),
        scratch_shapes=[
            pltpu.SemaphoreType.DMA((n_copies,)),
            pltpu.SemaphoreType.DMA((n_copies,)),
            pltpu.SemaphoreType.DMA((2, count)),
            pltpu.SemaphoreType.DMA((count,)),
        ],
        compiler_params=pltpu.CompilerParams(collective_id=cid, has_side_effects=True),
    )(*arrays)
    return [g.reshape(2 * ring * rows, a.shape[1]) for g, a in zip(got, arrays)]


def _ring_sum_kernel(axis, outer, chunks, count, *refs):
    xs = refs[:count]
    outs = refs[count:2 * count]
    send_bufs = refs[2 * count:3 * count]
    recv_bufs = refs[3 * count:4 * count]
    swap_bufs = refs[4 * count:5 * count]
    held = refs[5 * count:6 * count]
    send_sems, recv_sems, swap_sems, load_sems = refs[6 * count:]
    me = lax.axis_index(axis)
    y = me // 2
    x = me % 2
    ring = outer
    up = lax.rem(y + 1, ring) * 2 + x
    down = lax.rem(y + ring - 1, ring) * 2 + x
    partner = y * 2 + 1 - x
    rows = xs[0].shape[1]
    half = rows // 2
    part = half // chunks

    loads = []
    for t in range(count):
        ld = pltpu.make_async_copy(xs[t], held[t], load_sems.at[t])
        ld.start()
        loads.append(ld)

    barrier = pltpu.get_barrier_semaphore()
    for peer in (partner, up, down):
        pl.semaphore_signal(barrier, inc=1, device_id={axis: peer}, device_id_type=MESH)
    pl.semaphore_wait(barrier, 3)

    targets = (up, down)
    copies = {}

    def dest(d, step):
        return lax.rem(y - step + ring, ring) if d == 0 else lax.rem(y + step, ring)

    for step in range(1, ring):
        for c in range(chunks):
            for d in range(2):
                for t in range(count):
                    rs = pl.ds(d * half + c * part, part)
                    local = pl.ds(c * part, part)
                    blocks = pl.ds(dest(d, step) * 2, 2)
                    if step == 1:
                        src = xs[t].at[blocks, rs]
                    else:
                        if loads:
                            for ld in loads:
                                ld.wait()
                            loads.clear()
                        copies[(d, step - 1, c, t)].wait_recv()
                        send_bufs[t][d, step, :, local] = (
                            recv_bufs[t][d, step - 1, :, local] + held[t][blocks, rs]
                        )
                        src = send_bufs[t].at[d, step, :, local]
                    cp = pltpu.make_async_remote_copy(
                        src_ref=src, dst_ref=recv_bufs[t].at[d, step, :, local],
                        send_sem=send_sems.at[t, d, step, c], recv_sem=recv_sems.at[t, d, step, c],
                        device_id={axis: targets[d]}, device_id_type=MESH)
                    cp.start()
                    copies[(d, step, c, t)] = cp
    for ld in loads:
        ld.wait()
    swaps = []
    for c in range(chunks):
        for d in range(2):
            for t in range(count):
                rs = pl.ds(d * half + c * part, part)
                local = pl.ds(c * part, part)
                copies[(d, ring - 1, c, t)].wait_recv()
                swap_bufs[t][0, d, local] = recv_bufs[t][d, ring - 1, 1 - x, local] + held[t][y * 2 + 1 - x, rs]
                outs[t][rs] = recv_bufs[t][d, ring - 1, x, local] + held[t][y * 2 + x, rs]
                sw = pltpu.make_async_remote_copy(
                    src_ref=swap_bufs[t].at[0, d, local], dst_ref=swap_bufs[t].at[1, d, local],
                    send_sem=swap_sems.at[t, 0, d, c], recv_sem=swap_sems.at[t, 1, d, c],
                    device_id={axis: partner}, device_id_type=MESH)
                sw.start()
                swaps.append((d, c, t, sw))
    for d, c, t, sw in swaps:
        rs = pl.ds(d * half + c * part, part)
        sw.wait_recv()
        outs[t][rs] = outs[t][rs] + swap_bufs[t][1, d, pl.ds(c * part, part)]
    for d, c, t, sw in swaps:
        sw.wait_send()
    for cp in copies.values():
        cp.wait_send()


def ring_sum(partials, axis, outer, cid, chunks=4):
    count = len(partials)
    rows = partials[0].shape[1]
    half = rows // 2
    scratch = []
    for kind in range(4):
        for p in partials:
            width = p.shape[2]
            if kind < 2:
                scratch.append(pltpu.VMEM((2, outer, 2, half, width), jnp.float32))
            elif kind == 2:
                scratch.append(pltpu.VMEM((2, 2, half, width), jnp.float32))
            else:
                scratch.append(pltpu.VMEM(p.shape, jnp.float32))
    scratch += [
        pltpu.SemaphoreType.DMA((count, 2, outer, chunks)),
        pltpu.SemaphoreType.DMA((count, 2, outer, chunks)),
        pltpu.SemaphoreType.DMA((count, 2, 2, chunks)),
        pltpu.SemaphoreType.DMA((count,)),
    ]
    return pl.pallas_call(
        functools.partial(_ring_sum_kernel, axis, outer, chunks, count),
        out_shape=tuple(jax.ShapeDtypeStruct((rows, p.shape[2]), jnp.float32) for p in partials),
        in_specs=[pl.BlockSpec(memory_space=pl.ANY)] * count,
        out_specs=tuple(pl.BlockSpec(memory_space=pltpu.VMEM) for _ in partials),
        scratch_shapes=scratch,
        compiler_params=pltpu.CompilerParams(collective_id=cid, has_side_effects=True, vmem_limit_bytes=60 * 1024 * 1024),
    )(*partials)


def per_device(
    forward_acts, backward_grad, stored_gate, stored_up, gate_weight, up_weight, down_weight
):
    n_pipe = lax.axis_size("pipe")
    n_tensor = lax.axis_size("tensor")
    hidden_width = gate_weight.shape[1]
    model_width = forward_acts.shape[1]
    contract_last = (((1,), (1,)), ((), ()))

    whole_acts, whole_grad = ring_gather(
        [forward_acts, backward_grad], "tensor", 2, n_tensor // 2, True, 0
    )

    gate_part = jnp.dot(whole_acts, gate_weight, preferred_element_type=jnp.float32)
    up_part = jnp.dot(whole_acts, up_weight, preferred_element_type=jnp.float32)
    grad_part = lax.dot_general(
        whole_grad, down_weight, contract_last, preferred_element_type=jnp.float32
    )
    gate_pre, up_pre, hidden_grad = ring_sum(
        [p.reshape((n_pipe, p.shape[0] // n_pipe, p.shape[1])) for p in (gate_part, up_part, grad_part)],
        "pipe",
        n_pipe // 2,
        1,
    )
    hidden_part = (jax.nn.silu(gate_pre) * up_pre).astype(jnp.bfloat16)
    local_gate_slope, local_up_slope = make_slopes(hidden_grad, stored_gate, stored_up)

    hidden, gate_slopes, up_slopes = ring_gather(
        [hidden_part, local_gate_slope, local_up_slope], "pipe", n_pipe // 2, 2, False, 2
    )

    out_part = jnp.dot(hidden, down_weight, preferred_element_type=jnp.float32)
    in_part = lax.dot_general(
        gate_slopes, gate_weight, contract_last, preferred_element_type=jnp.float32
    ) + lax.dot_general(up_slopes, up_weight, contract_last, preferred_element_type=jnp.float32)
    finished = scatter_sum_rows(
        jnp.concatenate([out_part, in_part], axis=1), "tensor", n_tensor, TENSOR_LINK
    ).astype(jnp.bfloat16)
    return (finished[:, :model_width], finished[:, model_width:])


def solution(mesh):
    in_specs = (
        P(("dp", "tensor"), "pipe"),
        P(("dp", "tensor"), "pipe"),
        P(("dp", "pipe"), "tensor"),
        P(("dp", "pipe"), "tensor"),
        P("pipe", "tensor"),
        P("pipe", "tensor"),
        P("tensor", "pipe"),
    )
    out_specs = (P(("dp", "tensor"), "pipe"), P(("dp", "tensor"), "pipe"))
    return jax.shard_map(
        per_device, mesh=mesh, in_specs=in_specs, out_specs=out_specs, check_vma=False
    )
```

```python
import functools

import jax
import jax.numpy as jnp
from jax import lax
from jax.experimental import pallas as pl
from jax.experimental.pallas import tpu as pltpu
from jax.sharding import PartitionSpec as P

PIPE_LINK = jnp.float32
TENSOR_LINK = jnp.bfloat16
MESH = pl.DeviceIdType.MESH


def make_slopes(hidden_grad, gate_vals, up_vals):
    gate_wide = gate_vals.astype(jnp.float32)
    up_wide = up_vals.astype(jnp.float32)
    sigma = jax.nn.sigmoid(gate_wide)
    gate_slope = (hidden_grad * up_wide * sigma * (1.0 + gate_wide * (1.0 - sigma))).astype(
        jnp.bfloat16
    )
    up_slope = (hidden_grad * gate_wide * sigma).astype(jnp.bfloat16)
    return gate_slope, up_slope


def scatter_sum_rows(partial, axis, count, link_dtype):
    rows = partial.shape[0] // count
    sent = partial.reshape((count, rows) + partial.shape[1:]).astype(link_dtype)
    got = lax.all_to_all(sent, axis, 0, 0, tiled=False)
    return got.astype(jnp.float32).sum(axis=0)


def _ring_gather_kernel(axis, outer, inner, ring_on_inner, halves, count, *refs):
    me = lax.axis_index(axis)
    o = me // inner
    i = me % inner
    if ring_on_inner:
        ring = inner
        pos, other = i, o
        def at(p, q):
            return q * inner + p
    else:
        ring = outer
        pos, other = o, i
        def at(p, q):
            return p * inner + q
    partner = at(pos, 1 - other)
    up = at(lax.rem(pos + 1, ring), other)
    down = at(lax.rem(pos + ring - 1, ring), other)
    ins = refs[:count]
    outs = refs[count:2 * count]
    send_sems, recv_sems, swap_sems, local_sems = refs[2 * count:]
    rows = ins[0].shape[0]
    part = rows // halves
    steps = (ring // 2, ring // 2)

    def carries(d, step, r):
        if ring % 2 == 1 or step < ring // 2:
            return True
        return (r < halves // 2) == (d == 0)

    barrier = pltpu.get_barrier_semaphore()
    for peer in (partner, up, down):
        pl.semaphore_signal(barrier, inc=1, device_id={axis: peer}, device_id_type=MESH)
    pl.semaphore_wait(barrier, 3)


    def slot_of(a, half, slot):
        return outs[a].at[half, slot] if ring_on_inner else outs[a].at[slot, half]
    locals_ = []
    swaps = []
    for a in range(count):
        c = pltpu.make_async_copy(ins[a], slot_of(a, other, pos), local_sems.at[a])
        c.start()
        locals_.append(c)
        s = pltpu.make_async_remote_copy(
            src_ref=ins[a], dst_ref=slot_of(a, other, pos),
            send_sem=swap_sems.at[0, a], recv_sem=swap_sems.at[1, a],
            device_id={axis: partner}, device_id_type=MESH)
        s.start()
        swaps.append(s)

    targets = (up, down)
    copies = {}

    def chunk_copy(d, step, which, r, a):
        slot = lax.rem(pos - step + 1 + ring, ring) if d == 0 else lax.rem(pos + step - 1, ring)
        half = other if which == 0 else 1 - other
        rs = pl.ds(r * part, part)
        if step == 1 and which == 0:
            src = ins[a].at[rs]
        else:
            src = slot_of(a, half, slot).at[rs]
        k = (((d * ring + step - 1) * 2 + which) * halves + r) * count + a
        return pltpu.make_async_remote_copy(
            src_ref=src, dst_ref=slot_of(a, half, slot).at[rs],
            send_sem=send_sems.at[k], recv_sem=recv_sems.at[k],
            device_id={axis: targets[d]}, device_id_type=MESH)

    last = {}
    for step in range(1, steps[0] + 1):
        for which in range(2):
            if step == 1 and which == 1:
                for s in swaps:
                    s.wait_recv()
            for r in range(halves):
                for a in range(count):
                    for d in range(2):
                        if not carries(d, step, r):
                            continue
                        if step > 1:
                            last[(d, which, r, a)].wait_recv()
                        c = chunk_copy(d, step, which, r, a)
                        c.start()
                        copies[(d, step, which, r, a)] = c
                        last[(d, which, r, a)] = c
    for c in last.values():
        c.wait_recv()
    for c in locals_:
        c.wait()
    for s in swaps:
        s.wait_send()
    for c in copies.values():
        c.wait_send()


def ring_gather(arrays, axis, outer, inner, ring_on_inner, cid, halves=2):
    rows = arrays[0].shape[0]
    count = len(arrays)
    ring = inner if ring_on_inner else outer
    shapes = [
        (2, ring, rows, a.shape[1]) if ring_on_inner else (ring, 2, rows, a.shape[1]) for a in arrays
    ]
    n_copies = 2 * ring * 2 * halves * count
    got = pl.pallas_call(
        functools.partial(_ring_gather_kernel, axis, outer, inner, ring_on_inner, halves, count),
        out_shape=tuple(jax.ShapeDtypeStruct(s, a.dtype) for s, a in zip(shapes, arrays)),
        in_specs=[pl.BlockSpec(memory_space=pltpu.VMEM)] * count,
        out_specs=tuple(pl.BlockSpec(memory_space=pltpu.VMEM) for _ in arrays),
        scratch_shapes=[
            pltpu.SemaphoreType.DMA((n_copies,)),
            pltpu.SemaphoreType.DMA((n_copies,)),
            pltpu.SemaphoreType.DMA((2, count)),
            pltpu.SemaphoreType.DMA((count,)),
        ],
        compiler_params=pltpu.CompilerParams(collective_id=cid, has_side_effects=True),
    )(*arrays)
    return [g.reshape(2 * ring * rows, a.shape[1]) for g, a in zip(got, arrays)]


def _ring_sum_kernel(axis, outer, chunks, count, *refs):
    xs = refs[:count]
    outs = refs[count:2 * count]
    send_bufs = refs[2 * count:3 * count]
    recv_bufs = refs[3 * count:4 * count]
    swap_bufs = refs[4 * count:5 * count]
    held = refs[5 * count:6 * count]
    send_sems, recv_sems, swap_sems, load_sems = refs[6 * count:]
    me = lax.axis_index(axis)
    y = me // 2
    x = me % 2
    ring = outer
    up = lax.rem(y + 1, ring) * 2 + x
    down = lax.rem(y + ring - 1, ring) * 2 + x
    partner = y * 2 + 1 - x
    rows = xs[0].shape[1]
    half = rows // 2
    part = half // chunks

    loads = []
    for t in range(count):
        ld = pltpu.make_async_copy(xs[t], held[t], load_sems.at[t])
        ld.start()
        loads.append(ld)

    barrier = pltpu.get_barrier_semaphore()
    for peer in (partner, up, down):
        pl.semaphore_signal(barrier, inc=1, device_id={axis: peer}, device_id_type=MESH)
    pl.semaphore_wait(barrier, 3)

    targets = (up, down)
    copies = {}

    def dest(d, step):
        return lax.rem(y - step + ring, ring) if d == 0 else lax.rem(y + step, ring)

    for step in range(1, ring):
        for c in range(chunks):
            for d in range(2):
                for t in range(count):
                    rs = pl.ds(d * half + c * part, part)
                    local = pl.ds(c * part, part)
                    blocks = pl.ds(dest(d, step) * 2, 2)
                    if step == 1:
                        src = xs[t].at[blocks, rs]
                    else:
                        if loads:
                            for ld in loads:
                                ld.wait()
                            loads.clear()
                        copies[(d, step - 1, c, t)].wait_recv()
                        send_bufs[t][d, step, :, local] = (
                            recv_bufs[t][d, step - 1, :, local] + held[t][blocks, rs]
                        )
                        src = send_bufs[t].at[d, step, :, local]
                    cp = pltpu.make_async_remote_copy(
                        src_ref=src, dst_ref=recv_bufs[t].at[d, step, :, local],
                        send_sem=send_sems.at[t, d, step, c], recv_sem=recv_sems.at[t, d, step, c],
                        device_id={axis: targets[d]}, device_id_type=MESH)
                    cp.start()
                    copies[(d, step, c, t)] = cp
    for ld in loads:
        ld.wait()
    swaps = []
    for c in range(chunks):
        for d in range(2):
            for t in range(count):
                rs = pl.ds(d * half + c * part, part)
                local = pl.ds(c * part, part)
                copies[(d, ring - 1, c, t)].wait_recv()
                swap_bufs[t][0, d, local] = recv_bufs[t][d, ring - 1, 1 - x, local] + held[t][y * 2 + 1 - x, rs]
                outs[t][rs] = recv_bufs[t][d, ring - 1, x, local] + held[t][y * 2 + x, rs]
                sw = pltpu.make_async_remote_copy(
                    src_ref=swap_bufs[t].at[0, d, local], dst_ref=swap_bufs[t].at[1, d, local],
                    send_sem=swap_sems.at[t, 0, d, c], recv_sem=swap_sems.at[t, 1, d, c],
                    device_id={axis: partner}, device_id_type=MESH)
                sw.start()
                swaps.append((d, c, t, sw))
    for d, c, t, sw in swaps:
        rs = pl.ds(d * half + c * part, part)
        sw.wait_recv()
        outs[t][rs] = outs[t][rs] + swap_bufs[t][1, d, pl.ds(c * part, part)]
    for d, c, t, sw in swaps:
        sw.wait_send()
    for cp in copies.values():
        cp.wait_send()


def ring_sum(partials, axis, outer, cid, chunks=4):
    count = len(partials)
    rows = partials[0].shape[1]
    half = rows // 2
    scratch = []
    for kind in range(4):
        for p in partials:
            width = p.shape[2]
            if kind < 2:
                scratch.append(pltpu.VMEM((2, outer, 2, half, width), jnp.float32))
            elif kind == 2:
                scratch.append(pltpu.VMEM((2, 2, half, width), jnp.float32))
            else:
                scratch.append(pltpu.VMEM(p.shape, jnp.float32))
    scratch += [
        pltpu.SemaphoreType.DMA((count, 2, outer, chunks)),
        pltpu.SemaphoreType.DMA((count, 2, outer, chunks)),
        pltpu.SemaphoreType.DMA((count, 2, 2, chunks)),
        pltpu.SemaphoreType.DMA((count,)),
    ]
    return pl.pallas_call(
        functools.partial(_ring_sum_kernel, axis, outer, chunks, count),
        out_shape=tuple(jax.ShapeDtypeStruct((rows, p.shape[2]), jnp.float32) for p in partials),
        in_specs=[pl.BlockSpec(memory_space=pl.ANY)] * count,
        out_specs=tuple(pl.BlockSpec(memory_space=pltpu.VMEM) for _ in partials),
        scratch_shapes=scratch,
        compiler_params=pltpu.CompilerParams(collective_id=cid, has_side_effects=True, vmem_limit_bytes=60 * 1024 * 1024),
    )(*partials)


def per_device(
    forward_acts, backward_grad, stored_gate, stored_up, gate_weight, up_weight, down_weight
):
    n_pipe = lax.axis_size("pipe")
    n_tensor = lax.axis_size("tensor")
    hidden_width = gate_weight.shape[1]
    model_width = forward_acts.shape[1]
    contract_last = (((1,), (1,)), ((), ()))

    whole_acts, whole_grad = ring_gather(
        [forward_acts, backward_grad], "tensor", 2, n_tensor // 2, True, 0
    )

    gate_part = jnp.dot(whole_acts, gate_weight, preferred_element_type=jnp.float32)
    up_part = jnp.dot(whole_acts, up_weight, preferred_element_type=jnp.float32)
    grad_part = lax.dot_general(
        whole_grad, down_weight, contract_last, preferred_element_type=jnp.float32
    )
    gate_pre, up_pre, hidden_grad = ring_sum(
        [p.reshape((n_pipe, p.shape[0] // n_pipe, p.shape[1])) for p in (gate_part, up_part, grad_part)],
        "pipe",
        n_pipe // 2,
        1,
    )
    hidden_part = (jax.nn.silu(gate_pre) * up_pre).astype(jnp.bfloat16)
    local_gate_slope, local_up_slope = make_slopes(hidden_grad, stored_gate, stored_up)

    hidden, gate_slopes, up_slopes = ring_gather(
        [hidden_part, local_gate_slope, local_up_slope], "pipe", n_pipe // 2, 2, False, 2, halves=4
    )

    out_part = jnp.dot(hidden, down_weight, preferred_element_type=jnp.float32)
    in_part = lax.dot_general(
        gate_slopes, gate_weight, contract_last, preferred_element_type=jnp.float32
    ) + lax.dot_general(up_slopes, up_weight, contract_last, preferred_element_type=jnp.float32)
    finished = scatter_sum_rows(
        jnp.concatenate([out_part, in_part], axis=1), "tensor", n_tensor, TENSOR_LINK
    ).astype(jnp.bfloat16)
    return (finished[:, :model_width], finished[:, model_width:])


def solution(mesh):
    in_specs = (
        P(("dp", "tensor"), "pipe"),
        P(("dp", "tensor"), "pipe"),
        P(("dp", "pipe"), "tensor"),
        P(("dp", "pipe"), "tensor"),
        P("pipe", "tensor"),
        P("pipe", "tensor"),
        P("tensor", "pipe"),
    )
    out_specs = (P(("dp", "tensor"), "pipe"), P(("dp", "tensor"), "pipe"))
    return jax.shard_map(
        per_device, mesh=mesh, in_specs=in_specs, out_specs=out_specs, check_vma=False
    )
```

```python
import functools

import jax
import jax.numpy as jnp
from jax import lax
from jax.experimental import pallas as pl
from jax.experimental.pallas import tpu as pltpu
from jax.sharding import PartitionSpec as P

PIPE_LINK = jnp.float32
TENSOR_LINK = jnp.bfloat16
MESH = pl.DeviceIdType.MESH


def make_slopes(hidden_grad, gate_vals, up_vals):
    gate_wide = gate_vals.astype(jnp.float32)
    up_wide = up_vals.astype(jnp.float32)
    sigma = jax.nn.sigmoid(gate_wide)
    gate_slope = (hidden_grad * up_wide * sigma * (1.0 + gate_wide * (1.0 - sigma))).astype(
        jnp.bfloat16
    )
    up_slope = (hidden_grad * gate_wide * sigma).astype(jnp.bfloat16)
    return gate_slope, up_slope


def scatter_sum_rows(partial, axis, count, link_dtype):
    rows = partial.shape[0] // count
    sent = partial.reshape((count, rows) + partial.shape[1:]).astype(link_dtype)
    got = lax.all_to_all(sent, axis, 0, 0, tiled=False)
    return got.astype(jnp.float32).sum(axis=0)


def _ring_gather_kernel(axis, outer, inner, ring_on_inner, halves, count, *refs):
    me = lax.axis_index(axis)
    o = me // inner
    i = me % inner
    if ring_on_inner:
        ring = inner
        pos, other = i, o
        def at(p, q):
            return q * inner + p
    else:
        ring = outer
        pos, other = o, i
        def at(p, q):
            return p * inner + q
    partner = at(pos, 1 - other)
    up = at(lax.rem(pos + 1, ring), other)
    down = at(lax.rem(pos + ring - 1, ring), other)
    ins = refs[:count]
    outs = refs[count:2 * count]
    send_sems, recv_sems, swap_sems, local_sems = refs[2 * count:]
    rows = ins[0].shape[0]
    part = rows // halves
    steps = (ring // 2, ring // 2)

    def carries(d, step, r):
        if ring % 2 == 1 or step < ring // 2:
            return True
        return (r < halves // 2) == (d == 0)

    barrier = pltpu.get_barrier_semaphore()
    for peer in (partner, up, down):
        pl.semaphore_signal(barrier, inc=1, device_id={axis: peer}, device_id_type=MESH)
    pl.semaphore_wait(barrier, 3)


    def slot_of(a, half, slot):
        return outs[a].at[half, slot] if ring_on_inner else outs[a].at[slot, half]
    locals_ = []
    swaps = []
    for a in range(count):
        c = pltpu.make_async_copy(ins[a], slot_of(a, other, pos), local_sems.at[a])
        c.start()
        locals_.append(c)
        s = pltpu.make_async_remote_copy(
            src_ref=ins[a], dst_ref=slot_of(a, other, pos),
            send_sem=swap_sems.at[0, a], recv_sem=swap_sems.at[1, a],
            device_id={axis: partner}, device_id_type=MESH)
        s.start()
        swaps.append(s)

    targets = (up, down)
    copies = {}

    def chunk_copy(d, step, which, r, a):
        slot = lax.rem(pos - step + 1 + ring, ring) if d == 0 else lax.rem(pos + step - 1, ring)
        half = other if which == 0 else 1 - other
        rs = pl.ds(r * part, part)
        if step == 1 and which == 0:
            src = ins[a].at[rs]
        else:
            src = slot_of(a, half, slot).at[rs]
        k = (((d * ring + step - 1) * 2 + which) * halves + r) * count + a
        return pltpu.make_async_remote_copy(
            src_ref=src, dst_ref=slot_of(a, half, slot).at[rs],
            send_sem=send_sems.at[k], recv_sem=recv_sems.at[k],
            device_id={axis: targets[d]}, device_id_type=MESH)

    last = {}
    for step in range(1, steps[0] + 1):
        for which in range(2):
            if step == 1 and which == 1:
                for s in swaps:
                    s.wait_recv()
            for r in range(halves):
                for a in range(count):
                    for d in range(2):
                        if not carries(d, step, r):
                            continue
                        if step > 1:
                            last[(d, which, r, a)].wait_recv()
                        c = chunk_copy(d, step, which, r, a)
                        c.start()
                        copies[(d, step, which, r, a)] = c
                        last[(d, which, r, a)] = c
    for c in last.values():
        c.wait_recv()
    for c in locals_:
        c.wait()
    for s in swaps:
        s.wait_send()
    for c in copies.values():
        c.wait_send()


def ring_gather(arrays, axis, outer, inner, ring_on_inner, cid, halves=2):
    rows = arrays[0].shape[0]
    count = len(arrays)
    ring = inner if ring_on_inner else outer
    shapes = [
        (2, ring, rows, a.shape[1]) if ring_on_inner else (ring, 2, rows, a.shape[1]) for a in arrays
    ]
    n_copies = 2 * ring * 2 * halves * count
    got = pl.pallas_call(
        functools.partial(_ring_gather_kernel, axis, outer, inner, ring_on_inner, halves, count),
        out_shape=tuple(jax.ShapeDtypeStruct(s, a.dtype) for s, a in zip(shapes, arrays)),
        in_specs=[pl.BlockSpec(memory_space=pl.ANY)] * count,
        out_specs=tuple(pl.BlockSpec(memory_space=pl.ANY) for _ in arrays),
        scratch_shapes=[
            pltpu.SemaphoreType.DMA((n_copies,)),
            pltpu.SemaphoreType.DMA((n_copies,)),
            pltpu.SemaphoreType.DMA((2, count)),
            pltpu.SemaphoreType.DMA((count,)),
        ],
        compiler_params=pltpu.CompilerParams(collective_id=cid, has_side_effects=True),
    )(*arrays)
    return [g.reshape(2 * ring * rows, a.shape[1]) for g, a in zip(got, arrays)]


def _ring_sum_kernel(axis, outer, chunks, count, *refs):
    xs = refs[:count]
    outs = refs[count:2 * count]
    send_bufs = refs[2 * count:3 * count]
    recv_bufs = refs[3 * count:4 * count]
    swap_bufs = refs[4 * count:5 * count]
    held = refs[5 * count:6 * count]
    send_sems, recv_sems, swap_sems, load_sems = refs[6 * count:]
    me = lax.axis_index(axis)
    y = me // 2
    x = me % 2
    ring = outer
    up = lax.rem(y + 1, ring) * 2 + x
    down = lax.rem(y + ring - 1, ring) * 2 + x
    partner = y * 2 + 1 - x
    rows = xs[0].shape[1]
    half = rows // 2
    part = half // chunks

    loads = []
    for t in range(count):
        ld = pltpu.make_async_copy(xs[t], held[t], load_sems.at[t])
        ld.start()
        loads.append(ld)

    barrier = pltpu.get_barrier_semaphore()
    for peer in (partner, up, down):
        pl.semaphore_signal(barrier, inc=1, device_id={axis: peer}, device_id_type=MESH)
    pl.semaphore_wait(barrier, 3)

    targets = (up, down)
    copies = {}

    def dest(d, step):
        return lax.rem(y - step + ring, ring) if d == 0 else lax.rem(y + step, ring)

    for step in range(1, ring):
        for c in range(chunks):
            for d in range(2):
                for t in range(count):
                    rs = pl.ds(d * half + c * part, part)
                    local = pl.ds(c * part, part)
                    blocks = pl.ds(dest(d, step) * 2, 2)
                    if step == 1:
                        src = xs[t].at[blocks, rs]
                    else:
                        if loads:
                            for ld in loads:
                                ld.wait()
                            loads.clear()
                        copies[(d, step - 1, c, t)].wait_recv()
                        send_bufs[t][d, step, :, local] = (
                            recv_bufs[t][d, step - 1, :, local] + held[t][blocks, rs]
                        )
                        src = send_bufs[t].at[d, step, :, local]
                    cp = pltpu.make_async_remote_copy(
                        src_ref=src, dst_ref=recv_bufs[t].at[d, step, :, local],
                        send_sem=send_sems.at[t, d, step, c], recv_sem=recv_sems.at[t, d, step, c],
                        device_id={axis: targets[d]}, device_id_type=MESH)
                    cp.start()
                    copies[(d, step, c, t)] = cp
    for ld in loads:
        ld.wait()
    swaps = []
    for c in range(chunks):
        for d in range(2):
            for t in range(count):
                rs = pl.ds(d * half + c * part, part)
                local = pl.ds(c * part, part)
                copies[(d, ring - 1, c, t)].wait_recv()
                swap_bufs[t][0, d, local] = recv_bufs[t][d, ring - 1, 1 - x, local] + held[t][y * 2 + 1 - x, rs]
                outs[t][rs] = recv_bufs[t][d, ring - 1, x, local] + held[t][y * 2 + x, rs]
                sw = pltpu.make_async_remote_copy(
                    src_ref=swap_bufs[t].at[0, d, local], dst_ref=swap_bufs[t].at[1, d, local],
                    send_sem=swap_sems.at[t, 0, d, c], recv_sem=swap_sems.at[t, 1, d, c],
                    device_id={axis: partner}, device_id_type=MESH)
                sw.start()
                swaps.append((d, c, t, sw))
    for d, c, t, sw in swaps:
        rs = pl.ds(d * half + c * part, part)
        sw.wait_recv()
        outs[t][rs] = outs[t][rs] + swap_bufs[t][1, d, pl.ds(c * part, part)]
    for d, c, t, sw in swaps:
        sw.wait_send()
    for cp in copies.values():
        cp.wait_send()


def ring_sum(partials, axis, outer, cid, chunks=4):
    count = len(partials)
    rows = partials[0].shape[1]
    half = rows // 2
    scratch = []
    for kind in range(4):
        for p in partials:
            width = p.shape[2]
            if kind < 2:
                scratch.append(pltpu.VMEM((2, outer, 2, half, width), jnp.float32))
            elif kind == 2:
                scratch.append(pltpu.VMEM((2, 2, half, width), jnp.float32))
            else:
                scratch.append(pltpu.VMEM(p.shape, jnp.float32))
    scratch += [
        pltpu.SemaphoreType.DMA((count, 2, outer, chunks)),
        pltpu.SemaphoreType.DMA((count, 2, outer, chunks)),
        pltpu.SemaphoreType.DMA((count, 2, 2, chunks)),
        pltpu.SemaphoreType.DMA((count,)),
    ]
    return pl.pallas_call(
        functools.partial(_ring_sum_kernel, axis, outer, chunks, count),
        out_shape=tuple(jax.ShapeDtypeStruct((rows, p.shape[2]), jnp.float32) for p in partials),
        in_specs=[pl.BlockSpec(memory_space=pl.ANY)] * count,
        out_specs=tuple(pl.BlockSpec(memory_space=pltpu.VMEM) for _ in partials),
        scratch_shapes=scratch,
        compiler_params=pltpu.CompilerParams(collective_id=cid, has_side_effects=True, vmem_limit_bytes=60 * 1024 * 1024),
    )(*partials)


def per_device(
    forward_acts, backward_grad, stored_gate, stored_up, gate_weight, up_weight, down_weight
):
    n_pipe = lax.axis_size("pipe")
    n_tensor = lax.axis_size("tensor")
    hidden_width = gate_weight.shape[1]
    model_width = forward_acts.shape[1]
    contract_last = (((1,), (1,)), ((), ()))

    whole_acts, whole_grad = ring_gather(
        [forward_acts, backward_grad], "tensor", 2, n_tensor // 2, True, 0
    )

    gate_part = jnp.dot(whole_acts, gate_weight, preferred_element_type=jnp.float32)
    up_part = jnp.dot(whole_acts, up_weight, preferred_element_type=jnp.float32)
    grad_part = lax.dot_general(
        whole_grad, down_weight, contract_last, preferred_element_type=jnp.float32
    )
    gate_pre, up_pre, hidden_grad = ring_sum(
        [p.reshape((n_pipe, p.shape[0] // n_pipe, p.shape[1])) for p in (gate_part, up_part, grad_part)],
        "pipe",
        n_pipe // 2,
        1,
    )
    hidden_part = (jax.nn.silu(gate_pre) * up_pre).astype(jnp.bfloat16)
    local_gate_slope, local_up_slope = make_slopes(hidden_grad, stored_gate, stored_up)

    hidden, gate_slopes, up_slopes = ring_gather(
        [hidden_part, local_gate_slope, local_up_slope], "pipe", n_pipe // 2, 2, False, 2
    )

    out_part = jnp.dot(hidden, down_weight, preferred_element_type=jnp.float32)
    in_part = lax.dot_general(
        gate_slopes, gate_weight, contract_last, preferred_element_type=jnp.float32
    ) + lax.dot_general(up_slopes, up_weight, contract_last, preferred_element_type=jnp.float32)
    finished = scatter_sum_rows(
        jnp.concatenate([out_part, in_part], axis=1), "tensor", n_tensor, TENSOR_LINK
    ).astype(jnp.bfloat16)
    return (finished[:, :model_width], finished[:, model_width:])


def solution(mesh):
    in_specs = (
        P(("dp", "tensor"), "pipe"),
        P(("dp", "tensor"), "pipe"),
        P(("dp", "pipe"), "tensor"),
        P(("dp", "pipe"), "tensor"),
        P("pipe", "tensor"),
        P("pipe", "tensor"),
        P("tensor", "pipe"),
    )
    out_specs = (P(("dp", "tensor"), "pipe"), P(("dp", "tensor"), "pipe"))
    return jax.shard_map(
        per_device, mesh=mesh, in_specs=in_specs, out_specs=out_specs, check_vma=False
    )
```

```python
import functools

import jax
import jax.numpy as jnp
from jax import lax
from jax.experimental import pallas as pl
from jax.experimental.pallas import tpu as pltpu
from jax.sharding import PartitionSpec as P

PIPE_LINK = jnp.float32
TENSOR_LINK = jnp.bfloat16
MESH = pl.DeviceIdType.MESH


def make_slopes(hidden_grad, gate_vals, up_vals):
    gate_wide = gate_vals.astype(jnp.float32)
    up_wide = up_vals.astype(jnp.float32)
    sigma = jax.nn.sigmoid(gate_wide)
    gate_slope = (hidden_grad * up_wide * sigma * (1.0 + gate_wide * (1.0 - sigma))).astype(
        jnp.bfloat16
    )
    up_slope = (hidden_grad * gate_wide * sigma).astype(jnp.bfloat16)
    return gate_slope, up_slope


def scatter_sum_rows(partial, axis, count, link_dtype):
    rows = partial.shape[0] // count
    sent = partial.reshape((count, rows) + partial.shape[1:]).astype(link_dtype)
    got = lax.all_to_all(sent, axis, 0, 0, tiled=False)
    if count % 4 == 0:
        grouped = got.reshape((count // 4, 4) + got.shape[1:]).astype(jnp.float32).sum(axis=1)
        return lax.optimization_barrier(grouped).sum(axis=0)
    return got.astype(jnp.float32).sum(axis=0)


def _ring_gather_kernel(axis, outer, inner, ring_on_inner, halves, count, *refs):
    me = lax.axis_index(axis)
    o = me // inner
    i = me % inner
    if ring_on_inner:
        ring = inner
        pos, other = i, o
        def at(p, q):
            return q * inner + p
    else:
        ring = outer
        pos, other = o, i
        def at(p, q):
            return p * inner + q
    partner = at(pos, 1 - other)
    up = at(lax.rem(pos + 1, ring), other)
    down = at(lax.rem(pos + ring - 1, ring), other)
    ins = refs[:count]
    outs = refs[count:2 * count]
    send_sems, recv_sems, swap_sems, local_sems = refs[2 * count:]
    rows = ins[0].shape[0]
    part = rows // halves
    steps = (ring // 2, ring // 2)

    def carries(d, step, r):
        if ring % 2 == 1 or step < ring // 2:
            return True
        return (r < halves // 2) == (d == 0)

    barrier = pltpu.get_barrier_semaphore()
    for peer in (partner, up, down):
        pl.semaphore_signal(barrier, inc=1, device_id={axis: peer}, device_id_type=MESH)
    pl.semaphore_wait(barrier, 3)


    def slot_of(a, half, slot):
        return outs[a].at[half, slot] if ring_on_inner else outs[a].at[slot, half]
    locals_ = []
    swaps = []
    for a in range(count):
        c = pltpu.make_async_copy(ins[a], slot_of(a, other, pos), local_sems.at[a])
        c.start()
        locals_.append(c)
        s = pltpu.make_async_remote_copy(
            src_ref=ins[a], dst_ref=slot_of(a, other, pos),
            send_sem=swap_sems.at[0, a], recv_sem=swap_sems.at[1, a],
            device_id={axis: partner}, device_id_type=MESH)
        s.start()
        swaps.append(s)

    targets = (up, down)
    copies = {}

    def chunk_copy(d, step, which, r, a):
        slot = lax.rem(pos - step + 1 + ring, ring) if d == 0 else lax.rem(pos + step - 1, ring)
        half = other if which == 0 else 1 - other
        rs = pl.ds(r * part, part)
        if step == 1 and which == 0:
            src = ins[a].at[rs]
        else:
            src = slot_of(a, half, slot).at[rs]
        k = (((d * ring + step - 1) * 2 + which) * halves + r) * count + a
        return pltpu.make_async_remote_copy(
            src_ref=src, dst_ref=slot_of(a, half, slot).at[rs],
            send_sem=send_sems.at[k], recv_sem=recv_sems.at[k],
            device_id={axis: targets[d]}, device_id_type=MESH)

    last = {}
    for step in range(1, steps[0] + 1):
        for which in range(2):
            if step == 1 and which == 1:
                for s in swaps:
                    s.wait_recv()
            for r in range(halves):
                for a in range(count):
                    for d in range(2):
                        if not carries(d, step, r):
                            continue
                        if step > 1:
                            last[(d, which, r, a)].wait_recv()
                        c = chunk_copy(d, step, which, r, a)
                        c.start()
                        copies[(d, step, which, r, a)] = c
                        last[(d, which, r, a)] = c
    for c in last.values():
        c.wait_recv()
    for c in locals_:
        c.wait()
    for s in swaps:
        s.wait_send()
    for c in copies.values():
        c.wait_send()


def ring_gather(arrays, axis, outer, inner, ring_on_inner, cid, halves=2):
    rows = arrays[0].shape[0]
    count = len(arrays)
    ring = inner if ring_on_inner else outer
    shapes = [
        (2, ring, rows, a.shape[1]) if ring_on_inner else (ring, 2, rows, a.shape[1]) for a in arrays
    ]
    n_copies = 2 * ring * 2 * halves * count
    got = pl.pallas_call(
        functools.partial(_ring_gather_kernel, axis, outer, inner, ring_on_inner, halves, count),
        out_shape=tuple(jax.ShapeDtypeStruct(s, a.dtype) for s, a in zip(shapes, arrays)),
        in_specs=[pl.BlockSpec(memory_space=pl.ANY)] * count,
        out_specs=tuple(pl.BlockSpec(memory_space=pl.ANY) for _ in arrays),
        scratch_shapes=[
            pltpu.SemaphoreType.DMA((n_copies,)),
            pltpu.SemaphoreType.DMA((n_copies,)),
            pltpu.SemaphoreType.DMA((2, count)),
            pltpu.SemaphoreType.DMA((count,)),
        ],
        compiler_params=pltpu.CompilerParams(collective_id=cid, has_side_effects=True),
    )(*arrays)
    return [g.reshape(2 * ring * rows, a.shape[1]) for g, a in zip(got, arrays)]


def _ring_sum_kernel(axis, outer, chunks, count, *refs):
    xs = refs[:count]
    outs = refs[count:2 * count]
    send_bufs = refs[2 * count:3 * count]
    recv_bufs = refs[3 * count:4 * count]
    swap_bufs = refs[4 * count:5 * count]
    held = refs[5 * count:6 * count]
    send_sems, recv_sems, swap_sems, load_sems = refs[6 * count:]
    me = lax.axis_index(axis)
    y = me // 2
    x = me % 2
    ring = outer
    up = lax.rem(y + 1, ring) * 2 + x
    down = lax.rem(y + ring - 1, ring) * 2 + x
    partner = y * 2 + 1 - x
    rows = xs[0].shape[1]
    half = rows // 2
    part = half // chunks

    loads = []
    for t in range(count):
        ld = pltpu.make_async_copy(xs[t], held[t], load_sems.at[t])
        ld.start()
        loads.append(ld)

    barrier = pltpu.get_barrier_semaphore()
    for peer in (partner, up, down):
        pl.semaphore_signal(barrier, inc=1, device_id={axis: peer}, device_id_type=MESH)
    pl.semaphore_wait(barrier, 3)

    targets = (up, down)
    copies = {}

    def dest(d, step):
        return lax.rem(y - step + ring, ring) if d == 0 else lax.rem(y + step, ring)

    for step in range(1, ring):
        for c in range(chunks):
            for d in range(2):
                for t in range(count):
                    rs = pl.ds(d * half + c * part, part)
                    local = pl.ds(c * part, part)
                    blocks = pl.ds(dest(d, step) * 2, 2)
                    if step == 1:
                        src = xs[t].at[blocks, rs]
                    else:
                        if loads:
                            for ld in loads:
                                ld.wait()
                            loads.clear()
                        copies[(d, step - 1, c, t)].wait_recv()
                        send_bufs[t][d, step, :, local] = (
                            recv_bufs[t][d, step - 1, :, local] + held[t][blocks, rs]
                        )
                        src = send_bufs[t].at[d, step, :, local]
                    cp = pltpu.make_async_remote_copy(
                        src_ref=src, dst_ref=recv_bufs[t].at[d, step, :, local],
                        send_sem=send_sems.at[t, d, step, c], recv_sem=recv_sems.at[t, d, step, c],
                        device_id={axis: targets[d]}, device_id_type=MESH)
                    cp.start()
                    copies[(d, step, c, t)] = cp
    for ld in loads:
        ld.wait()
    swaps = []
    for c in range(chunks):
        for d in range(2):
            for t in range(count):
                rs = pl.ds(d * half + c * part, part)
                local = pl.ds(c * part, part)
                copies[(d, ring - 1, c, t)].wait_recv()
                swap_bufs[t][0, d, local] = recv_bufs[t][d, ring - 1, 1 - x, local] + held[t][y * 2 + 1 - x, rs]
                outs[t][rs] = recv_bufs[t][d, ring - 1, x, local] + held[t][y * 2 + x, rs]
                sw = pltpu.make_async_remote_copy(
                    src_ref=swap_bufs[t].at[0, d, local], dst_ref=swap_bufs[t].at[1, d, local],
                    send_sem=swap_sems.at[t, 0, d, c], recv_sem=swap_sems.at[t, 1, d, c],
                    device_id={axis: partner}, device_id_type=MESH)
                sw.start()
                swaps.append((d, c, t, sw))
    for d, c, t, sw in swaps:
        rs = pl.ds(d * half + c * part, part)
        sw.wait_recv()
        outs[t][rs] = outs[t][rs] + swap_bufs[t][1, d, pl.ds(c * part, part)]
    for d, c, t, sw in swaps:
        sw.wait_send()
    for cp in copies.values():
        cp.wait_send()


def ring_sum(partials, axis, outer, cid, chunks=4):
    count = len(partials)
    rows = partials[0].shape[1]
    half = rows // 2
    scratch = []
    for kind in range(4):
        for p in partials:
            width = p.shape[2]
            if kind < 2:
                scratch.append(pltpu.VMEM((2, outer, 2, half, width), jnp.float32))
            elif kind == 2:
                scratch.append(pltpu.VMEM((2, 2, half, width), jnp.float32))
            else:
                scratch.append(pltpu.VMEM(p.shape, jnp.float32))
    scratch += [
        pltpu.SemaphoreType.DMA((count, 2, outer, chunks)),
        pltpu.SemaphoreType.DMA((count, 2, outer, chunks)),
        pltpu.SemaphoreType.DMA((count, 2, 2, chunks)),
        pltpu.SemaphoreType.DMA((count,)),
    ]
    return pl.pallas_call(
        functools.partial(_ring_sum_kernel, axis, outer, chunks, count),
        out_shape=tuple(jax.ShapeDtypeStruct((rows, p.shape[2]), jnp.float32) for p in partials),
        in_specs=[pl.BlockSpec(memory_space=pl.ANY)] * count,
        out_specs=tuple(pl.BlockSpec(memory_space=pltpu.VMEM) for _ in partials),
        scratch_shapes=scratch,
        compiler_params=pltpu.CompilerParams(collective_id=cid, has_side_effects=True, vmem_limit_bytes=60 * 1024 * 1024),
    )(*partials)


def per_device(
    forward_acts, backward_grad, stored_gate, stored_up, gate_weight, up_weight, down_weight
):
    n_pipe = lax.axis_size("pipe")
    n_tensor = lax.axis_size("tensor")
    hidden_width = gate_weight.shape[1]
    model_width = forward_acts.shape[1]
    contract_last = (((1,), (1,)), ((), ()))

    whole_acts, whole_grad = ring_gather(
        [forward_acts, backward_grad], "tensor", 2, n_tensor // 2, True, 0
    )

    gate_part = jnp.dot(whole_acts, gate_weight, preferred_element_type=jnp.float32)
    up_part = jnp.dot(whole_acts, up_weight, preferred_element_type=jnp.float32)
    grad_part = lax.dot_general(
        whole_grad, down_weight, contract_last, preferred_element_type=jnp.float32
    )
    gate_pre, up_pre, hidden_grad = ring_sum(
        [p.reshape((n_pipe, p.shape[0] // n_pipe, p.shape[1])) for p in (gate_part, up_part, grad_part)],
        "pipe",
        n_pipe // 2,
        1,
    )
    hidden_part = (jax.nn.silu(gate_pre) * up_pre).astype(jnp.bfloat16)
    local_gate_slope, local_up_slope = make_slopes(hidden_grad, stored_gate, stored_up)

    hidden, gate_slopes, up_slopes = ring_gather(
        [hidden_part, local_gate_slope, local_up_slope], "pipe", n_pipe // 2, 2, False, 2
    )

    out_part = jnp.dot(hidden, down_weight, preferred_element_type=jnp.float32)
    in_part = lax.dot_general(
        gate_slopes, gate_weight, contract_last, preferred_element_type=jnp.float32
    ) + lax.dot_general(up_slopes, up_weight, contract_last, preferred_element_type=jnp.float32)
    finished = scatter_sum_rows(
        jnp.concatenate([out_part, in_part], axis=1), "tensor", n_tensor, TENSOR_LINK
    ).astype(jnp.bfloat16)
    return (finished[:, :model_width], finished[:, model_width:])


def solution(mesh):
    in_specs = (
        P(("dp", "tensor"), "pipe"),
        P(("dp", "tensor"), "pipe"),
        P(("dp", "pipe"), "tensor"),
        P(("dp", "pipe"), "tensor"),
        P("pipe", "tensor"),
        P("pipe", "tensor"),
        P("tensor", "pipe"),
    )
    out_specs = (P(("dp", "tensor"), "pipe"), P(("dp", "tensor"), "pipe"))
    return jax.shard_map(
        per_device, mesh=mesh, in_specs=in_specs, out_specs=out_specs, check_vma=False
    )
```
